32 devices in a mesh: seq: 4 (over y, x), dp: 8 (over z, core).
Axes of the slice: x: 2, y: 2, z: 4, core: 2. Of those that a mesh axis runs over, the one named last changes fastest.
Arguments:
- tokens: bfloat16 [32, 1024, 768], P('dp', 'seq'), may hold values from -6 to 6
- encoded: bfloat16 [32, 1024, 768], P('dp', 'seq'), may hold values from -6 to 6
- cotangent: bfloat16 [32, 1024, 768], P('dp', 'seq'), may hold values from -6 to 6
- doc_starts: int32 [32, 4], P('dp'), may hold values from 0 to 1023, as said below
- rel_bucket: int32 [1024], replicated, may hold values from 0 to 31
- self_query: bfloat16 [768, 768], P(('seq', 'dp')), may hold values from -0.02734375 to 0.02734375
- self_key: bfloat16 [768, 768], P(('seq', 'dp')), may hold values from -0.21875 to 0.21875
- self_value: bfloat16 [768, 768], P(('seq', 'dp')), may hold values from -0.21875 to 0.21875
- self_output_weight: bfloat16 [768, 768], P(('seq', 'dp')), may hold values from -0.875 to 0.875
- cross_query: bfloat16 [768, 768], P(('seq', 'dp')), may hold values from -0.02734375 to 0.02734375
- cross_key: bfloat16 [768, 768], P(('seq', 'dp')), may hold values from -0.21875 to 0.21875
- cross_value: bfloat16 [768, 768], P(('seq', 'dp')), may hold values from -0.21875 to 0.21875
- cross_output_weight: bfloat16 [768, 768], P(('seq', 'dp')), may hold values from -3.5 to 3.5
- feed_input_weight: bfloat16 [768, 3072], P(('seq', 'dp')), may hold values from -0.21875 to 0.21875
- feed_output_weight: bfloat16 [3072, 768], P(('seq', 'dp')), may hold values from -0.15625 to 0.15625
- gain_self: bfloat16 [768], P(('seq', 'dp')), may hold values from 0.5 to 1.5
- gain_cross: bfloat16 [768], P(('seq', 'dp')), may hold values from 0.5 to 1.5
- gain_feed: bfloat16 [768], P(('seq', 'dp')), may hold values from 0.5 to 1.5
- mix_pre: float32 [12, 12], replicated, may hold values from -1.75 to 1.75
- mix_post: float32 [12, 12], replicated, may hold values from -1.75 to 1.75
- rel_table: float32 [32, 12], replicated, may hold values from -4 to 4
Outputs:
- output: bfloat16 [32, 1024, 768], P('dp', 'seq')
- grad_tokens: float32 [32, 1024, 768], P('dp', 'seq')
- grad_encoded: float32 [32, 1024, 768], P('dp', 'seq')
- grad_self_query: float32 [768, 768], P(('seq', 'dp'))
- grad_self_key: float32 [768, 768], P(('seq', 'dp'))
- grad_self_value: float32 [768, 768], P(('seq', 'dp'))
- grad_self_out: float32 [768, 768], P(('seq', 'dp'))
- grad_cross_query: float32 [768, 768], P(('seq', 'dp'))
- grad_cross_key: float32 [768, 768], P(('seq', 'dp'))
- grad_cross_value: float32 [768, 768], P(('seq', 'dp'))
- grad_cross_out: float32 [768, 768], P(('seq', 'dp'))
- grad_feed_in: float32 [768, 3072], P(('seq', 'dp'))
- grad_feed_out: float32 [3072, 768], P(('seq', 'dp'))
- grad_gain_self: float32 [768], P(('seq', 'dp'))
- grad_gain_cross: float32 [768], P(('seq', 'dp'))
- grad_gain_feed: float32 [768], P(('seq', 'dp'))
- grad_mix_pre: float32 [12, 12], replicated
- grad_mix_post: float32 [12, 12], replicated
- grad_rel_table: float32 [32, 12], replicated
The draws below stay inside these ranges and needn't reach their ends.
Inputs may be any that keep to these rules, and one draw needn't show every extreme that they name: `doc_starts`: each stream's 4 document starts rise strictly, and the first is 0.
All inputs are finite; a program needn't handle non-finite values.
Results may differ from the reference program's by a relative error of at most 0.024.
Values may be sent and summed in bfloat16 or wider, within the bound.
A program may use at most 576 MiB of HBM per device.

```python
import jax
import jax.numpy as jnp
from jax import lax

D = 768
H = 12
DH = 64
FF = 3072
NB = 32
LEN = 1024
ENC = 1024
DOCS = 4
STREAMS = 32


def draw_doc_starts(key, part):
    stream_keys = jax.random.split(jax.random.fold_in(key, 11), STREAMS)

    def one_stream(stream_key):
        picked = jax.random.permutation(stream_key, LEN - 1)[:DOCS - 1] + 1
        return jnp.concatenate([jnp.zeros((1,), jnp.int32), jnp.sort(picked).astype(jnp.int32)])
    return jax.vmap(one_stream)(stream_keys)


def with_ends(array, key, least, largest):
    dims = array.shape
    index_at = [jax.random.randint(jax.random.fold_in(key, axis), (), 0, dims[axis]) for axis in range(len(dims))]
    array = array.at[tuple(index_at)].set(least)
    longest = dims.index(max(dims))
    index_at[longest] = (index_at[longest] + 1) % dims[longest]
    return array.at[tuple(index_at)].set(largest)


def levels(key, shape, pieces, low, largest):
    level = 1.0
    for dim, blocks in pieces:
        steps = jax.random.uniform(jax.random.fold_in(jax.random.fold_in(key, 6), dim), (blocks,), jnp.float32, low / len(pieces), largest / len(pieces))
        level = level * jnp.repeat(jnp.exp(steps), shape[dim] // blocks).reshape((-1,) + (1,) * (len(shape) - 1 - dim))
    return level


def centred(rng, extent, spread, reach, pieces=(), kind=jnp.bfloat16):
    array = jax.random.normal(rng, extent, jnp.float32) * spread
    if len(pieces) > 0:
        array = levels(rng, extent, pieces, -0.22, 0.18) * array
    return jnp.clip(array, min=-reach, max=reach).astype(kind)


def setup_inputs(seed: int = 0) -> dict:
    streams_of = jax.random.split(jax.random.key(seed), 22)
    tokens = centred(streams_of[0], (STREAMS, LEN, D), 1.0, 6.0, ((0, 8), (1, 4)))
    encoded = centred(streams_of[1], (STREAMS, ENC, D), 1.0, 6.0, ((0, 8), (1, 4)))
    cotangent = centred(streams_of[2], (STREAMS, LEN, D), 1.0, 6.0, ((0, 8), (1, 4)))
    doc_starts = draw_doc_starts(jax.random.fold_in(streams_of[21], 71), 0)
    rel_bucket = with_ends(jax.random.randint(streams_of[4], (LEN,), 0, NB), jax.random.fold_in(streams_of[4], 1), 0, NB - 1).astype(jnp.int32)
    self_query = centred(streams_of[5], (D, D), (D * DH) ** -0.5, 0.02734375, ((0, 32),))
    self_key = centred(streams_of[6], (D, D), D ** -0.5, 0.21875, ((0, 32),))
    self_value = centred(streams_of[7], (D, D), D ** -0.5, 0.21875, ((0, 32),))
    self_output_weight = centred(streams_of[8], (D, D), (D // 16) ** -0.5, 0.875, ((0, 32),))
    cross_query = centred(streams_of[9], (D, D), (D * DH) ** -0.5, 0.02734375, ((0, 32),))
    cross_key = centred(streams_of[10], (D, D), D ** -0.5, 0.21875, ((0, 32),))
    cross_value = centred(streams_of[11], (D, D), D ** -0.5, 0.21875, ((0, 32),))
    cross_output_weight = centred(streams_of[12], (D, D), (max(D // 256, 1)) ** -0.5, 3.5, ((0, 32),))
    feed_input_weight = centred(streams_of[13], (D, FF), D ** -0.5, 0.21875, ((0, 32),))
    feed_output_weight = centred(streams_of[14], (FF, D), (FF // 2) ** -0.5, 0.15625, ((0, 32),))
    gain_self = jnp.clip(1.0 + 0.1 * jax.random.normal(streams_of[15], (D,), jnp.float32), 0.5, 1.5).astype(jnp.bfloat16)
    gain_cross = jnp.clip(1.0 + 0.1 * jax.random.normal(streams_of[16], (D,), jnp.float32), 0.5, 1.5).astype(jnp.bfloat16)
    gain_feed = jnp.clip(1.0 + 0.1 * jax.random.normal(streams_of[17], (D,), jnp.float32), 0.5, 1.5).astype(jnp.bfloat16)
    mix_pre = centred(streams_of[18], (H, H), H ** -0.5, 1.75, (), jnp.float32)
    mix_post = centred(streams_of[19], (H, H), H ** -0.5, 1.75, (), jnp.float32)
    rel_table = centred(streams_of[20], (NB, H), 1.0, 4.0, (), jnp.float32)
    return {"tokens": tokens, "encoded": encoded, "cotangent": cotangent, "doc_starts": doc_starts, "rel_bucket": rel_bucket, "self_query": self_query, "self_key": self_key, "self_value": self_value, "self_output_weight": self_output_weight, "cross_query": cross_query, "cross_key": cross_key, "cross_value": cross_value, "cross_output_weight": cross_output_weight, "feed_input_weight": feed_input_weight, "feed_output_weight": feed_output_weight, "gain_self": gain_self, "gain_cross": gain_cross, "gain_feed": gain_feed, "mix_pre": mix_pre, "mix_post": mix_post, "rel_table": rel_table}


@jax.custom_vjp
def low(v):
    return lax.optimization_barrier(v.astype(jnp.bfloat16)).astype(jnp.float32)

@jax.custom_vjp
def low_back(v):
    return v

def low_keep(v):
    return (low(v), None)

def low_pass(kept, grad):
    return (grad,)

def back_keep(v):
    return (v, None)

def back_low(kept, grad):
    return (low(grad),)
low.defvjp(low_keep, low_pass)
low_back.defvjp(back_keep, back_low)

def exact_answer(form, left, right):
    return jnp.einsum(form, left, right, precision=lax.Precision.HIGHEST)

def norm_apply(value_rows, gain):
    return value_rows * lax.rsqrt(lax.optimization_barrier(jnp.mean(value_rows * value_rows, axis=-1, keepdims=True)) + 1e-06) * gain

def rounded_twice(value_rows):
    return low_back(low(value_rows))

def self_attend(query, keys, value_rows, starts, mix_pre, mix_post, table_rows):
    logits = low_back(exact_answer('qhd,khd->hqk', query, keys))
    position = jnp.arange(LEN, dtype=jnp.int32)
    offset = (position[:, None] - position[None, :]).astype(jnp.int32)
    bias = jnp.take(table_rows.T, jnp.clip(offset, 0, LEN - 1).astype(jnp.int32), axis=1)
    mixed = exact_answer('gh,gqk->hqk', mix_pre, logits) + bias
    document = lax.optimization_barrier(jnp.sum((starts.astype(jnp.int32)[None, :] <= position[:, None]).astype(jnp.int32), axis=1)).astype(jnp.int32)
    allowed = (offset >= 0) & (document[:, None] == document[None, :])
    probs = jax.nn.softmax(jnp.where(allowed[None], mixed, -1e+30), axis=-1)
    blended = low(exact_answer('gh,gqk->hqk', mix_post, probs))
    return exact_answer('hqk,khd->qhd', blended, value_rows)

def cross_attend(query, keys, value_rows):
    logits = low_back(exact_answer('qhd,khd->hqk', query, keys))
    probs = low(jax.nn.softmax(logits, axis=-1))
    return exact_answer('hqk,khd->qhd', probs, value_rows)

def forward(tokens, encoded, self_query, self_key, self_value, self_output_weight, cross_query, cross_key, cross_value, cross_output_weight, feed_input_weight, feed_output_weight, gain_self, gain_cross, gain_feed, mix_pre, mix_post, rel_table, doc_starts, rel_bucket):
    streams = tokens.shape[0]
    table_rows = jnp.take(rel_table, rel_bucket.astype(jnp.int32), axis=0)

    def heads(value_rows):
        return value_rows.reshape(streams, value_rows.shape[1], H, DH)

    def project(value_rows, weight_matrix):
        return rounded_twice(exact_answer('tqg,gh->tqh', value_rows, weight_matrix))
    normed_self = low(norm_apply(tokens, gain_self))
    query = heads(project(normed_self, self_query))
    keys = heads(project(normed_self, self_key))
    value_rows = heads(project(normed_self, self_value))
    attend_self = jax.checkpoint(lambda items: self_attend(items[0], items[1], items[2], items[3], mix_pre, mix_post, table_rows))
    attention_result = lax.map(attend_self, (query, keys, value_rows, doc_starts))
    attention_result = rounded_twice(attention_result.reshape(streams, LEN, D))
    hidden_after_self = tokens + low_back(exact_answer('tqg,gh->tqh', attention_result, self_output_weight))
    normed_cross = low(norm_apply(hidden_after_self, gain_cross))
    cross_q = heads(project(normed_cross, cross_query))
    cross_k = heads(project(encoded, cross_key))
    cross_v = heads(project(encoded, cross_value))
    attend_cross = jax.checkpoint(lambda items: cross_attend(items[0], items[1], items[2]))
    cross_attention_value = lax.map(attend_cross, (cross_q, cross_k, cross_v))
    cross_attention_value = rounded_twice(cross_attention_value.reshape(streams, LEN, D))
    hidden_after_cross = hidden_after_self + low_back(exact_answer('tqg,gh->tqh', cross_attention_value, cross_output_weight))
    feed_normalized = low(norm_apply(hidden_after_cross, gain_feed))
    inner_pre = low_back(exact_answer('tqg,gh->tqh', feed_normalized, feed_input_weight))
    inner_activation = low(jax.nn.gelu(inner_pre, approximate=True))
    return hidden_after_cross + low_back(exact_answer('iry,yb->irb', inner_activation, feed_output_weight))

def reference(tokens, encoded, cotangent, doc_starts, rel_bucket, self_query, self_key, self_value, self_output_weight, cross_query, cross_key, cross_value, cross_output_weight, feed_input_weight, feed_output_weight, gain_self, gain_cross, gain_feed, mix_pre, mix_post, rel_table):
    floats = [tokens, encoded, self_query, self_key, self_value, self_output_weight, cross_query, cross_key, cross_value, cross_output_weight, feed_input_weight, feed_output_weight, gain_self, gain_cross, gain_feed, mix_pre, mix_post, rel_table]
    floats = [item.astype(jnp.float32) for item in floats]

    def wrapped(*params):
        return forward(*params, doc_starts, rel_bucket)
    result, pullback = jax.vjp(wrapped, *floats)
    gradient_tree = pullback(cotangent.astype(jnp.float32))
    return (result.astype(jnp.bfloat16), gradient_tree[0], gradient_tree[1], gradient_tree[2], gradient_tree[3], gradient_tree[4], gradient_tree[5], gradient_tree[6], gradient_tree[7], gradient_tree[8], gradient_tree[9], gradient_tree[10], gradient_tree[11], gradient_tree[12], gradient_tree[13], gradient_tree[14], gradient_tree[15], gradient_tree[16], gradient_tree[17])
```

```python
import functools
import jax, jax.numpy as jnp
from jax import lax
from jax.experimental import pallas as pl
from jax.experimental.pallas import tpu as pltpu
F32=jnp.float32; BF=jnp.bfloat16
NEG=-1e30
H=12; DH=64; D=768; L=1024; BLK=256; NBK=L//BLK

def dot(a,b,ca,cb):
    return lax.dot_general(a,b,(((ca,),(cb,)),((),())),preferred_element_type=F32)

def toep_kernel(base_ref, out_ref):
    for dl in range(NBK):
        row = jnp.broadcast_to(base_ref[0, dl], (BLK, 2*BLK))
        t = pltpu.roll(row, 0, 1, stride=1, stride_axis=0)[:, :BLK]
        if dl == 0:
            a = lax.broadcasted_iota(jnp.int32, (BLK,BLK),0); b=lax.broadcasted_iota(jnp.int32,(BLK,BLK),1)
            t = jnp.where(a>=b, t, NEG)
        out_ref[0, dl] = t

def toeplitz(base):
    return pl.pallas_call(toep_kernel, grid=(H,),
        in_specs=[pl.BlockSpec((1,NBK,1,2*BLK), lambda h:(h,0,0,0))],
        out_specs=pl.BlockSpec((1,NBK,BLK,BLK), lambda h:(h,0,0,0)),
        out_shape=jax.ShapeDtypeStruct((H,NBK,BLK,BLK),F32))(base)

def make_base(trow):
    dl = jnp.arange(NBK)[:,None]*BLK
    y = jnp.arange(2*BLK)[None,:]
    rows=[]
    for d in range(NBK):
        lo = d*BLK
        a = trow[:, max(lo-BLK+1,0):lo+1][:, ::-1]
        if d==0: a = jnp.concatenate([a, jnp.zeros((H,BLK-1),F32)],1)
        b = trow[:, lo+1:lo+BLK][:, ::-1]
        rows.append(jnp.concatenate([a, jnp.zeros((H,1),F32), b],1))
    return jnp.stack(rows,1)[:,:,None,:]

def self_fwd_kernel(st_ref, q_ref, k_ref, v_ref, bias_ref, mpre_ref, mpost_ref, att_ref, p_ref, acc_ref, lo_ref):
    s = pl.program_id(0)
    h = pl.program_id(1)
    @pl.when(h==0)
    def _():
        acc_ref[...] = jnp.zeros_like(acc_ref)
        pos = lax.broadcasted_iota(jnp.int32,(L,128),0)
        lo = jnp.zeros((L,128),jnp.int32)
        for d in range(1,4):
            sd = st_ref[s,d]
            lo = jnp.where(pos>=sd, sd, lo)
        lo_ref[...] = lo
    mp = mpre_ref[pl.ds(h,1),:]
    mo = mpost_ref[pl.ds(h,1),:]
    for I in range(NBK):
        r = slice(I*BLK,(I+1)*BLK); n=(I+1)*BLK
        qm = (q_ref[0,r,:].astype(F32)*mp).astype(BF)
        sc = dot(qm, k_ref[0,:n,:],1,1)
        bias = jnp.concatenate([bias_ref[0,I-J] for J in range(I+1)],1) if I else bias_ref[0,0]
        sc = sc + bias
        col = lax.broadcasted_iota(jnp.int32,(BLK,n),1)
        sc = jnp.where(col>=lo_ref[r,:1], sc, NEG)
        m = jnp.max(sc,1,keepdims=True)
        e = jnp.exp(sc-m)
        l = jnp.sum(e,1,keepdims=True)
        p = (e*(1.0/l)).astype(BF)
        p_ref[0,0,r,:n] = p
        acc_ref[r,:] += dot(p, v_ref[0,:n,:],1,0)*mo
    @pl.when(h==H-1)
    def _():
        att_ref[0] = acc_ref[...].astype(BF)

def self_fwd(starts,q,k,v,bias,mpre,mpost):
    B=q.shape[0]
    full=lambda s,h,st:(s,0,0)
    return pl.pallas_call(self_fwd_kernel,
      grid_spec=pltpu.PrefetchScalarGridSpec(num_scalar_prefetch=1, grid=(B,H),
        in_specs=[pl.BlockSpec((1,L,D),full)]*3+[pl.BlockSpec((1,NBK,BLK,BLK),lambda s,h,st:(h,0,0,0)),
                  pl.BlockSpec((H,D),lambda s,h,st:(0,0)),pl.BlockSpec((H,D),lambda s,h,st:(0,0))],
        out_specs=[pl.BlockSpec((1,L,D),full),pl.BlockSpec((1,1,L,L),lambda s,h,st:(s,h,0,0))],
        scratch_shapes=[pltpu.VMEM((L,D),F32),pltpu.VMEM((L,128),jnp.int32)]),
      out_shape=[jax.ShapeDtypeStruct((B,L,D),BF),jax.ShapeDtypeStruct((B,H,L,L),BF)],
      compiler_params=pltpu.CompilerParams(vmem_limit_bytes=56<<20),
      cost_estimate=pl.CostEstimate(flops=B*48_000_000_000,bytes_accessed=B*40_000_000,transcendentals=B*8_000_000),
      name="self_fwd")(starts,q,k,v,bias,mpre,mpost)

def self_bwd_kernel(q_ref,k_ref,v_ref,ba_ref,p_ref,mpre_ref,mpost_ref,
      dq_ref,dk_ref,dv_ref,gpre_ref,gpost_ref,diag_ref,
      qT,baT,dqa,dkT,dvT,dm):
    h=pl.program_id(1)
    @pl.when(h==0)
    def _():
        qT[...]=q_ref[0].T
        baT[...]=ba_ref[0].T
        dqa[...]=jnp.zeros_like(dqa)
        dkT[...]=jnp.zeros_like(dkT)
        dvT[...]=jnp.zeros_like(dvT)
        gpre_ref[...]=jnp.zeros_like(gpre_ref)
        gpost_ref[...]=jnp.zeros_like(gpost_ref)
    mp = mpre_ref[pl.ds(h,1),:]
    mo = mpost_ref[pl.ds(h,1),:]
    gp = jnp.zeros((8,D),F32)
    dacc=[None]*NBK
    for I in range(NBK):
        r = slice(I*BLK,(I+1)*BLK); n=(I+1)*BLK
        bam=(ba_ref[0,r,:].astype(F32)*mo).astype(BF)
        dp=dot(bam,v_ref[0,:n,:],1,1)
        p=p_ref[0,0,r,:n].astype(F32)
        dl=jnp.sum(dp*p,1,keepdims=True)
        d=p*(dp-dl)
        for J in range(I+1):
            t=d[:,J*BLK:(J+1)*BLK]
            dacc[I-J]= t if dacc[I-J] is None else dacc[I-J]+t
        db=d.astype(BF)
        dm[r,:n]=db
        R=dot(db,k_ref[0,:n,:],1,0)
        dqa[r,:]+=R*mp
        gp = gp + jnp.sum((R*q_ref[0,r,:].astype(F32)).reshape(BLK//8,8,D),0)
    gpre_ref[0,pl.ds(h,1),:]=jnp.sum(gp,0,keepdims=True)
    for dlt in range(NBK):
        x=jnp.concatenate([jnp.zeros((BLK,BLK),F32),dacc[dlt]],1)
        n=BLK//2
        while n>=1:
            x=x[:n]+pltpu.roll(x[n:],2*BLK-n,1)
            n//=2
        diag_ref[0,0,dlt]=x
    mpc=jnp.transpose(jnp.broadcast_to(mp,(8,D)))[:,:1]
    moc=jnp.transpose(jnp.broadcast_to(mo,(8,D)))[:,:1]
    gq=jnp.zeros((8,D),F32)
    for J in range(NBK):
        c=slice(J*BLK,(J+1)*BLK); i0=J*BLK
        T=dot(baT[:,i0:],p_ref[0,0,i0:,c],1,0)
        dvT[:,c]+=T*moc
        vv=v_ref[0,c,:].astype(F32)
        gq=gq+jnp.sum((T.T*vv).reshape(BLK//8,8,D),0)
        U=dot(qT[:,i0:],dm[i0:,c],1,0)
        dkT[:,c]+=U*mpc
    gpost_ref[0,pl.ds(h,1),:]=jnp.sum(gq,0,keepdims=True)
    @pl.when(h==H-1)
    def _():
        dq_ref[0]=dqa[...].astype(BF)
        dk_ref[0]=dkT[...].T.astype(BF)
        dv_ref[0]=dvT[...].T.astype(BF)

def self_bwd(q,k,v,ba,p,mpre,mpost):
    B=q.shape[0]
    full=lambda s,h:(s,0,0)
    one=pl.BlockSpec((1,L,D),full)
    lane=pl.BlockSpec((H,D),lambda s,h:(0,0))
    return pl.pallas_call(self_bwd_kernel,grid=(B,H),
      in_specs=[one]*4+[pl.BlockSpec((1,1,L,L),lambda s,h:(s,h,0,0)),lane,lane],
      out_specs=[one]*3+[pl.BlockSpec((1,H,D),full)]*2+[pl.BlockSpec((1,1,NBK,1,2*BLK),lambda s,h:(s,h,0,0,0))],
      out_shape=[jax.ShapeDtypeStruct((B,L,D),BF)]*3+[jax.ShapeDtypeStruct((B,H,D),F32)]*2+[jax.ShapeDtypeStruct((B,H,NBK,1,2*BLK),F32)],
      scratch_shapes=[pltpu.VMEM((D,L),BF)]*2+[pltpu.VMEM((L,D),F32)]+[pltpu.VMEM((D,L),F32)]*2+[pltpu.VMEM((L,L),BF)],
      compiler_params=pltpu.CompilerParams(vmem_limit_bytes=58<<20),
      cost_estimate=pl.CostEstimate(flops=B*121_000_000_000,bytes_accessed=B*40_000_000,transcendentals=0),
      name="self_bwd")(q,k,v,ba,p,mpre,mpost)
def cross_fwd_kernel(q_ref,k_ref,v_ref,att_ref,p_ref):
    first=lax.broadcasted_iota(jnp.int32,(1,128),1)<DH
    k=k_ref[0]; v=v_ref[0]
    for I in range(NBK):
        r=slice(I*BLK,(I+1)*BLK)
        q=q_ref[0,r,:]
        outs=[]
        for e in range(2):
            qe=jnp.where(first if e==0 else ~first,q,jnp.zeros_like(q))
            sc=dot(qe,k,1,1)
            m=jnp.max(sc,1,keepdims=True)
            ex=jnp.exp(sc-m)
            l=jnp.sum(ex,1,keepdims=True)
            p=(ex*(1.0/l)).astype(BF)
            p_ref[0,e,r,:]=p
            outs.append(dot(p,v,1,0))
        att_ref[0,r,:]=jnp.where(first,outs[0],outs[1]).astype(BF)
def cross_fwd(q,k,v):
    B=q.shape[0]
    pair=pl.BlockSpec((1,L,128),lambda s,h:(s,0,h))
    return pl.pallas_call(cross_fwd_kernel,grid=(B,H//2),in_specs=[pair]*3,
      out_specs=[pair,pl.BlockSpec((1,2,L,L),lambda s,h:(s,h,0,0))],
      out_shape=[jax.ShapeDtypeStruct((B,L,D),BF),jax.ShapeDtypeStruct((B,H,L,L),BF)],
      compiler_params=pltpu.CompilerParams(vmem_limit_bytes=40<<20),
      cost_estimate=pl.CostEstimate(flops=B*26_000_000_000,bytes_accessed=B*35_000_000,transcendentals=B*12_000_000),
      name="cross_fwd")(q,k,v)
def cross_bwd_kernel(q_ref,k_ref,v_ref,do_ref,p_ref,dq_ref,dk_ref,dv_ref,qT,doT,ds):
    first=lax.broadcasted_iota(jnp.int32,(1,128),1)<DH
    topT=lax.broadcasted_iota(jnp.int32,(128,1),0)<DH
    k=k_ref[0]; v=v_ref[0]
    qT[...]=q_ref[0].T; doT[...]=do_ref[0].T
    dqs=[]; dks=[]; dvs=[]
    for e in range(2):
        fe=first if e==0 else ~first
        dq=[]
        for I in range(NBK):
            r=slice(I*BLK,(I+1)*BLK)
            do=do_ref[0,r,:]
            dp=dot(jnp.where(fe,do,jnp.zeros_like(do)),v,1,1)
            p=p_ref[0,e,r,:].astype(F32)
            dl=jnp.sum(dp*p,1,keepdims=True)
            d=(p*(dp-dl)).astype(BF)
            ds[e,r,:]=d
            x=dot(d,k,1,0)
            if e==0: dq_ref[0,r,:]=x.astype(BF)
            else: dq_ref[0,r,:]=jnp.where(first,dq_ref[0,r,:],x.astype(BF))
        dvs.append(dot(doT[...],p_ref[0,e],1,0))
        dks.append(dot(qT[...],ds[e],1,0))
    dk_ref[0]=jnp.where(topT,dks[0],dks[1]).T.astype(BF)
    dv_ref[0]=jnp.where(topT,dvs[0],dvs[1]).T.astype(BF)
def cross_bwd(q,k,v,do,p):
    B=q.shape[0]
    pair=pl.BlockSpec((1,L,128),lambda s,h:(s,0,h))
    return pl.pallas_call(cross_bwd_kernel,grid=(B,H//2),
      in_specs=[pair]*4+[pl.BlockSpec((1,2,L,L),lambda s,h:(s,h,0,0))],
      out_specs=[pair]*3,
      out_shape=[jax.ShapeDtypeStruct((B,L,D),BF)]*3,
      scratch_shapes=[pltpu.VMEM((128,L),BF)]*2+[pltpu.VMEM((2,L,L),BF)],
      compiler_params=pltpu.CompilerParams(vmem_limit_bytes=40<<20),
      cost_estimate=pl.CostEstimate(flops=B*26_000_000_000,bytes_accessed=B*35_000_000,transcendentals=0),
      name="cross_bwd")(q,k,v,do,p)
from jax.sharding import PartitionSpec as P
AX = ("seq", "dp")
GATE = 0.7978845608028654


def mm(a, b):
    return jnp.dot(a, b, preferred_element_type=F32)


def mm_t(a, b):
    return lax.dot_general(a, b, (((1,), (1,)), ((), ())), preferred_element_type=F32)


def wgrad(a, b):
    return lax.dot_general(a, b, (((0,), (0,)), ((), ())), preferred_element_type=F32)


def norm(x, g):
    r = lax.rsqrt(jnp.mean(x * x, -1, keepdims=True) + 1e-6)
    return x * r * g


def norm_grad(x, g, dn):
    r = lax.rsqrt(jnp.mean(x * x, -1, keepdims=True) + 1e-6)
    gd = g * dn
    dx = r * gd - x * (r * r * r) * jnp.mean(gd * x, -1, keepdims=True)
    return dx, jnp.sum(dn * x * r, 0)


def gelu_pair(x):
    t = jnp.tanh(GATE * (x + 0.044715 * x * x * x))
    y = 0.5 * x * (1.0 + t)
    d = 0.5 * (1.0 + t) + 0.5 * x * (1.0 - t * t) * GATE * (1.0 + 3 * 0.044715 * x * x)
    return y, d


def gather(w):
    return lax.all_gather(w, AX, axis=0, tiled=True)


def scatter(g):
    return lax.psum_scatter(g.astype(BF), AX, scatter_dimension=0, tiled=True).astype(F32)


def per_device(tokens, encoded, cotangent, doc_starts, rel_bucket, sq, sk, sv, so, cq, ck, cv, co, fi, fo,
               gs, gc, gf, mix_pre, mix_post, rel_table):
    nseq = lax.axis_size("seq")
    nb = tokens.shape[0] // nseq
    buckets = rel_table.shape[0]
    to_stream = lambda x: lax.all_to_all(x, "seq", 0, 1, tiled=True)
    from_stream = lambda x: lax.all_to_all(x, "seq", 1, 0, tiled=True)
    gains = jnp.pad(jnp.stack([gs, gc, gf], 1), ((0, 0), (0, 125)))
    w1 = gather(jnp.concatenate([sq, sk, sv, gains], 1))
    w2 = gather(jnp.concatenate([so, cq, ck, cv, co], 1))
    w3 = gather(fi)
    w4 = gather(fo)
    wqkv = w1[:, :3 * D]
    g_all = w1[:, 3 * D:3 * D + 3].astype(F32).T
    g_self, g_cross, g_feed = g_all[0], g_all[1], g_all[2]
    w_o, w_cq, w_ckv, w_co = w2[:, :D], w2[:, D:2 * D], w2[:, 2 * D:4 * D], w2[:, 4 * D:]
    x = to_stream(tokens).reshape(nb * L, D).astype(F32)
    enc = to_stream(encoded).reshape(nb * L, D)
    cot = to_stream(cotangent).reshape(nb * L, D)
    starts = lax.dynamic_slice_in_dim(doc_starts, lax.axis_index("seq") * nb, nb, 0)
    hot = (rel_bucket[:, None] == jnp.arange(buckets)[None, :]).astype(F32)
    trow = lax.dot_general(rel_table, hot, (((0,), (1,)), ((), ())), precision=lax.Precision.HIGHEST)
    bias = toeplitz(make_base(trow))
    mpre = jnp.repeat(mix_pre.T, DH, axis=1)
    mpost = jnp.repeat(mix_post, DH, axis=1)
    s3 = lambda a: a.reshape(nb, L, D)
    s2 = lambda a: a.reshape(nb * L, D)
    n1 = norm(x, g_self).astype(BF)
    qkv = mm(n1, wqkv).astype(BF)
    q, k, v = qkv[:, :D], qkv[:, D:2 * D], qkv[:, 2 * D:]
    att, p = self_fwd(starts, s3(q), s3(k), s3(v), bias, mpre, mpost)
    att = s2(att)
    h1 = x + mm(att, w_o)
    n2 = norm(h1, g_cross).astype(BF)
    cqx = mm(n2, w_cq).astype(BF)
    ckv = mm(enc, w_ckv).astype(BF)
    ckx, cvx = ckv[:, :D], ckv[:, D:]
    catt, cp = cross_fwd(s3(cqx), s3(ckx), s3(cvx))
    catt = s2(catt)
    h2 = h1 + mm(catt, w_co)
    n3 = norm(h2, g_feed).astype(BF)
    inner, dgelu = gelu_pair(mm(n3, w3))
    inner = inner.astype(BF)
    out = (h2 + mm(inner, w4)).astype(BF)
    bi = (mm_t(cot, w4) * dgelu).astype(BF)
    g_fo = scatter(wgrad(inner, cot))
    g_fi = scatter(wgrad(n3, bi))
    dx, d_gf = norm_grad(h2, g_feed, mm_t(bi, w3))
    bh2 = cot.astype(F32) + dx
    bcb = bh2.astype(BF)
    bca = mm_t(bcb, w_co).astype(BF)
    gw_co = wgrad(catt, bcb)
    dcq, dck, dcv = cross_bwd(s3(cqx), s3(ckx), s3(cvx), s3(bca), cp)
    dcq, dck, dcv = s2(dcq), s2(dck), s2(dcv)
    dckv = jnp.concatenate([dck, dcv], 1)
    gw_cq = wgrad(n2, dcq)
    gw_ckv = wgrad(enc, dckv)
    g_enc = mm_t(dckv, w_ckv)
    dx, d_gc = norm_grad(h1, g_cross, mm_t(dcq, w_cq))
    bh1 = bh2 + dx
    bsb = bh1.astype(BF)
    bat = mm_t(bsb, w_o).astype(BF)
    gw_o = wgrad(att, bsb)
    r_mid = scatter(jnp.concatenate([gw_co, gw_cq, gw_ckv, gw_o], 1))
    dq, dk, dv, gpre, gpost, diag = self_bwd(s3(q), s3(k), s3(v), s3(bat), p, mpre, mpost)
    dqkv = jnp.concatenate([s2(dq), s2(dk), s2(dv)], 1)
    gw_qkv = wgrad(n1, dqkv)
    dx, d_gs = norm_grad(x, g_self, mm_t(dqkv, wqkv))
    g_tok = bh1 + dx
    r_end = scatter(gw_qkv)
    gpre = jnp.sum(gpre, 0).reshape(H, H, DH).sum(-1).T
    gpost = jnp.sum(gpost, 0).reshape(H, H, DH).sum(-1)
    dg = jnp.sum(diag, 0)[:, :, 0, ::-1]
    gt = 0.0
    for d in range(NBK):
        gt = gt + jnp.pad(dg[:, d], ((0, 0), (d * BLK + 1, L - d * BLK - 1)))
    gt = gt[:, BLK:BLK + L]
    gtab = lax.dot_general(hot, gt, (((0,), (1,)), ((), ())), precision=lax.Precision.HIGHEST)
    gpre, gpost, gtab, dgain = lax.psum((gpre, gpost, gtab, jnp.stack([d_gs, d_gc, d_gf])), AX)
    rows = gs.shape[0]
    me = lax.axis_index("seq") * lax.axis_size("dp") + lax.axis_index("dp")
    dgain = lax.dynamic_slice_in_dim(dgain, me * rows, rows, 1)
    o3 = lambda a: from_stream(s3(a))
    return (o3(out), o3(g_tok), o3(g_enc),
            r_end[:, :D], r_end[:, D:2 * D], r_end[:, 2 * D:], r_mid[:, 4 * D:],
            r_mid[:, D:2 * D], r_mid[:, 2 * D:3 * D], r_mid[:, 3 * D:4 * D], r_mid[:, :D],
            g_fi, g_fo, dgain[0], dgain[1], dgain[2], gpre, gpost, gtab)


def solution(mesh):
    act = P("dp", "seq", None)
    w = P(("seq", "dp"), None)
    g = P(("seq", "dp"))
    return jax.shard_map(per_device, mesh=mesh,
        in_specs=(act, act, act, P("dp", None), P()) + (w,) * 10 + (g,) * 3 + (P(),) * 3,
        out_specs=(act,) * 3 + (w,) * 10 + (g,) * 3 + (P(),) * 3, check_vma=False)
```

```python
import functools

import jax
import jax.numpy as jnp
from jax import lax
from jax.experimental import pallas as pl
from jax.experimental.pallas import tpu as pltpu
from jax.sharding import PartitionSpec as P

F32 = jnp.float32
BF = jnp.bfloat16
NEG = -1e30
H, DH, D, L = 12, 64, 768, 1024
BLK = 256
NBK = L // BLK


def dot(a, b, ca, cb):
    return lax.dot_general(a, b, (((ca,), (cb,)), ((), ())), preferred_element_type=F32)


def toep_kernel(base_ref, out_ref):
    for d in range(NBK):
        row = jnp.broadcast_to(base_ref[0, d], (BLK, 2 * BLK))
        t = pltpu.roll(row, 0, 1, stride=1, stride_axis=0)[:, :BLK]
        if d == 0:
            a = lax.broadcasted_iota(jnp.int32, (BLK, BLK), 0)
            b = lax.broadcasted_iota(jnp.int32, (BLK, BLK), 1)
            t = jnp.where(a >= b, t, NEG)
        out_ref[0, d] = t


def toeplitz(base):
    return pl.pallas_call(
        toep_kernel, grid=(H,), in_specs=[pl.BlockSpec((1, NBK, 1, 2 * BLK), lambda h: (h, 0, 0, 0))],
        out_specs=pl.BlockSpec((1, NBK, BLK, BLK), lambda h: (h, 0, 0, 0)),
        out_shape=jax.ShapeDtypeStruct((H, NBK, BLK, BLK), F32), name="bias_tiles")(base)


def make_base(trow):
    rows = []
    for d in range(NBK):
        lo = d * BLK
        a = trow[:, max(lo - BLK + 1, 0):lo + 1][:, ::-1]
        if d == 0:
            a = jnp.concatenate([a, jnp.zeros((H, BLK - 1), F32)], 1)
        b = trow[:, lo + 1:lo + BLK][:, ::-1]
        rows.append(jnp.concatenate([a, jnp.zeros((H, 1), F32), b], 1))
    return jnp.stack(rows, 1)[:, :, None, :]


ANY = pl.BlockSpec(memory_space=pl.ANY)
VM = pl.BlockSpec(memory_space=pltpu.VMEM)
DMA = pltpu.SemaphoreType.DMA
EPS = 1e-6
GATE = 0.7978845608028654


def cst(shape):
    return pl.BlockSpec(shape, lambda *a: (0,) * len(shape), pipeline_mode=pl.Buffered(1))


def col(shape, j):
    return pl.BlockSpec(shape, lambda *a: (0, j), pipeline_mode=pl.Buffered(1))


def sds(shape, dt):
    return jax.ShapeDtypeStruct(shape, dt)


def rows8(v):
    return jnp.sum(v.reshape(v.shape[0] // 8, 8, v.shape[1]), 0)


def norm(x, g):
    return x * lax.rsqrt(jnp.mean(x * x, -1, keepdims=True) + EPS) * g


def norm_grad(x, g, dn):
    r = lax.rsqrt(jnp.mean(x * x, -1, keepdims=True) + EPS)
    gd = g * dn
    dx = r * gd - x * (r * r * r) * jnp.mean(gd * x, -1, keepdims=True)
    return dx, rows8(dn * x * r)


def gelu_pair(x):
    x2 = x * x
    t = jnp.tanh(x * (GATE + GATE * 0.044715 * x2))
    hp = 0.5 + 0.5 * t
    y = x * hp
    d = hp + 0.5 * x * (1.0 - t * t) * (GATE + 3 * GATE * 0.044715 * x2)
    return y, d


def blocks(n=NBK):
    return [slice(i * BLK, (i + 1) * BLK) for i in range(n)]


def self_fwd_kernel(st_ref, x_ref, w_ref, gn_ref, bias_ref, mpre_ref, mpost_ref,
                    q_ref, k_ref, v_ref, att_ref, gain_ref, p_ref, acc_ref, lo_ref):
    h = pl.program_id(0)

    @pl.when(h == 0)
    def _():
        acc_ref[...] = jnp.zeros_like(acc_ref)
        gt = gn_ref[...].astype(F32).T
        gain_ref[...] = gt[:8]
        g = gt[:1]
        for r in blocks():
            n1 = norm(x_ref[r, :].astype(F32), g).astype(BF)
            for j, o in enumerate((q_ref, k_ref, v_ref)):
                o[r, :] = dot(n1, w_ref[:, j * D:(j + 1) * D], 1, 0).astype(BF)
        pos = lax.broadcasted_iota(jnp.int32, (L, 128), 0)
        lo = jnp.zeros((L, 128), jnp.int32)
        for d in range(1, st_ref.shape[0]):
            sd = st_ref[d]
            lo = jnp.where(pos >= sd, sd, lo)
        lo_ref[...] = lo

    mp = mpre_ref[pl.ds(h, 1), :]
    mo = mpost_ref[pl.ds(h, 1), :]

    def scores(i):
        n = (i + 1) * BLK
        qm = (q_ref[i * BLK:n, :].astype(F32) * mp).astype(BF)
        return dot(qm, k_ref[:n, :], 1, 1)

    sc = scores(NBK - 1)
    for i in reversed(range(NBK)):
        nxt = scores(i - 1) if i else None
        n = (i + 1) * BLK
        r = slice(i * BLK, n)
        bias = jnp.concatenate([bias_ref[0, i - j] for j in range(i + 1)], 1) if i else bias_ref[0, 0]
        c = lax.broadcasted_iota(jnp.int32, (BLK, n), 1)
        sc = jnp.where(c >= lo_ref[r, :1], sc + bias, NEG)
        e = jnp.exp(sc - jnp.max(sc, 1, keepdims=True))
        p = (e * (1.0 / jnp.sum(e, 1, keepdims=True))).astype(BF)
        p_ref[0, r, :n] = p
        acc_ref[r, :] += dot(p, v_ref[:n, :], 1, 0) * mo
        sc = nxt

    @pl.when(h == H - 1)
    def _():
        att_ref[...] = acc_ref[...].astype(BF)


def self_fwd(starts, x, w1, bias, mpre, mpost):
    one = cst((L, D))
    return pl.pallas_call(
        self_fwd_kernel,
        grid_spec=pltpu.PrefetchScalarGridSpec(
            num_scalar_prefetch=1, grid=(H,),
            in_specs=[one, col((D, 3 * D), 0), col((D, 128), 18),
                      pl.BlockSpec((1, NBK, BLK, BLK), lambda h, st: (h, 0, 0, 0)), cst((H, D)), cst((H, D))],
            out_specs=[one] * 4 + [cst((8, D)), pl.BlockSpec((1, L, L), lambda h, st: (h, 0, 0))],
            scratch_shapes=[pltpu.VMEM((L, D), F32), pltpu.VMEM((L, 128), jnp.int32)]),
        out_shape=[sds((L, D), BF)] * 4 + [sds((8, D), F32), sds((H, L, L), BF)],
        compiler_params=pltpu.CompilerParams(vmem_limit_bytes=56 << 20),
        cost_estimate=pl.CostEstimate(flops=52_000_000_000, bytes_accessed=45_000_000, transcendentals=8_000_000),
        name="self_fwd")(starts, x, w1, w1, bias, mpre, mpost)


def cross_fwd_kernel(x_ref, att_ref, wo_ref, wq_ref, wk_ref, wv_ref, enc_ref, gain_ref,
                     h1_ref, n2_ref, q_ref, k_ref, v_ref, catt_ref, p_ref):
    h = pl.program_id(0)

    @pl.when(h == 0)
    def _():
        g = gain_ref[1:2, :]
        for r in blocks():
            h1 = x_ref[r, :].astype(F32) + dot(att_ref[r, :], wo_ref[...], 1, 0)
            h1_ref[r, :] = h1
            n2 = norm(h1, g).astype(BF)
            n2_ref[r, :] = n2
            q_ref[r, :] = dot(n2, wq_ref[...], 1, 0).astype(BF)
            k_ref[r, :] = dot(enc_ref[r, :], wk_ref[...], 1, 0).astype(BF)
            v_ref[r, :] = dot(enc_ref[r, :], wv_ref[...], 1, 0).astype(BF)

    cols = pl.ds(pl.multiple_of(h * 128, 128), 128)
    first = lax.broadcasted_iota(jnp.int32, (1, 128), 1) < DH
    k = k_ref[:, cols]
    v = v_ref[:, cols]
    steps = [(r, e) for r in blocks() for e in range(2)]

    def scores(r, e):
        q = q_ref[r, cols]
        return dot(jnp.where(first if e == 0 else ~first, q, jnp.zeros_like(q)), k, 1, 1)

    sc = scores(*steps[0])
    keep = None
    for n, (r, e) in enumerate(steps):
        nxt = scores(*steps[n + 1]) if n + 1 < len(steps) else None
        ex = jnp.exp(sc - jnp.max(sc, 1, keepdims=True))
        p = (ex * (1.0 / jnp.sum(ex, 1, keepdims=True))).astype(BF)
        p_ref[e, r, :] = p
        o = dot(p, v, 1, 0)
        if e == 0:
            keep = o
        else:
            catt_ref[r, cols] = jnp.where(first, keep, o).astype(BF)
        sc = nxt


def cross_fwd(x, att, wmid, enc, gains):
    one = cst((L, D))
    return pl.pallas_call(
        cross_fwd_kernel, grid=(H // 2,),
        in_specs=[one, one] + [col((D, D), j) for j in range(4)] + [one, cst((8, D))],
        out_specs=[one] * 6 + [pl.BlockSpec((2, L, L), lambda h: (h, 0, 0))],
        out_shape=[sds((L, D), F32)] + [sds((L, D), BF)] * 5 + [sds((H, L, L), BF)],
        compiler_params=pltpu.CompilerParams(vmem_limit_bytes=56 << 20),
        cost_estimate=pl.CostEstimate(flops=31_000_000_000, bytes_accessed=50_000_000, transcendentals=12_000_000),
        name="cross_fwd")(x, att, wmid, wmid, wmid, wmid, enc, gains)


def feed_kernel(h1_ref, catt_ref, wco_ref, cot_ref, gain_ref, fi_ref, fo_ref,
                out_ref, bh2_ref, bca_ref, gw_ref, dg_ref,
                n3, n3t, cott, acc, dn, inner, bi):
    a = pl.program_id(0)
    g = gain_ref[2:3, :]

    @pl.when(a == 0)
    def _():
        for r in blocks():
            h2 = h1_ref[r, :] + dot(catt_ref[r, :], wco_ref[...], 1, 0)
            bh2_ref[r, :] = h2
            acc[r, :] = h2
            n3[r, :] = norm(h2, g).astype(BF)
        n3t[...] = n3[...].T
        cott[...] = cot_ref[...].T
        dn[...] = jnp.zeros_like(dn)

    for r in blocks():
        u = dot(n3[r, :], fi_ref[...], 1, 0)
        y, d = gelu_pair(u)
        y = y.astype(BF)
        inner[r, :] = y
        gy = dot(cot_ref[r, :], fo_ref[...], 1, 1)
        b = (gy * d).astype(BF)
        bi[r, :] = b
        acc[r, :] += dot(y, fo_ref[...], 1, 0)
        dn[r, :] += dot(b, fi_ref[...], 1, 1)
    gw_ref[:, :D] = dot(n3t[...], bi[...], 1, 0).astype(BF)
    gw_ref[:, D:] = dot(cott[...], inner[...], 1, 0).T.astype(BF)

    @pl.when(a == pl.num_programs(0) - 1)
    def _():
        dg = jnp.zeros((8, D), F32)
        for r in blocks():
            out_ref[r, :] = acc[r, :].astype(BF)
            dx, s = norm_grad(bh2_ref[r, :], g, dn[r, :])
            dg = dg + s
            b2 = cot_ref[r, :].astype(F32) + dx
            bh2_ref[r, :] = b2
            bca_ref[r, :] = dot(b2.astype(BF), wco_ref[...], 1, 1).astype(BF)
        dg_ref[...] = dg


def feed(h1, catt, wmid, cot, gains, wfeed):
    one = cst((L, D))
    nf = wfeed.shape[1] // (2 * D)
    return pl.pallas_call(
        feed_kernel, grid=(nf,),
        in_specs=[one, one, col((D, D), 4), one, cst((8, D)),
                  pl.BlockSpec((D, D), lambda a: (0, 2 * a)), pl.BlockSpec((D, D), lambda a: (0, 2 * a + 1))],
        out_specs=[one, one, one, pl.BlockSpec((D, 2 * D), lambda a: (0, a)), cst((8, D))],
        out_shape=[sds((L, D), BF), sds((L, D), F32), sds((L, D), BF), sds((D, wfeed.shape[1]), BF), sds((8, D), F32)],
        scratch_shapes=[pltpu.VMEM((L, D), BF), pltpu.VMEM((D, L), BF), pltpu.VMEM((D, L), BF), pltpu.VMEM((L, D), F32),
                        pltpu.VMEM((L, D), F32), pltpu.VMEM((L, D), BF), pltpu.VMEM((L, D), BF)],
        compiler_params=pltpu.CompilerParams(vmem_limit_bytes=60 << 20),
        cost_estimate=pl.CostEstimate(flops=32_000_000_000, bytes_accessed=50_000_000, transcendentals=3_000_000),
        name="feed")(h1, catt, wmid, cot, gains, wfeed, wfeed)


def cross_bwd_kernel(q_ref, k_ref, v_ref, do_ref, p_ref, gain_ref,
                     n2_h, enc_h, att_h, catt_h, h1_h, bh2_h, w_h,
                     gw_ref, genc_ref, bh1_ref, bat_ref, dg_ref,
                     qt, dot_, ds, dq, dk, dv, n2, enc, att, catt, h1, bh2, w, sems):
    h = pl.program_id(0)
    late = [(n2_h, n2), (enc_h, enc), (att_h, att), (catt_h, catt), (h1_h, h1), (bh2_h, bh2)]
    late += [(w_h.at[:, pl.ds(0, 4 * D)], w)]
    copies = [pltpu.make_async_copy(a, b, sems.at[i]) for i, (a, b) in enumerate(late)]

    @pl.when(h == 0)
    def _():
        for c in copies:
            c.start()

    cols = pl.ds(pl.multiple_of(h * 128, 128), 128)
    first = lax.broadcasted_iota(jnp.int32, (1, 128), 1) < DH
    top = lax.broadcasted_iota(jnp.int32, (128, 1), 0) < DH
    k = k_ref[...]
    v = v_ref[...]
    qt[...] = q_ref[...].T
    dot_[...] = do_ref[...].T
    dks, dvs = [], []
    for e in range(2):
        fe = first if e == 0 else ~first
        for r in blocks():
            do = do_ref[r, :]
            dp = dot(jnp.where(fe, do, jnp.zeros_like(do)), v, 1, 1)
            p = p_ref[e, r, :].astype(F32)
            d = (p * (dp - jnp.sum(dp * p, 1, keepdims=True))).astype(BF)
            ds[e, r, :] = d
            o = dot(d, k, 1, 0).astype(BF)
            dq[r, cols] = o if e == 0 else jnp.where(first, dq[r, cols], o)
        dvs.append(dot(dot_[...], p_ref[e], 1, 0))
        dks.append(dot(qt[...], ds[e], 1, 0))
    dk[:, cols] = jnp.where(top, dks[0], dks[1]).T.astype(BF)
    dv[:, cols] = jnp.where(top, dvs[0], dvs[1]).T.astype(BF)

    @pl.when(h == H // 2 - 1)
    def _():
        for c in copies:
            c.wait()
        g = gain_ref[1:2, :]
        dg = jnp.zeros((8, D), F32)
        gw_ref[:, D:2 * D] = dot(n2[...], dq[...], 0, 0).astype(BF)
        gw_ref[:, 2 * D:3 * D] = dot(enc[...], dk[...], 0, 0).astype(BF)
        gw_ref[:, 3 * D:4 * D] = dot(enc[...], dv[...], 0, 0).astype(BF)
        for r in blocks():
            genc_ref[r, :] = (dot(dk[r, :], w[:, 2 * D:3 * D], 1, 1) + dot(dv[r, :], w[:, 3 * D:], 1, 1)).astype(genc_ref.dtype)
            dx, s = norm_grad(h1[r, :], g, dot(dq[r, :], w[:, D:2 * D], 1, 1))
            dg = dg + s
            b2 = bh2[r, :]
            b1 = b2 + dx
            bh1_ref[r, :] = b1
            b1 = b1.astype(BF)
            n2[r, :] = b1
            enc[r, :] = b2.astype(BF)
            bat_ref[r, :] = dot(b1, w[:, :D], 1, 1).astype(BF)
        gw_ref[:, :D] = dot(att[...], n2[...], 0, 0).astype(BF)
        gw_ref[:, 4 * D:] = dot(catt[...], enc[...], 0, 0).astype(BF)
        dg_ref[...] = dg


def cross_bwd(q, k, v, do, p, gains, n2, enc, att, catt, h1, bh2, wmid):
    one = cst((L, D))
    pair = pl.BlockSpec((L, 128), lambda h: (0, h))
    act = pltpu.VMEM((L, D), BF)
    return pl.pallas_call(
        cross_bwd_kernel, grid=(H // 2,),
        in_specs=[pair] * 4 + [pl.BlockSpec((2, L, L), lambda h: (h, 0, 0)), cst((8, D))] + [ANY] * 7,
        out_specs=[cst((D, 5 * D)), one, one, one, cst((8, D))],
        out_shape=[sds((D, 5 * D), BF), sds((L, D), BF), sds((L, D), F32), sds((L, D), BF), sds((8, D), F32)],
        scratch_shapes=[pltpu.VMEM((128, L), BF)] * 2 + [pltpu.VMEM((2, L, L), BF)] + [act] * 7
        + [pltpu.VMEM((L, D), F32)] * 2 + [pltpu.VMEM((D, 4 * D), BF), DMA((7,))],
        compiler_params=pltpu.CompilerParams(vmem_limit_bytes=60 << 20),
        cost_estimate=pl.CostEstimate(flops=37_000_000_000, bytes_accessed=70_000_000, transcendentals=0),
        name="cross_bwd")(q, k, v, do, p, gains, n2, enc, att, catt, h1, bh2, wmid)


def self_bwd_kernel(q_ref, k_ref, v_ref, ba_ref, p_ref, mpre_ref, mpost_ref, gain_ref, x_h, bh1_h, w_h,
                    gw_ref, gtok_ref, gpre_ref, gpost_ref, diag_ref, dg_ref,
                    qt, bat, dqa, dkt, dvt, dm, x, bh1, w, sems):
    h = pl.program_id(0)
    late = [(x_h, x), (bh1_h, bh1), (w_h.at[:, pl.ds(0, 3 * D)], w)]
    copies = [pltpu.make_async_copy(a, b, sems.at[i]) for i, (a, b) in enumerate(late)]

    @pl.when(h == 0)
    def _():
        for c in copies:
            c.start()
        qt[...] = q_ref[...].T
        bat[...] = ba_ref[...].T
        dqa[...] = jnp.zeros_like(dqa)
        dkt[...] = jnp.zeros_like(dkt)
        dvt[...] = jnp.zeros_like(dvt)

    mp = mpre_ref[pl.ds(h, 1), :]
    mo = mpost_ref[pl.ds(h, 1), :]
    gp = jnp.zeros((8, D), F32)
    dacc = [None] * NBK
    for i, r in enumerate(blocks()):
        n = (i + 1) * BLK
        bam = (ba_ref[r, :].astype(F32) * mo).astype(BF)
        dp = dot(bam, v_ref[:n, :], 1, 1)
        p = p_ref[0, r, :n].astype(F32)
        d = p * (dp - jnp.sum(dp * p, 1, keepdims=True))
        for j in range(i + 1):
            t = d[:, j * BLK:(j + 1) * BLK]
            dacc[i - j] = t if dacc[i - j] is None else dacc[i - j] + t
        db = d.astype(BF)
        dm[r, :n] = db
        rr = dot(db, k_ref[:n, :], 1, 0)
        dqa[r, :] += rr * mp
        gp = gp + rows8(rr * q_ref[r, :].astype(F32))
    gpre_ref[pl.ds(h, 1), :] = jnp.sum(gp, 0, keepdims=True)
    for t in range(NBK):
        y = jnp.concatenate([jnp.zeros((BLK, BLK), F32), dacc[t]], 1)
        n = BLK // 2
        while n >= 1:
            y = y[:n] + pltpu.roll(y[n:], 2 * BLK - n, 1)
            n //= 2
        diag_ref[0, t] = y
    mpc = jnp.broadcast_to(mp, (8, D)).T[:, :1]
    moc = jnp.broadcast_to(mo, (8, D)).T[:, :1]
    gq = jnp.zeros((8, D), F32)
    for c in blocks():
        i0 = c.start
        t = dot(bat[:, i0:], p_ref[0, i0:, c], 1, 0)
        dvt[:, c] += t * moc
        gq = gq + rows8(t.T * v_ref[c, :].astype(F32))
        u = dot(qt[:, i0:], dm[i0:, c], 1, 0)
        dkt[:, c] += u * mpc
    gpost_ref[pl.ds(h, 1), :] = jnp.sum(gq, 0, keepdims=True)

    @pl.when(h == H - 1)
    def _():
        for c in copies:
            c.wait()
        g = gain_ref[:1, :]
        dg = jnp.zeros((8, D), F32)
        for r in blocks():
            xr = x[r, :].astype(F32)
            n1 = norm(xr, g).astype(BF)
            dk = dkt[:, r].T.astype(BF)
            dv = dvt[:, r].T.astype(BF)
            dq = dqa[r, :].astype(BF)
            bat[:, r] = n1.T
            dm[r, :D] = dq
            dqa[r, :] = dk.astype(F32)
            back = dot(dq, w[:, :D], 1, 1) + dot(dk, w[:, D:2 * D], 1, 1) + dot(dv, w[:, 2 * D:], 1, 1)
            dx, s = norm_grad(xr, g, back)
            dg = dg + s
            gtok_ref[r, :] = (bh1[r, :] + dx).astype(gtok_ref.dtype)
        gw_ref[:, :D] = dot(bat[...], dm[:, :D], 1, 0).astype(BF)
        gw_ref[:, D:2 * D] = dot(bat[...], dqa[...].astype(BF), 1, 0).astype(BF)
        gw_ref[:, 2 * D:] = dot(bat[...], dvt[...].astype(BF), 1, 1).astype(BF)
        dg_ref[...] = dg


def self_bwd(q, k, v, ba, p, mpre, mpost, gains, x, bh1, w1):
    one = cst((L, D))
    return pl.pallas_call(
        self_bwd_kernel, grid=(H,),
        in_specs=[one] * 4 + [pl.BlockSpec((1, L, L), lambda h: (h, 0, 0)), cst((H, D)), cst((H, D)), cst((8, D))] + [ANY] * 3,
        out_specs=[cst((D, 3 * D)), one, cst((H, D)), cst((H, D)),
                   pl.BlockSpec((1, NBK, 1, 2 * BLK), lambda h: (h, 0, 0, 0)), cst((8, D))],
        out_shape=[sds((D, 3 * D), BF), sds((L, D), BF), sds((H, D), F32), sds((H, D), F32),
                   sds((H, NBK, 1, 2 * BLK), F32), sds((8, D), F32)],
        scratch_shapes=[pltpu.VMEM((D, L), BF)] * 2 + [pltpu.VMEM((L, D), F32)] + [pltpu.VMEM((D, L), F32)] * 2
        + [pltpu.VMEM((L, L), BF), pltpu.VMEM((L, D), BF), pltpu.VMEM((L, D), F32), pltpu.VMEM((D, 3 * D), BF), DMA((3,))],
        compiler_params=pltpu.CompilerParams(vmem_limit_bytes=60 << 20),
        cost_estimate=pl.CostEstimate(flops=128_000_000_000, bytes_accessed=50_000_000, transcendentals=0),
        name="self_bwd")(q, k, v, ba, p, mpre, mpost, gains, x, bh1, w1)


MESH = pl.DeviceIdType.MESH
NS, NZ, NCORE = 4, 4, 2
CHUNK = D


def place():
    s = lax.axis_index("seq")
    d = lax.axis_index("dp")
    return s, d // NCORE, d % NCORE


def flat(s, z, c):
    return (s * NZ + z) * NCORE + c


def partners(s, z, c):
    zs = [{"seq": s, "dp": ((z + k) % NZ) * NCORE + c} for k in (1, 2, 3)]
    ss = [{"seq": (s + k) % NS, "dp": z * NCORE + c} for k in (1, 2, 3)]
    return zs, ss, {"seq": s, "dp": z * NCORE + 1 - c}


def meet(devices):
    bar = pltpu.get_barrier_semaphore()
    for p in devices:
        pl.semaphore_signal(bar, inc=1, device_id=p, device_id_type=MESH)
    pl.semaphore_wait(bar, len(devices))


def remote(src, dst, ssem, rsem, dev):
    return pltpu.make_async_remote_copy(src, dst, ssem, rsem, device_id=dev, device_id_type=MESH)


def weights_in_kernel(w_ref, x_ref, out_ref, xo_ref, ssem, rsem, xs, xr, lsem):
    s, z, c = place()
    zs, ss, co = partners(s, z, c)
    own = flat(s, z, c)
    local = [pltpu.make_async_copy(w_ref, out_ref.at[own], lsem.at[0]),
             pltpu.make_async_copy(x_ref.at[s], xo_ref.at[s], lsem.at[1])]
    for cp in local:
        cp.start()
    meet(zs + ss + [co])
    sends = []

    def send(i, dev, src=None):
        n = len(sends)
        cp = remote(out_ref.at[i] if src is None else src, out_ref.at[i], ssem.at[n], rsem.at[i], dev)
        cp.start()
        sends.append(cp)

    def arrived(i):
        remote(out_ref.at[i], out_ref.at[i], ssem.at[0], rsem.at[i], co).wait_recv()

    for p in zs:
        send(own, p, w_ref)
    xc = []
    for k in (1, 2, 3):
        cp = remote(x_ref.at[(s + k) % NS], xo_ref.at[s], xs.at[k - 1], xr.at[k - 1], ss[k - 1])
        cp.start()
        xc.append(cp)
    for p in ss:
        send(own, p, w_ref)
    send(own, co, w_ref)
    for k in (1, 2, 3):
        i = flat(s, (z + NZ - k) % NZ, c)
        arrived(i)
        for p in ss:
            send(i, p)
        send(i, co)
    for kz in range(NZ):
        for k in (1, 2, 3):
            i = flat((s + NS - k) % NS, (z + NZ - kz) % NZ, c)
            arrived(i)
            send(i, co)
    for kz in range(NZ):
        for k in range(NS):
            arrived(flat((s + k) % NS, (z + kz) % NZ, 1 - c))
    for cp in xc:
        cp.wait_recv()
    for cp in sends + xc:
        cp.wait_send()
    for cp in local:
        cp.wait()


def weights_in(w, x, cid):
    r, n = w.shape
    return pl.pallas_call(
        weights_in_kernel, in_specs=[ANY, ANY], out_specs=[ANY, ANY],
        out_shape=[sds((NS * NZ * NCORE, r, n), w.dtype), sds(x.shape, x.dtype)],
        scratch_shapes=[DMA((31,)), DMA((32,)), DMA((3,)), DMA((3,)), DMA((2,))],
        compiler_params=pltpu.CompilerParams(collective_id=cid, has_side_effects=True),
        name="weights_in")(w, x)


def grads_out_kernel(n, *refs):
    gs, small = refs[:n], refs[n]
    outs, osmall = refs[n + 1:2 * n + 1], refs[2 * n + 1]
    rc, acc, rx, sz, rz, own, mc, mx, mz, cs, cr, xs, xr, zsm, zr, ms, mr = refs[2 * n + 2:]
    s, z, c = place()
    zs, ss, co = partners(s, z, c)
    chunks = [(g, o, pl.ds(j * CHUNK, CHUNK)) for g, o in zip(gs, outs) for j in range(g.shape[2] // CHUNK)]
    meet(zs + ss + [co])
    cs0 = remote(small, mc, ms.at[0], mr.at[0], co)
    cs0.start()
    order = [(k, kz) for k in (2, 1, 3, 0) for kz in (1, 2, 3, 0)]
    sent = [cs0]
    cc = []
    for q, (g, o, cols) in enumerate(chunks):
        cq = []
        for m, (k, kz) in enumerate(order):
            i = flat((s + k) % NS, (z + kz) % NZ, 1 - c)
            cp = remote(g.at[i, :, cols], rc.at[q, flat((s + k) % NS, (z + kz) % NZ, 0) // NCORE], cs.at[q, m],
                        cr.at[q, flat((s + k) % NS, (z + kz) % NZ, 0) // NCORE], co)
            cp.start()
            cq.append(cp)
        cc.append(cq)
        sent += cq
    cs0.wait_recv()
    mx[s] = small[...] + mc[...]
    mxs = []
    for k in (1, 2, 3):
        cp = remote(mx.at[s], mx.at[s], ms.at[k], mr.at[k], ss[k - 1])
        cp.start()
        mxs.append(cp)
    sent += mxs

    def xy_arrived(q, kz):
        g, o, cols = chunks[q]
        v = own[q % 2, kz]
        for k in (2, 1, 3):
            remote(acc.at[0, 0], rx.at[q, kz, k - 1], xs.at[0, 0], xr.at[q, kz, k - 1], ss[k - 1]).wait_recv()
            v = v + rx[q, kz, k - 1].astype(F32)
        if kz:
            sz[q, kz - 1] = v.astype(BF)
            cp = remote(sz.at[q, kz - 1], rz.at[q, kz - 1], zsm.at[q, kz - 1], zr.at[q, kz - 1], zs[kz - 1])
            cp.start()
            sent.append(cp)
        else:
            o[:, cols] = v

    for q, (g, o, cols) in enumerate(chunks):
        for m, (k, kz) in enumerate(order):
            js, jz = (s + k) % NS, (z + kz) % NZ
            cc[q][m].wait_recv()
            v = g[flat(js, jz, c), :, cols].astype(F32) + rc[q, js * NZ + jz].astype(F32)
            if k:
                acc[q, m] = v.astype(BF)
                cp = remote(acc.at[q, m], rx.at[q, kz, k - 1], xs.at[q, m], xr.at[q, kz, k - 1], ss[k - 1])
                cp.start()
                sent.append(cp)
            else:
                own[q % 2, kz] = v
        if q:
            for kz in (1, 2, 3, 0):
                xy_arrived(q - 1, kz)
        if q == 0:
            for cp in mxs:
                cp.wait_recv()
            mz[z] = (mx[0] + mx[1]) + (mx[2] + mx[3])
            mzs = []
            for k in (1, 2, 3):
                cp = remote(mz.at[z], mz.at[z], ms.at[3 + k], mr.at[3 + k], zs[k - 1])
                cp.start()
                mzs.append(cp)
            sent += mzs
    for kz in (1, 2, 3, 0):
        xy_arrived(len(chunks) - 1, kz)
    for cp in mzs:
        cp.wait_recv()
    osmall[...] = (mz[0] + mz[1]) + (mz[2] + mz[3])
    for q, (g, o, cols) in enumerate(chunks):
        for kz in (1, 2, 3):
            remote(sz.at[0, 0], rz.at[q, kz - 1], zsm.at[0, 0], zr.at[q, kz - 1], zs[0]).wait_recv()
            o[:, cols] += rz[q, kz - 1].astype(F32)
    for cp in sent:
        cp.wait_send()


def grads_out(gs, small, cid):
    r = gs[0].shape[1]
    q = sum(g.shape[2] for g in gs) // CHUNK
    sm = pltpu.VMEM(small.shape, F32)
    sm4 = pltpu.VMEM((4,) + small.shape, F32)
    return pl.pallas_call(
        functools.partial(grads_out_kernel, len(gs)),
        in_specs=[VM] * (len(gs) + 1), out_specs=[VM] * (len(gs) + 1),
        out_shape=[sds(g.shape[1:], F32) for g in gs] + [sds(small.shape, F32)],
        scratch_shapes=[pltpu.VMEM((q, 16, r, CHUNK), BF), pltpu.VMEM((q, 12, r, CHUNK), BF), pltpu.VMEM((q, 4, 3, r, CHUNK), BF),
                        pltpu.VMEM((q, 3, r, CHUNK), BF), pltpu.VMEM((q, 3, r, CHUNK), BF), pltpu.VMEM((2, 4, r, CHUNK), F32),
                        sm, sm4, sm4, DMA((q, 16)), DMA((q, 16)), DMA((q, 12)), DMA((q, 4, 3)), DMA((q, 3)), DMA((q, 3)),
                        DMA((7,)), DMA((7,))],
        compiler_params=pltpu.CompilerParams(collective_id=cid, has_side_effects=True, vmem_limit_bytes=56 << 20),
        name="grads_out")(*gs, small)


AX = ("seq", "dp")


def gather(w):
    return lax.all_gather(w, AX, axis=0, tiled=True)


def scatter(g):
    return lax.psum_scatter(g, AX, scatter_dimension=0, tiled=True).astype(F32)


def per_device(tokens, encoded, cotangent, doc_starts, rel_bucket, sq, sk, sv, so, cq, ck, cv, co, fi, fo,
               gs, gc, gf, mix_pre, mix_post, rel_table):
    nseq, ndp = lax.axis_size("seq"), lax.axis_size("dp")
    rows = sq.shape[0]
    nf = fo.shape[0] // rows
    ndev = nseq * ndp
    buckets = rel_table.shape[0]
    near = nseq == NS and ndp == NZ * NCORE and rows % 8 == 0
    to_stream = lambda x: lax.all_to_all(x, "seq", 0, 1, tiled=True).reshape(L, D)
    from_stream = lambda x: lax.all_to_all(x.reshape(1, L, D), "seq", 1, 0, tiled=True)
    gains = jnp.pad(jnp.stack([gs, gc, gf], 1), ((0, 0), (0, 125)))
    w1 = jnp.concatenate([sq, sk, sv, gains], 1)
    wmid = jnp.concatenate([so, cq, ck, cv, co], 1)
    wfeed = jnp.stack([fi.reshape(rows, D, nf).transpose(0, 2, 1), fo.reshape(rows, nf, D)], 2).reshape(rows, 2 * nf * D)
    if near:
        w1, x = weights_in(w1, tokens, 1)
        w1 = w1.reshape(D, -1)
        x = x.reshape(L, D)
    else:
        w1 = gather(w1)
        x = to_stream(tokens)
    wmid = gather(wmid)
    wfeed = gather(wfeed)
    enc = to_stream(encoded)
    cot = to_stream(cotangent)
    starts = lax.dynamic_index_in_dim(doc_starts, lax.axis_index("seq"), 0, keepdims=False)
    hot = (rel_bucket[:, None] == jnp.arange(buckets)[None, :]).astype(F32)
    trow = lax.dot_general(rel_table, hot, (((0,), (1,)), ((), ())), precision=lax.Precision.HIGHEST)
    bias = toeplitz(make_base(trow))
    mpre = jnp.repeat(mix_pre.T, DH, axis=1)
    mpost = jnp.repeat(mix_post, DH, axis=1)
    q, k, v, att, gain, p = self_fwd(starts, x, w1, bias, mpre, mpost)
    h1, n2, cqx, ckx, cvx, catt, cp = cross_fwd(x, att, wmid, enc, gain)
    out, bh2, bca, gw_feed, dgf = feed(h1, catt, wmid, cot, gain, wfeed)
    r_feed = scatter(gw_feed).reshape(rows, nf, 2, D)
    gw_mid, g_enc, bh1, bat, dgc = cross_bwd(cqx, ckx, cvx, bca, cp, gain, n2, enc, att, catt, h1, bh2, wmid)
    gw_qkv, g_tok, gpre, gpost, diag, dgs = self_bwd(q, k, v, bat, p, mpre, mpost, gain, x, bh1, w1)
    gpre = gpre.reshape(H, H, DH).sum(-1).T
    gpost = gpost.reshape(H, H, DH).sum(-1)
    dg = diag[:, :, 0, ::-1]
    gt = 0.0
    for d in range(NBK):
        gt = gt + jnp.pad(dg[:, d], ((0, 0), (d * BLK + 1, L - d * BLK - 1)))
    gt = gt[:, BLK:BLK + L]
    gtab = lax.dot_general(hot, gt, (((0,), (1,)), ((), ())), precision=lax.Precision.HIGHEST)
    dgain = jnp.stack([dgs.sum(0), dgc.sum(0), dgf.sum(0)])
    if near:
        parts = [dgain, gpre, gpost, gtab]
        vec = jnp.concatenate([a.reshape(-1) for a in parts])
        vec = jnp.pad(vec, (0, 3072 - vec.shape[0])).reshape(24, 128)
        r_mid, r_qkv, vec = grads_out([gw_mid.reshape(ndev, rows, -1), gw_qkv.reshape(ndev, rows, -1)], vec, 2)
        vec = vec.reshape(-1)
        o = 0
        got = []
        for a in parts:
            got.append(vec[o:o + a.size].reshape(a.shape))
            o += a.size
        dgain, gpre, gpost, gtab = got
    else:
        r_mid, r_qkv = scatter(gw_mid), scatter(gw_qkv)
        dgain, gpre, gpost, gtab = lax.psum((dgain, gpre, gpost, gtab), AX)
    me = lax.axis_index("seq") * ndp + lax.axis_index("dp")
    dgain = lax.dynamic_slice_in_dim(dgain, me * rows, rows, 1)
    m = lambda a, j: a[:, j * D:(j + 1) * D]
    return (from_stream(out), from_stream(g_tok).astype(F32), from_stream(g_enc).astype(F32),
            m(r_qkv, 0), m(r_qkv, 1), m(r_qkv, 2), m(r_mid, 0), m(r_mid, 1), m(r_mid, 2), m(r_mid, 3), m(r_mid, 4),
            r_feed[:, :, 0].transpose(0, 2, 1).reshape(rows, nf * D), r_feed[:, :, 1].reshape(rows * nf, D),
            dgain[0], dgain[1], dgain[2], gpre, gpost, gtab)


def solution(mesh):
    act = P("dp", "seq", None)
    w = P(AX, None)
    g = P(AX)
    return jax.shard_map(
        per_device, mesh=mesh, in_specs=(act, act, act, P("dp", None), P()) + (w,) * 10 + (g,) * 3 + (P(),) * 3,
        out_specs=(act,) * 3 + (w,) * 10 + (g,) * 3 + (P(),) * 3, check_vma=False)
```

```python
import functools

import jax
import jax.numpy as jnp
from jax import lax
from jax.experimental import pallas as pl
from jax.experimental.pallas import tpu as pltpu
from jax.sharding import PartitionSpec as P

F32 = jnp.float32
BF = jnp.bfloat16
NEG = -1e30
H, DH, D, L = 12, 64, 768, 1024
BLK = 256
NBK = L // BLK


def dot(a, b, ca, cb):
    return lax.dot_general(a, b, (((ca,), (cb,)), ((), ())), preferred_element_type=F32)


def toep_kernel(base_ref, out_ref):
    for d in range(NBK):
        row = jnp.broadcast_to(base_ref[0, d], (BLK, 2 * BLK))
        t = pltpu.roll(row, 0, 1, stride=1, stride_axis=0)[:, :BLK]
        if d == 0:
            a = lax.broadcasted_iota(jnp.int32, (BLK, BLK), 0)
            b = lax.broadcasted_iota(jnp.int32, (BLK, BLK), 1)
            t = jnp.where(a >= b, t, NEG)
        out_ref[0, d] = t


def toeplitz(base):
    return pl.pallas_call(
        toep_kernel, grid=(H,), in_specs=[pl.BlockSpec((1, NBK, 1, 2 * BLK), lambda h: (h, 0, 0, 0))],
        out_specs=pl.BlockSpec((1, NBK, BLK, BLK), lambda h: (h, 0, 0, 0)),
        out_shape=jax.ShapeDtypeStruct((H, NBK, BLK, BLK), F32), name="bias_tiles")(base)


def make_base(trow):
    rows = []
    for d in range(NBK):
        lo = d * BLK
        a = trow[:, max(lo - BLK + 1, 0):lo + 1][:, ::-1]
        if d == 0:
            a = jnp.concatenate([a, jnp.zeros((H, BLK - 1), F32)], 1)
        b = trow[:, lo + 1:lo + BLK][:, ::-1]
        rows.append(jnp.concatenate([a, jnp.zeros((H, 1), F32), b], 1))
    return jnp.stack(rows, 1)[:, :, None, :]


ANY = pl.BlockSpec(memory_space=pl.ANY)
VM = pl.BlockSpec(memory_space=pltpu.VMEM)
DMA = pltpu.SemaphoreType.DMA
MESH = pl.DeviceIdType.MESH
NS, NZ, NCORE = 4, 4, 2
ND = NS * NZ * NCORE


def sds(shape, dt):
    return jax.ShapeDtypeStruct(shape, dt)


def params(mib, cid):
    if cid is None:
        return pltpu.CompilerParams(vmem_limit_bytes=mib << 20)
    return pltpu.CompilerParams(vmem_limit_bytes=mib << 20, collective_id=cid, has_side_effects=True)


def split(refs, n, *groups):
    out = list(refs[:n])
    for g in groups:
        out.append(refs[n:n + g])
        n += g
    return out


def place():
    s = lax.axis_index("seq")
    d = lax.axis_index("dp")
    return s, d // NCORE, d % NCORE


def flat(s, z, c):
    return (s * NZ + z) * NCORE + c


def partners(s, z, c):
    zs = [{"seq": s, "dp": ((z + k) % NZ) * NCORE + c} for k in (1, 2, 3)]
    ss = [{"seq": (s + k) % NS, "dp": z * NCORE + c} for k in (1, 2, 3)]
    return zs, ss, {"seq": s, "dp": z * NCORE + 1 - c}


def meet(devices):
    bar = pltpu.get_barrier_semaphore()
    for p in devices:
        pl.semaphore_signal(bar, inc=1, device_id=p, device_id_type=MESH)
    pl.semaphore_wait(bar, len(devices))


def meet_all():
    zs, ss, co = partners(*place())
    meet(zs + ss + [co])


def meet_seq():
    meet(partners(*place())[1])


def remote(src, dst, ssem, rsem, dev):
    return pltpu.make_async_remote_copy(src, dst, ssem, rsem, device_id=dev, device_id_type=MESH)


class Exchange:
    def __init__(self, src, dst, ss, rs, ls):
        self.s, z, c = place()
        self.src, self.dst, self.ss, self.rs, self.ls = src, dst, ss, rs, ls
        self.to = partners(self.s, z, c)[1]

    @staticmethod
    def sems():
        return [DMA((3,)), DMA((3,)), DMA(())]

    def local(self):
        return pltpu.make_async_copy(self.src.at[self.s], self.dst.at[self.s], self.ls)

    def copy(self, k):
        return remote(self.src.at[(self.s + k) % NS], self.dst.at[self.s], self.ss.at[k - 1], self.rs.at[k - 1], self.to[k - 1])

    def start(self):
        for k in (2, 1, 3):
            self.copy(k).start()
        self.local().start()

    def end(self):
        for k in (1, 2, 3):
            self.copy(k).wait_recv()
            self.copy(k).wait_send()
        self.local().wait()


class Gather:
    def __init__(self, w, out, ssem, rsem, lsem):
        self.w, self.out, self.ssem, self.rsem, self.lsem = w, out, ssem, rsem, lsem
        self.s, self.z, self.c = place()
        self.zs, self.ss, self.co = partners(self.s, self.z, self.c)
        self.own = flat(self.s, self.z, self.c)

    @staticmethod
    def sems():
        return [DMA((ND - 1,)), DMA((ND,)), DMA(())]

    def send(self, i, dev, n, src=None):
        remote(self.out.at[i] if src is None else src, self.out.at[i], self.ssem.at[n], self.rsem.at[i], dev).start()

    def got(self, i):
        remote(self.out.at[i], self.out.at[i], self.ssem.at[0], self.rsem.at[i], self.co).wait_recv()

    def local(self):
        return pltpu.make_async_copy(self.w, self.out.at[self.own], self.lsem)

    def start(self):
        for k in range(3):
            self.send(self.own, self.zs[k], k, self.w)
        for k in range(3):
            self.send(self.own, self.ss[k], 3 + k, self.w)
        self.send(self.own, self.co, 6, self.w)
        self.local().start()

    def line(self, k):
        i = flat(self.s, (self.z + NZ - k) % NZ, self.c)
        self.got(i)
        for j in range(3):
            self.send(i, self.ss[j], 4 * k + 3 + j)
        self.send(i, self.co, 4 * k + 6)

    def plane(self, kz):
        for k in (1, 2, 3):
            i = flat((self.s + NS - k) % NS, (self.z + NZ - kz) % NZ, self.c)
            self.got(i)
            self.send(i, self.co, 19 + 3 * kz + k - 1)

    def end(self):
        for kz in range(NZ):
            for k in range(NS):
                self.got(flat((self.s + k) % NS, (self.z + kz) % NZ, 1 - self.c))
        for n in range(ND - 1):
            remote(self.w, self.out.at[self.own], self.ssem.at[n], self.rsem.at[0], self.co).wait_send()
        self.local().wait()


ORDER = [(k, kz) for k in (2, 1, 3, 0) for kz in (1, 2, 3, 0)]


class Scatter:
    def __init__(self, g, out, mine, rc, acc, rx, own, sz, rz, lsem, cs, cr, xs, xr, zsem, zr):
        self.g, self.out = g, out
        self.mine, self.rc, self.acc, self.rx, self.own, self.sz, self.rz = mine, rc, acc, rx, own, sz, rz
        self.lsem, self.cs, self.cr, self.xs, self.xr, self.zsem, self.zr = lsem, cs, cr, xs, xr, zsem, zr
        self.s, self.z, self.c = place()
        self.zs, self.ss, self.co = partners(self.s, self.z, self.c)

    @staticmethod
    def bufs(shape):
        b = tuple(shape[1:])
        v = lambda *n: pltpu.VMEM(n + b, BF)
        return [v(16), v(16), v(12), v(4, 3), pltpu.VMEM((4,) + b, F32), v(3), v(3),
                DMA((16,)), DMA((16,)), DMA((16,)), DMA((12,)), DMA((4, 3)), DMA((3,)), DMA((3,))]

    def dest(self, m):
        k, kz = ORDER[m]
        return (self.s + k) % NS, (self.z + kz) % NZ

    def core(self, m):
        js, jz = self.dest(m)
        return remote(self.g.at[flat(js, jz, 1 - self.c)], self.rc.at[js * NZ + jz], self.cs.at[m], self.cr.at[js * NZ + jz], self.co)

    def load(self, m):
        js, jz = self.dest(m)
        return pltpu.make_async_copy(self.g.at[flat(js, jz, self.c)], self.mine.at[m], self.lsem.at[m])

    def xy(self, m):
        k, kz = ORDER[m]
        return remote(self.acc.at[m], self.rx.at[kz, k - 1], self.xs.at[m], self.xr.at[kz, k - 1], self.ss[k - 1])

    def zz(self, kz):
        return remote(self.sz.at[kz - 1], self.rz.at[kz - 1], self.zsem.at[kz - 1], self.zr.at[kz - 1], self.zs[kz - 1])

    def start(self):
        for m in range(16):
            self.core(m).start()
        for m in range(16):
            self.load(m).start()

    def plane(self, lo, hi):
        for m in range(lo, hi):
            k, kz = ORDER[m]
            js, jz = self.dest(m)
            self.load(m).wait()
            remote(self.mine.at[0], self.rc.at[js * NZ + jz], self.cs.at[m], self.cr.at[js * NZ + jz], self.co).wait_recv()
            v = self.mine[m].astype(F32) + self.rc[js * NZ + jz].astype(F32)
            if k:
                self.acc[m] = v.astype(BF)
                self.xy(m).start()
            else:
                self.own[kz] = v

    def line(self, lo, hi):
        for kz in (1, 2, 3, 0)[lo:hi]:
            v = self.own[kz]
            for k in (2, 1, 3):
                remote(self.acc.at[0], self.rx.at[kz, k - 1], self.xs.at[0], self.xr.at[kz, k - 1], self.ss[k - 1]).wait_recv()
                v = v + self.rx[kz, k - 1].astype(F32)
            if kz:
                self.sz[kz - 1] = v.astype(BF)
                self.zz(kz).start()
            else:
                self.own[0] = v

    def end(self):
        v = self.own[0]
        for kz in (1, 2, 3):
            self.zz(kz).wait_recv()
            v = v + self.rz[kz - 1].astype(F32)
        self.out[...] = v
        for m in range(16):
            self.core(m).wait_send()
        for m in range(12):
            self.xy(m).wait_send()
        for kz in (1, 2, 3):
            self.zz(kz).wait_send()


def weights_in_kernel(w_ref, x_ref, out_ref, xo_ref, ga, gb, gc, xa, xb, xc):
    gat = Gather(w_ref, out_ref, ga, gb, gc)
    exc = Exchange(x_ref, xo_ref, xa, xb, xc)
    meet_all()
    gat.start()
    exc.start()
    for k in (1, 2, 3):
        gat.line(k)
    for kz in range(NZ):
        gat.plane(kz)
    gat.end()
    exc.end()


def weights_in(w, x, cid):
    return pl.pallas_call(
        weights_in_kernel, in_specs=[ANY, ANY], out_specs=[ANY, ANY],
        out_shape=[sds((ND,) + w.shape, w.dtype), sds(x.shape, x.dtype)],
        scratch_shapes=Gather.sems() + Exchange.sems(),
        compiler_params=params(16, cid), name="weights_in")(w, x)


def grads_out_kernel(n, *refs):
    gs, small, gt = refs[:n], refs[n], refs[n + 1]
    outs, osmall, go = refs[n + 2:2 * n + 2], refs[2 * n + 2], refs[2 * n + 3]
    refs = refs[2 * n + 4:]
    nb = len(Scatter.bufs(gs[0].shape))
    mc, mx, mz, ms, mr, e1, e2, e3 = refs[:8]
    sca = [Scatter(gs[j], outs[j], *refs[8 + j * nb:8 + (j + 1) * nb]) for j in range(n)]
    s, z, c = place()
    zs, ss, co = partners(s, z, c)
    exc = Exchange(gt, go, e1, e2, e3)
    meet_all()
    first = remote(small, mc, ms.at[0], mr.at[0], co)
    first.start()
    for a in sca:
        a.start()
    exc.start()
    first.wait_recv()
    mx[s] = small[...] + mc[...]
    xy = [remote(mx.at[s], mx.at[s], ms.at[k], mr.at[k], ss[k - 1]) for k in (1, 2, 3)]
    for cp in xy:
        cp.start()
    sca[0].plane(0, 16)
    for cp in xy:
        cp.wait_recv()
    mz[z] = (mx[0] + mx[1]) + (mx[2] + mx[3])
    zz = [remote(mz.at[z], mz.at[z], ms.at[3 + k], mr.at[3 + k], zs[k - 1]) for k in (1, 2, 3)]
    for cp in zz:
        cp.start()
    for j in range(1, n):
        sca[j].plane(0, 16)
        sca[j - 1].line(0, 4)
    sca[n - 1].line(0, 4)
    for cp in zz:
        cp.wait_recv()
    osmall[...] = (mz[0] + mz[1]) + (mz[2] + mz[3])
    for a in sca:
        a.end()
    exc.end()
    for cp in [first] + xy + zz:
        cp.wait_send()


def grads_out(gs, small, gt, cid):
    sm = pltpu.VMEM(small.shape, F32)
    sm4 = pltpu.VMEM((4,) + small.shape, F32)
    return pl.pallas_call(
        functools.partial(grads_out_kernel, len(gs)),
        in_specs=[ANY] * len(gs) + [VM, ANY], out_specs=[VM] * (len(gs) + 1) + [ANY],
        out_shape=[sds(g.shape[1:], F32) for g in gs] + [sds(small.shape, F32), sds(gt.shape, BF)],
        scratch_shapes=[sm, sm4, sm4, DMA((7,)), DMA((7,))] + Exchange.sems() + sum([Scatter.bufs(g.shape) for g in gs], []),
        compiler_params=params(56, cid), name="grads_out")(*gs, small, gt)


EPS = 1e-6
GATE = 0.7978845608028654


def cst(shape):
    return pl.BlockSpec(shape, lambda *a: (0,) * len(shape), pipeline_mode=pl.Buffered(1))


def col(shape, j):
    return pl.BlockSpec(shape, lambda *a: (0, j), pipeline_mode=pl.Buffered(1))


def rows8(v):
    return jnp.sum(v.reshape(v.shape[0] // 8, 8, v.shape[1]), 0)


def norm(x, g):
    return x * lax.rsqrt(jnp.mean(x * x, -1, keepdims=True) + EPS) * g


def norm_grad(x, g, dn):
    r = lax.rsqrt(jnp.mean(x * x, -1, keepdims=True) + EPS)
    gd = g * dn
    dx = r * gd - x * (r * r * r) * jnp.mean(gd * x, -1, keepdims=True)
    return dx, rows8(dn * x * r)


def gelu_pair(x):
    x2 = x * x
    t = jnp.tanh(x * (GATE + GATE * 0.044715 * x2))
    hp = 0.5 + 0.5 * t
    y = x * hp
    d = hp + 0.5 * x * (1.0 - t * t) * (GATE + 3 * GATE * 0.044715 * x2)
    return y, d


def blocks(n=NBK):
    return [slice(i * BLK, (i + 1) * BLK) for i in range(n)]


def self_fwd_kernel(near, st_ref, x_ref, w_ref, gn_ref, bias_ref, mpre_ref, mpost_ref, *refs):
    if near:
        wm_h, enc_h, q_ref, k_ref, v_ref, att_ref, gain_ref, p_ref, wo_h, eo_h, acc_ref, lo_ref, ags, exs = split(refs, 12, 3, 3)
        gat = Gather(wm_h, wo_h, *ags)
        exc = Exchange(enc_h, eo_h, *exs)
    else:
        q_ref, k_ref, v_ref, att_ref, gain_ref, p_ref, acc_ref, lo_ref = refs
    h = pl.program_id(0)

    if near:
        @pl.when(h == 0)
        def _():
            meet_all()
            gat.start()
            exc.start()

        for hh, fns in ((2, [lambda: gat.line(1)]), (3, [lambda: gat.line(2), lambda: gat.line(3)]),
                        (7, [lambda: gat.plane(0), lambda: gat.plane(1)]), (9, [lambda: gat.plane(2), lambda: gat.plane(3)])):
            @pl.when(h == hh)
            def _(fns=fns):
                for f in fns:
                    f()

    @pl.when(h == 0)
    def _():
        acc_ref[...] = jnp.zeros_like(acc_ref)
        gt = gn_ref[...].astype(F32).T
        gain_ref[...] = gt[:8]
        g = gt[:1]
        for r in blocks():
            n1 = norm(x_ref[r, :].astype(F32), g).astype(BF)
            for j, o in enumerate((q_ref, k_ref, v_ref)):
                o[r, :] = dot(n1, w_ref[:, j * D:(j + 1) * D], 1, 0).astype(BF)
        pos = lax.broadcasted_iota(jnp.int32, (L, 128), 0)
        lo = jnp.zeros((L, 128), jnp.int32)
        for d in range(1, st_ref.shape[0]):
            sd = st_ref[d]
            lo = jnp.where(pos >= sd, sd, lo)
        lo_ref[...] = lo

    mp = mpre_ref[pl.ds(h, 1), :]
    mo = mpost_ref[pl.ds(h, 1), :]

    def scores(i):
        n = (i + 1) * BLK
        qm = (q_ref[i * BLK:n, :].astype(F32) * mp).astype(BF)
        return dot(qm, k_ref[:n, :], 1, 1)

    sc = scores(NBK - 1)
    for i in reversed(range(NBK)):
        nxt = scores(i - 1) if i else None
        n = (i + 1) * BLK
        r = slice(i * BLK, n)
        bias = jnp.concatenate([bias_ref[0, i - j] for j in range(i + 1)], 1) if i else bias_ref[0, 0]
        c = lax.broadcasted_iota(jnp.int32, (BLK, n), 1)
        sc = jnp.where(c >= lo_ref[r, :1], sc + bias, NEG)
        e = jnp.exp(sc - jnp.max(sc, 1, keepdims=True))
        p = (e * (1.0 / jnp.sum(e, 1, keepdims=True))).astype(BF)
        p_ref[0, r, :n] = p
        acc_ref[r, :] += dot(p, v_ref[:n, :], 1, 0) * mo
        sc = nxt

    @pl.when(h == H - 1)
    def _():
        att_ref[...] = acc_ref[...].astype(BF)
        if near:
            gat.end()
            exc.end()


def self_fwd(starts, x, w1, bias, mpre, mpost, far=None, cid=None):
    one = cst((L, D))
    near = far is not None
    extra_out = [sds((ND,) + far[0].shape, BF), sds(far[1].shape, BF)] if near else []
    return pl.pallas_call(
        functools.partial(self_fwd_kernel, near),
        grid_spec=pltpu.PrefetchScalarGridSpec(
            num_scalar_prefetch=1, grid=(H,),
            in_specs=[one, col((D, 3 * D), 0), col((D, 128), 18),
                      pl.BlockSpec((1, NBK, BLK, BLK), lambda h, st: (h, 0, 0, 0)), cst((H, D)), cst((H, D))]
            + [ANY] * (2 * near),
            out_specs=[one] * 4 + [cst((8, D)), pl.BlockSpec((1, L, L), lambda h, st: (h, 0, 0))] + [ANY] * (2 * near),
            scratch_shapes=[pltpu.VMEM((L, D), F32), pltpu.VMEM((L, 128), jnp.int32)]
            + (Gather.sems() + Exchange.sems() if near else [])),
        out_shape=[sds((L, D), BF)] * 4 + [sds((8, D), F32), sds((H, L, L), BF)] + extra_out,
        compiler_params=params(56, cid),
        cost_estimate=pl.CostEstimate(flops=52_000_000_000, bytes_accessed=45_000_000, transcendentals=8_000_000),
        name="self_fwd")(starts, x, w1, w1, bias, mpre, mpost, *(far or ()))


def cross_fwd_kernel(near, x_ref, att_ref, wo_ref, wq_ref, wk_ref, wv_ref, enc_ref, gain_ref, *refs):
    if near:
        cot_h, h1_ref, n2_ref, q_ref, k_ref, v_ref, catt_ref, p_ref, co_h, exs = split(refs, 9, 3)
        exc = Exchange(cot_h, co_h, *exs)
    else:
        h1_ref, n2_ref, q_ref, k_ref, v_ref, catt_ref, p_ref = refs
    h = pl.program_id(0)

    if near:
        @pl.when(h == 0)
        def _():
            meet_seq()
            exc.start()

    @pl.when(h == 0)
    def _():
        g = gain_ref[1:2, :]
        for r in blocks():
            h1 = x_ref[r, :].astype(F32) + dot(att_ref[r, :], wo_ref[...], 1, 0)
            h1_ref[r, :] = h1
            n2 = norm(h1, g).astype(BF)
            n2_ref[r, :] = n2
            q_ref[r, :] = dot(n2, wq_ref[...], 1, 0).astype(BF)
            k_ref[r, :] = dot(enc_ref[r, :], wk_ref[...], 1, 0).astype(BF)
            v_ref[r, :] = dot(enc_ref[r, :], wv_ref[...], 1, 0).astype(BF)

    cols = pl.ds(pl.multiple_of(h * 128, 128), 128)
    first = lax.broadcasted_iota(jnp.int32, (1, 128), 1) < DH
    k = k_ref[:, cols]
    v = v_ref[:, cols]
    steps = [(r, e) for r in blocks() for e in range(2)]

    def scores(r, e):
        q = q_ref[r, cols]
        return dot(jnp.where(first if e == 0 else ~first, q, jnp.zeros_like(q)), k, 1, 1)

    sc = scores(*steps[0])
    keep = None
    for n, (r, e) in enumerate(steps):
        nxt = scores(*steps[n + 1]) if n + 1 < len(steps) else None
        ex = jnp.exp(sc - jnp.max(sc, 1, keepdims=True))
        p = (ex * (1.0 / jnp.sum(ex, 1, keepdims=True))).astype(BF)
        p_ref[e, r, :] = p
        o = dot(p, v, 1, 0)
        if e == 0:
            keep = o
        else:
            catt_ref[r, cols] = jnp.where(first, keep, o).astype(BF)
        sc = nxt

    if near:
        @pl.when(h == H // 2 - 1)
        def _():
            exc.end()


def cross_fwd(x, att, wmid, enc, gains, far=None, cid=None):
    one = cst((L, D))
    near = far is not None
    return pl.pallas_call(
        functools.partial(cross_fwd_kernel, near), grid=(H // 2,),
        in_specs=[one, one] + [col((D, D), j) for j in range(4)] + [one, cst((8, D))] + [ANY] * near,
        out_specs=[one] * 6 + [pl.BlockSpec((2, L, L), lambda h: (h, 0, 0))] + [ANY] * near,
        out_shape=[sds((L, D), F32)] + [sds((L, D), BF)] * 5 + [sds((H, L, L), BF)] + [sds(f.shape, BF) for f in far or ()],
        scratch_shapes=Exchange.sems() if near else [],
        compiler_params=params(56, cid),
        cost_estimate=pl.CostEstimate(flops=31_000_000_000, bytes_accessed=50_000_000, transcendentals=12_000_000),
        name="cross_fwd")(x, att, wmid, wmid, wmid, wmid, enc, gains, *(far or ()))


def feed_kernel(h1_ref, catt_ref, wco_ref, cot_ref, gain_ref, fi_ref, fo_ref,
                out_ref, bh2_ref, bca_ref, gw_ref, dg_ref,
                n3, n3t, cott, acc, dn, inner, bi):
    a = pl.program_id(0)
    g = gain_ref[2:3, :]

    @pl.when(a == 0)
    def _():
        for r in blocks():
            h2 = h1_ref[r, :] + dot(catt_ref[r, :], wco_ref[...], 1, 0)
            bh2_ref[r, :] = h2
            acc[r, :] = h2
            n3[r, :] = norm(h2, g).astype(BF)
        n3t[...] = n3[...].T
        cott[...] = cot_ref[...].T
        dn[...] = jnp.zeros_like(dn)

    for r in blocks():
        u = dot(n3[r, :], fi_ref[...], 1, 0)
        y, d = gelu_pair(u)
        y = y.astype(BF)
        inner[r, :] = y
        gy = dot(cot_ref[r, :], fo_ref[...], 1, 1)
        b = (gy * d).astype(BF)
        bi[r, :] = b
        acc[r, :] += dot(y, fo_ref[...], 1, 0)
        dn[r, :] += dot(b, fi_ref[...], 1, 1)
    gw_ref[:, :D] = dot(n3t[...], bi[...], 1, 0).astype(BF)
    gw_ref[:, D:] = dot(cott[...], inner[...], 1, 0).T.astype(BF)

    @pl.when(a == pl.num_programs(0) - 1)
    def _():
        dg = jnp.zeros((8, D), F32)
        for r in blocks():
            out_ref[r, :] = acc[r, :].astype(BF)
            dx, s = norm_grad(bh2_ref[r, :], g, dn[r, :])
            dg = dg + s
            b2 = cot_ref[r, :].astype(F32) + dx
            bh2_ref[r, :] = b2
            bca_ref[r, :] = dot(b2.astype(BF), wco_ref[...], 1, 1).astype(BF)
        dg_ref[...] = dg


def feed(h1, catt, wmid, cot, gains, wfeed):
    one = cst((L, D))
    nf = wfeed.shape[1] // (2 * D)
    return pl.pallas_call(
        feed_kernel, grid=(nf,),
        in_specs=[one, one, col((D, D), 4), one, cst((8, D)),
                  pl.BlockSpec((D, D), lambda a: (0, 2 * a)), pl.BlockSpec((D, D), lambda a: (0, 2 * a + 1))],
        out_specs=[one, one, one, pl.BlockSpec((D, 2 * D), lambda a: (0, a)), cst((8, D))],
        out_shape=[sds((L, D), BF), sds((L, D), F32), sds((L, D), BF), sds((D, wfeed.shape[1]), BF), sds((8, D), F32)],
        scratch_shapes=[pltpu.VMEM((L, D), BF), pltpu.VMEM((D, L), BF), pltpu.VMEM((D, L), BF), pltpu.VMEM((L, D), F32),
                        pltpu.VMEM((L, D), F32), pltpu.VMEM((L, D), BF), pltpu.VMEM((L, D), BF)],
        compiler_params=pltpu.CompilerParams(vmem_limit_bytes=60 << 20),
        cost_estimate=pl.CostEstimate(flops=32_000_000_000, bytes_accessed=50_000_000, transcendentals=3_000_000),
        name="feed")(h1, catt, wmid, cot, gains, wfeed, wfeed)


def cross_bwd_kernel(q_ref, k_ref, v_ref, do_ref, p_ref, gain_ref,
                     n2_h, enc_h, att_h, catt_h, h1_h, bh2_h, w_h,
                     gw_ref, genc_ref, bh1_ref, bat_ref, dg_ref,
                     qt, dot_, ds, dq, dk, dv, n2, enc, att, catt, h1, bh2, w, sems):
    h = pl.program_id(0)
    late = [(n2_h, n2), (enc_h, enc), (att_h, att), (catt_h, catt), (h1_h, h1), (bh2_h, bh2)]
    late += [(w_h.at[:, pl.ds(0, 4 * D)], w)]
    copies = [pltpu.make_async_copy(a, b, sems.at[i]) for i, (a, b) in enumerate(late)]

    @pl.when(h == 0)
    def _():
        for c in copies:
            c.start()

    cols = pl.ds(pl.multiple_of(h * 128, 128), 128)
    first = lax.broadcasted_iota(jnp.int32, (1, 128), 1) < DH
    top = lax.broadcasted_iota(jnp.int32, (128, 1), 0) < DH
    k = k_ref[...]
    v = v_ref[...]
    qt[...] = q_ref[...].T
    dot_[...] = do_ref[...].T
    dks, dvs = [], []
    for e in range(2):
        fe = first if e == 0 else ~first
        for r in blocks():
            do = do_ref[r, :]
            dp = dot(jnp.where(fe, do, jnp.zeros_like(do)), v, 1, 1)
            p = p_ref[e, r, :].astype(F32)
            d = (p * (dp - jnp.sum(dp * p, 1, keepdims=True))).astype(BF)
            ds[e, r, :] = d
            o = dot(d, k, 1, 0).astype(BF)
            dq[r, cols] = o if e == 0 else jnp.where(first, dq[r, cols], o)
        dvs.append(dot(dot_[...], p_ref[e], 1, 0))
        dks.append(dot(qt[...], ds[e], 1, 0))
    dk[:, cols] = jnp.where(top, dks[0], dks[1]).T.astype(BF)
    dv[:, cols] = jnp.where(top, dvs[0], dvs[1]).T.astype(BF)

    @pl.when(h == H // 2 - 1)
    def _():
        for c in copies:
            c.wait()
        g = gain_ref[1:2, :]
        dg = jnp.zeros((8, D), F32)
        gw_ref[:, D:2 * D] = dot(n2[...], dq[...], 0, 0).astype(BF)
        gw_ref[:, 2 * D:3 * D] = dot(enc[...], dk[...], 0, 0).astype(BF)
        gw_ref[:, 3 * D:4 * D] = dot(enc[...], dv[...], 0, 0).astype(BF)
        for r in blocks():
            genc_ref[r, :] = (dot(dk[r, :], w[:, 2 * D:3 * D], 1, 1) + dot(dv[r, :], w[:, 3 * D:], 1, 1)).astype(genc_ref.dtype)
            dx, s = norm_grad(h1[r, :], g, dot(dq[r, :], w[:, D:2 * D], 1, 1))
            dg = dg + s
            b2 = bh2[r, :]
            b1 = b2 + dx
            bh1_ref[r, :] = b1
            b1 = b1.astype(BF)
            n2[r, :] = b1
            enc[r, :] = b2.astype(BF)
            bat_ref[r, :] = dot(b1, w[:, :D], 1, 1).astype(BF)
        gw_ref[:, :D] = dot(att[...], n2[...], 0, 0).astype(BF)
        gw_ref[:, 4 * D:] = dot(catt[...], enc[...], 0, 0).astype(BF)
        dg_ref[...] = dg


def cross_bwd(q, k, v, do, p, gains, n2, enc, att, catt, h1, bh2, wmid):
    one = cst((L, D))
    pair = pl.BlockSpec((L, 128), lambda h: (0, h))
    act = pltpu.VMEM((L, D), BF)
    return pl.pallas_call(
        cross_bwd_kernel, grid=(H // 2,),
        in_specs=[pair] * 4 + [pl.BlockSpec((2, L, L), lambda h: (h, 0, 0)), cst((8, D))] + [ANY] * 7,
        out_specs=[cst((D, 5 * D)), one, one, one, cst((8, D))],
        out_shape=[sds((D, 5 * D), BF), sds((L, D), BF), sds((L, D), F32), sds((L, D), BF), sds((8, D), F32)],
        scratch_shapes=[pltpu.VMEM((128, L), BF)] * 2 + [pltpu.VMEM((2, L, L), BF)] + [act] * 7
        + [pltpu.VMEM((L, D), F32)] * 2 + [pltpu.VMEM((D, 4 * D), BF), DMA((7,))],
        compiler_params=pltpu.CompilerParams(vmem_limit_bytes=60 << 20),
        cost_estimate=pl.CostEstimate(flops=37_000_000_000, bytes_accessed=70_000_000, transcendentals=0),
        name="cross_bwd")(q, k, v, do, p, gains, n2, enc, att, catt, h1, bh2, wmid)


def self_bwd_kernel(near, q_ref, k_ref, v_ref, ba_ref, p_ref, mpre_ref, mpost_ref, gain_ref, x_h, bh1_h, w_h, *refs):
    if near:
        gm_h, out_h, ge_h = refs[:3]
        gq_ref, gk_ref, gv_ref, gtok_ref, gpre_ref, gpost_ref, diag_ref, dg_ref, rm_ref, oo_h, go_h = refs[3:14]
        qt, bat, dqa, dkt, dvt, dm, x, bh1, w, sems, sca, ex1, ex2 = split(refs[14:], 10, len(Scatter.bufs(gm_h.shape)), 3, 3)
        sca = Scatter(gm_h, rm_ref, *sca)
        exc = [Exchange(out_h, oo_h, *ex1), Exchange(ge_h, go_h, *ex2)]
    else:
        gq_ref, gk_ref, gv_ref, gtok_ref, gpre_ref, gpost_ref, diag_ref, dg_ref = refs[:8]
        qt, bat, dqa, dkt, dvt, dm, x, bh1, w, sems = refs[8:]
    h = pl.program_id(0)

    if near:
        @pl.when(h == 0)
        def _():
            meet_all()
            sca.start()
            for e in exc:
                e.start()

        for hh, lo, hi in ((1, 0, 6), (2, 6, 12), (3, 12, 16)):
            @pl.when(h == hh)
            def _(lo=lo, hi=hi):
                sca.plane(lo, hi)

        for hh, lo, hi in ((9, 0, 2), (10, 2, 4)):
            @pl.when(h == hh)
            def _(lo=lo, hi=hi):
                sca.line(lo, hi)
    late = [(x_h, x), (bh1_h, bh1), (w_h.at[:, pl.ds(0, 3 * D)], w)]
    copies = [pltpu.make_async_copy(a, b, sems.at[i]) for i, (a, b) in enumerate(late)]

    @pl.when(h == 0)
    def _():
        for c in copies:
            c.start()
        qt[...] = q_ref[...].T
        bat[...] = ba_ref[...].T
        dqa[...] = jnp.zeros_like(dqa)
        dkt[...] = jnp.zeros_like(dkt)
        dvt[...] = jnp.zeros_like(dvt)

    mp = mpre_ref[pl.ds(h, 1), :]
    mo = mpost_ref[pl.ds(h, 1), :]
    gp = jnp.zeros((8, D), F32)
    dacc = [None] * NBK
    for i, r in enumerate(blocks()):
        n = (i + 1) * BLK
        bam = (ba_ref[r, :].astype(F32) * mo).astype(BF)
        dp = dot(bam, v_ref[:n, :], 1, 1)
        p = p_ref[0, r, :n].astype(F32)
        d = p * (dp - jnp.sum(dp * p, 1, keepdims=True))
        for j in range(i + 1):
            t = d[:, j * BLK:(j + 1) * BLK]
            dacc[i - j] = t if dacc[i - j] is None else dacc[i - j] + t
        db = d.astype(BF)
        dm[r, :n] = db
        rr = dot(db, k_ref[:n, :], 1, 0)
        dqa[r, :] += rr * mp
        gp = gp + rows8(rr * q_ref[r, :].astype(F32))
    gpre_ref[pl.ds(h, 1), :] = jnp.sum(gp, 0, keepdims=True)
    for t in range(NBK):
        y = jnp.concatenate([jnp.zeros((BLK, BLK), F32), dacc[t]], 1)
        n = BLK // 2
        while n >= 1:
            y = y[:n] + pltpu.roll(y[n:], 2 * BLK - n, 1)
            n //= 2
        diag_ref[0, t] = y
    mpc = jnp.broadcast_to(mp, (8, D)).T[:, :1]
    moc = jnp.broadcast_to(mo, (8, D)).T[:, :1]
    gq = jnp.zeros((8, D), F32)
    for c in blocks():
        i0 = c.start
        t = dot(bat[:, i0:], p_ref[0, i0:, c], 1, 0)
        dvt[:, c] += t * moc
        gq = gq + rows8(t.T * v_ref[c, :].astype(F32))
        u = dot(qt[:, i0:], dm[i0:, c], 1, 0)
        dkt[:, c] += u * mpc
    gpost_ref[pl.ds(h, 1), :] = jnp.sum(gq, 0, keepdims=True)

    @pl.when(h == H - 1)
    def _():
        for c in copies:
            c.wait()
        g = gain_ref[:1, :]
        dg = jnp.zeros((8, D), F32)
        for r in blocks():
            xr = x[r, :].astype(F32)
            n1 = norm(xr, g).astype(BF)
            dk = dkt[:, r].T.astype(BF)
            dv = dvt[:, r].T.astype(BF)
            dq = dqa[r, :].astype(BF)
            bat[:, r] = n1.T
            dm[r, :D] = dq
            dqa[r, :] = dk.astype(F32)
            back = dot(dq, w[:, :D], 1, 1) + dot(dk, w[:, D:2 * D], 1, 1) + dot(dv, w[:, 2 * D:], 1, 1)
            dx, s = norm_grad(xr, g, back)
            dg = dg + s
            gtok_ref[r, :] = (bh1[r, :] + dx).astype(gtok_ref.dtype)
        gq_ref[...] = dot(bat[...], dm[:, :D], 1, 0).astype(BF)
        gk_ref[...] = dot(bat[...], dqa[...].astype(BF), 1, 0).astype(BF)
        gv_ref[...] = dot(bat[...], dvt[...].astype(BF), 1, 1).astype(BF)
        dg_ref[...] = dg
        if near:
            sca.end()
            for e in exc:
                e.end()


def self_bwd(q, k, v, ba, p, mpre, mpost, gains, x, bh1, w1, far=None, cid=None):
    one = cst((L, D))
    near = far is not None
    more = [cst(far[0].shape[1:]), ANY, ANY] if near else []
    more_out = [sds(far[0].shape[1:], F32)] + [sds(f.shape, BF) for f in far[1:]] if near else []
    return pl.pallas_call(
        functools.partial(self_bwd_kernel, near), grid=(H,),
        in_specs=[one] * 4 + [pl.BlockSpec((1, L, L), lambda h: (h, 0, 0)), cst((H, D)), cst((H, D)), cst((8, D))] + [ANY] * (3 + 3 * near),
        out_specs=[cst((D, D))] * 3 + [one, cst((H, D)), cst((H, D)),
                   pl.BlockSpec((1, NBK, 1, 2 * BLK), lambda h: (h, 0, 0, 0)), cst((8, D))] + more,
        out_shape=[sds((D, D), BF)] * 3 + [sds((L, D), BF), sds((H, D), F32), sds((H, D), F32),
                   sds((H, NBK, 1, 2 * BLK), F32), sds((8, D), F32)] + more_out,
        scratch_shapes=[pltpu.VMEM((D, L), BF)] * 2 + [pltpu.VMEM((L, D), F32)] + [pltpu.VMEM((D, L), F32)] * 2
        + [pltpu.VMEM((L, L), BF), pltpu.VMEM((L, D), BF), pltpu.VMEM((L, D), F32), pltpu.VMEM((D, 3 * D), BF), DMA((3,))]
        + (Scatter.bufs(far[0].shape) + Exchange.sems() * 2 if near else []),
        compiler_params=params(61, cid),
        cost_estimate=pl.CostEstimate(flops=128_000_000_000, bytes_accessed=50_000_000, transcendentals=0),
        name="self_bwd")(q, k, v, ba, p, mpre, mpost, gains, x, bh1, w1, *(far or ()))


AX = ("seq", "dp")


def gather(w):
    return lax.all_gather(w, AX, axis=0, tiled=True)


def scatter(g):
    return lax.psum_scatter(g, AX, scatter_dimension=0, tiled=True).astype(F32)


def per_device(tokens, encoded, cotangent, doc_starts, rel_bucket, sq, sk, sv, so, cq, ck, cv, co, fi, fo,
               gs, gc, gf, mix_pre, mix_post, rel_table):
    nseq, ndp = lax.axis_size("seq"), lax.axis_size("dp")
    rows = sq.shape[0]
    nf = fo.shape[0] // rows
    ndev = nseq * ndp
    buckets = rel_table.shape[0]
    near = nseq == NS and ndp == NZ * NCORE and rows % 8 == 0
    to_stream = lambda x: lax.all_to_all(x, "seq", 0, 1, tiled=True).reshape(L, D)
    from_stream = lambda x: lax.all_to_all(x.reshape(1, L, D), "seq", 1, 0, tiled=True)
    gains = jnp.pad(jnp.stack([gs, gc, gf], 1), ((0, 0), (0, 125)))
    w1 = jnp.concatenate([sq, sk, sv, gains], 1)
    wmid = jnp.concatenate([so, cq, ck, cv, co], 1)
    wfeed = jnp.stack([fi.reshape(rows, D, nf).transpose(0, 2, 1), fo.reshape(rows, nf, D)], 2).reshape(rows, 2 * nf * D)
    if near:
        w1, x = weights_in(w1, tokens, 1)
        w1 = w1.reshape(D, -1)
        x = x.reshape(L, D)
    else:
        w1 = gather(w1)
        x = to_stream(tokens)
        wmid = gather(wmid)
        enc = to_stream(encoded)
        cot = to_stream(cotangent)
    wfeed = gather(wfeed)
    starts = lax.dynamic_index_in_dim(doc_starts, lax.axis_index("seq"), 0, keepdims=False)
    hot = (rel_bucket[:, None] == jnp.arange(buckets)[None, :]).astype(F32)
    trow = lax.dot_general(rel_table, hot, (((0,), (1,)), ((), ())), precision=lax.Precision.HIGHEST)
    bias = toeplitz(make_base(trow))
    mpre = jnp.repeat(mix_pre.T, DH, axis=1)
    mpost = jnp.repeat(mix_post, DH, axis=1)
    if near:
        q, k, v, att, gain, p, wmid, enc = self_fwd(starts, x, w1, bias, mpre, mpost, (wmid, encoded), 2)
        wmid = wmid.reshape(D, -1)
        enc = enc.reshape(L, D)
        h1, n2, cqx, ckx, cvx, catt, cp, cot = cross_fwd(x, att, wmid, enc, gain, (cotangent,), 3)
        cot = cot.reshape(L, D)
    else:
        q, k, v, att, gain, p = self_fwd(starts, x, w1, bias, mpre, mpost)
        h1, n2, cqx, ckx, cvx, catt, cp = cross_fwd(x, att, wmid, enc, gain)
    out, bh2, bca, gw_feed, dgf = feed(h1, catt, wmid, cot, gain, wfeed)
    r_feed = scatter(gw_feed).reshape(rows, nf, 2, D)
    gw_mid, g_enc, bh1, bat, dgc = cross_bwd(cqx, ckx, cvx, bca, cp, gain, n2, enc, att, catt, h1, bh2, wmid)
    blk = lambda a: a.reshape(nseq, L // nseq, D)
    if near:
        far = (gw_mid.reshape(ndev, rows, -1), blk(out), blk(g_enc))
        gw_q, gw_k, gw_v, g_tok, gpre, gpost, diag, dgs, r_mid, out, g_enc = self_bwd(
            q, k, v, bat, p, mpre, mpost, gain, x, bh1, w1, far, 4)
    else:
        gw_q, gw_k, gw_v, g_tok, gpre, gpost, diag, dgs = self_bwd(q, k, v, bat, p, mpre, mpost, gain, x, bh1, w1)
    gpre = gpre.reshape(H, H, DH).sum(-1).T
    gpost = gpost.reshape(H, H, DH).sum(-1)
    dg = diag[:, :, 0, ::-1]
    gt = 0.0
    for d in range(NBK):
        gt = gt + jnp.pad(dg[:, d], ((0, 0), (d * BLK + 1, L - d * BLK - 1)))
    gt = gt[:, BLK:BLK + L]
    gtab = lax.dot_general(hot, gt, (((0,), (1,)), ((), ())), precision=lax.Precision.HIGHEST)
    dgain = jnp.stack([dgs.sum(0), dgc.sum(0), dgf.sum(0)])
    if near:
        parts = [dgain, gpre, gpost, gtab]
        vec = jnp.concatenate([a.reshape(-1) for a in parts])
        vec = jnp.pad(vec, (0, 3072 - vec.shape[0])).reshape(24, 128)
        r_q, r_k, r_v, vec, g_tok = grads_out([a.reshape(ndev, rows, -1) for a in (gw_q, gw_k, gw_v)], vec, blk(g_tok), 5)
        vec = vec.reshape(-1)
        o = 0
        got = []
        for a in parts:
            got.append(vec[o:o + a.size].reshape(a.shape))
            o += a.size
        dgain, gpre, gpost, gtab = got
    else:
        r_mid, r_q, r_k, r_v = scatter(gw_mid), scatter(gw_q), scatter(gw_k), scatter(gw_v)
        out, g_tok, g_enc = from_stream(out), from_stream(g_tok), from_stream(g_enc)
        dgain, gpre, gpost, gtab = lax.psum((dgain, gpre, gpost, gtab), AX)
    me = lax.axis_index("seq") * ndp + lax.axis_index("dp")
    dgain = lax.dynamic_slice_in_dim(dgain, me * rows, rows, 1)
    m = lambda a, j: a[:, j * D:(j + 1) * D]
    return (out, g_tok.astype(F32), g_enc.astype(F32),
            r_q, r_k, r_v, m(r_mid, 0), m(r_mid, 1), m(r_mid, 2), m(r_mid, 3), m(r_mid, 4),
            r_feed[:, :, 0].transpose(0, 2, 1).reshape(rows, nf * D), r_feed[:, :, 1].reshape(rows * nf, D),
            dgain[0], dgain[1], dgain[2], gpre, gpost, gtab)


def solution(mesh):
    act = P("dp", "seq", None)
    w = P(AX, None)
    g = P(AX)
    return jax.shard_map(
        per_device, mesh=mesh, in_specs=(act, act, act, P("dp", None), P()) + (w,) * 10 + (g,) * 3 + (P(),) * 3,
        out_specs=(act,) * 3 + (w,) * 10 + (g,) * 3 + (P(),) * 3, check_vma=False)
```

```python
import functools

import jax
import jax.numpy as jnp
from jax import lax
from jax.experimental import pallas as pl
from jax.experimental.pallas import tpu as pltpu
from jax.sharding import PartitionSpec as P

F32 = jnp.float32
BF = jnp.bfloat16
NEG = -1e30
H, DH, D, L = 12, 64, 768, 1024
BLK = 256
NBK = L // BLK


def dot(a, b, ca, cb):
    return lax.dot_general(a, b, (((ca,), (cb,)), ((), ())), preferred_element_type=F32)


def bias_tiles(base_ref, h, out_ref):
    for d in range(NBK):
        row = jnp.broadcast_to(base_ref[h, d], (BLK, 2 * BLK))
        t = pltpu.roll(row, 0, 1, stride=1, stride_axis=0)[:, :BLK]
        if d == 0:
            a = lax.broadcasted_iota(jnp.int32, (BLK, BLK), 0)
            b = lax.broadcasted_iota(jnp.int32, (BLK, BLK), 1)
            t = jnp.where(a >= b, t, NEG)
        out_ref[d] = t


def toeplitz(base):
    def kernel(base_ref, out_ref):
        bias_tiles(base_ref, 0, out_ref.at[0])

    return pl.pallas_call(
        kernel, grid=(H,), in_specs=[pl.BlockSpec((1, NBK, 1, 2 * BLK), lambda h: (h, 0, 0, 0))],
        out_specs=pl.BlockSpec((1, NBK, BLK, BLK), lambda h: (h, 0, 0, 0)),
        out_shape=jax.ShapeDtypeStruct((H, NBK, BLK, BLK), F32), name="bias_tiles")(base)


def make_base(trow):
    rows = []
    for d in range(NBK):
        lo = d * BLK
        a = trow[:, max(lo - BLK + 1, 0):lo + 1][:, ::-1]
        if d == 0:
            a = jnp.concatenate([a, jnp.zeros((H, BLK - 1), F32)], 1)
        b = trow[:, lo + 1:lo + BLK][:, ::-1]
        rows.append(jnp.concatenate([a, jnp.zeros((H, 1), F32), b], 1))
    return jnp.stack(rows, 1)[:, :, None, :]


ANY = pl.BlockSpec(memory_space=pl.ANY)
VM = pl.BlockSpec(memory_space=pltpu.VMEM)
DMA = pltpu.SemaphoreType.DMA
MESH = pl.DeviceIdType.MESH
NS, NZ, NCORE = 4, 4, 2
ND = NS * NZ * NCORE


def sds(shape, dt):
    return jax.ShapeDtypeStruct(shape, dt)


def params(mib, cid):
    if cid is None:
        return pltpu.CompilerParams(vmem_limit_bytes=mib << 20)
    return pltpu.CompilerParams(vmem_limit_bytes=mib << 20, collective_id=cid, has_side_effects=True)


def split(refs, n, *groups):
    out = list(refs[:n])
    for g in groups:
        out.append(refs[n:n + g])
        n += g
    return out


def place():
    s = lax.axis_index("seq")
    d = lax.axis_index("dp")
    return s, d // NCORE, d % NCORE


def flat(s, z, c):
    return (s * NZ + z) * NCORE + c


def partners(s, z, c):
    zs = [{"seq": s, "dp": ((z + k) % NZ) * NCORE + c} for k in (1, 2, 3)]
    ss = [{"seq": (s + k) % NS, "dp": z * NCORE + c} for k in (1, 2, 3)]
    return zs, ss, {"seq": s, "dp": z * NCORE + 1 - c}


def plane(s):
    return s + 1 - 2 * (s % 2), (s + 2) % NS, NS - 1 - s


def meet(devices):
    bar = pltpu.get_barrier_semaphore()
    for p in devices:
        pl.semaphore_signal(bar, inc=1, device_id=p, device_id_type=MESH)
    pl.semaphore_wait(bar, len(devices))


def meet_all():
    zs, ss, co = partners(*place())
    meet(zs + ss + [co])


def meet_seq():
    meet(partners(*place())[1])


def remote(src, dst, ssem, rsem, dev):
    return pltpu.make_async_remote_copy(src, dst, ssem, rsem, device_id=dev, device_id_type=MESH)


class Exchange:
    def __init__(self, src, dst, ss, rs, ls, part=(0, 1)):
        self.s, z, c = place()
        self.src, self.dst, self.ss, self.rs, self.ls = src, dst, ss, rs, ls
        n = src.shape[1] // part[1]
        self.rows = pl.ds(part[0] * n, n)
        self.to = partners(self.s, z, c)[1]

    @staticmethod
    def sems():
        return [DMA((3,)), DMA((3,)), DMA(())]

    def local(self):
        return pltpu.make_async_copy(self.src.at[self.s, self.rows], self.dst.at[self.s, self.rows], self.ls)

    def copy(self, k):
        return remote(self.src.at[(self.s + k) % NS, self.rows], self.dst.at[self.s, self.rows], self.ss.at[k - 1], self.rs.at[k - 1], self.to[k - 1])

    def start(self):
        for k in (2, 1, 3):
            self.copy(k).start()
        self.local().start()

    def end(self):
        for k in (1, 2, 3):
            self.copy(k).wait_recv()
            self.copy(k).wait_send()
        self.local().wait()


class Gather:
    def __init__(self, w, out, ssem, rsem, lsem, cols=None):
        self.w, self.out, self.ssem, self.rsem, self.lsem, self.cols = w, out, ssem, rsem, lsem, cols
        self.s, self.z, self.c = place()
        self.zs, self.ss, self.co = partners(self.s, self.z, self.c)
        self.px, self.py, self.pd = plane(self.s)

    @staticmethod
    def sems():
        return [DMA((ND - 1,)), DMA((ND,)), DMA(())]

    def slot(self, i):
        return self.out.at[i] if self.cols is None else self.out.at[i, :, self.cols]

    def at(self, s, kz, c):
        return flat(s, (self.z + NZ - kz) % NZ, c)

    def there(self, s):
        return {"seq": s, "dp": self.z * NCORE + self.c}

    def send(self, i, dev, n, src=None):
        remote(self.slot(i) if src is None else src, self.slot(i), self.ssem.at[n], self.rsem.at[i], dev).start()

    def got(self, i):
        remote(self.slot(i), self.slot(i), self.ssem.at[0], self.rsem.at[i], self.co).wait_recv()

    def local(self):
        return pltpu.make_async_copy(self.w, self.slot(self.at(self.s, 0, self.c)), self.lsem)

    def start(self):
        own = self.at(self.s, 0, self.c)
        for k in range(3):
            self.send(own, self.zs[k], k, self.w)
        self.send(own, self.there(self.px), 3, self.w)
        self.send(own, self.there(self.py), 4, self.w)
        self.send(own, self.co, 5, self.w)
        self.local().start()

    def line(self, k):
        i = self.at(self.s, k, self.c)
        self.got(i)
        self.send(i, self.there(self.px), 3 * k + 3)
        self.send(i, self.there(self.py), 3 * k + 4)
        self.send(i, self.co, 3 * k + 5)

    def hop(self, kz):
        for j, (a, b) in enumerate(((self.px, self.py), (self.py, self.px))):
            i = self.at(a, kz, self.c)
            self.got(i)
            if kz % 2 == j:
                self.send(i, self.there(b), 15 + kz)
            self.send(i, self.co, 19 + 3 * kz + j)

    def diag(self, kz):
        i = self.at(self.pd, kz, self.c)
        self.got(i)
        self.send(i, self.co, 21 + 3 * kz)

    def end(self):
        for kz in range(NZ):
            for k in range(NS):
                self.got(self.at((self.s + k) % NS, kz, 1 - self.c))
        for n in range(ND - 1):
            remote(self.w, self.slot(0), self.ssem.at[n], self.rsem.at[0], self.co).wait_send()
        self.local().wait()


class LineGather:
    def __init__(self, w, out, ss, rs, ls):
        self.w, self.out, self.ss, self.rs, self.ls = w, out, ss, rs, ls
        s, self.z, c = place()
        self.zs = partners(s, self.z, c)[0]

    @staticmethod
    def sems():
        return [DMA((3,)), DMA((3,)), DMA(())]

    def local(self):
        return pltpu.make_async_copy(self.w, self.out.at[self.z], self.ls)

    def copy(self, k):
        return remote(self.w, self.out.at[self.z], self.ss.at[k], self.rs.at[k], self.zs[k])

    def start(self):
        for k in range(3):
            self.copy(k).start()
        self.local().start()

    def end(self):
        for k in range(3):
            self.copy(k).wait_recv()
            self.copy(k).wait_send()
        self.local().wait()


class PlaneGather(Gather):
    def src(self, kz):
        return self.w.at[(self.z + NZ - kz) % NZ]

    def local(self, kz):
        return pltpu.make_async_copy(self.src(kz), self.slot(self.at(self.s, kz, self.c)), self.lsem.at[kz])

    @staticmethod
    def sems():
        return [DMA((ND - 4,)), DMA((ND,)), DMA((4,))]

    def start(self):
        for kz in range(NZ):
            i = self.at(self.s, kz, self.c)
            self.send(i, self.there(self.px), 3 * kz, self.src(kz))
            self.send(i, self.there(self.py), 3 * kz + 1, self.src(kz))
            self.send(i, self.co, 3 * kz + 2, self.src(kz))
            self.local(kz).start()

    def hop(self, kz):
        for j, (a, b) in enumerate(((self.px, self.py), (self.py, self.px))):
            i = self.at(a, kz, self.c)
            self.got(i)
            if kz % 2 == j:
                self.send(i, self.there(b), 12 + kz)
            self.send(i, self.co, 16 + 3 * kz + j)

    def diag(self, kz):
        i = self.at(self.pd, kz, self.c)
        self.got(i)
        self.send(i, self.co, 18 + 3 * kz)

    def end(self):
        for kz in range(NZ):
            for k in range(NS):
                self.got(self.at((self.s + k) % NS, kz, 1 - self.c))
        for n in range(ND - 4):
            remote(self.src(0), self.slot(0), self.ssem.at[n], self.rsem.at[0], self.co).wait_send()
        for kz in range(NZ):
            self.local(kz).wait()


class Scatter:
    def __init__(self, g, cols, outs, mine, rc, rd, rn, rz, lsem, cs, cr, xs, dr, nr, zsem, zr):
        self.g, self.cols, self.outs = g, cols, outs
        self.mine, self.rc, self.rd, self.rn, self.rz = mine, rc, rd, rn, rz
        self.lsem, self.cs, self.cr, self.xs, self.dr, self.nr, self.zsem, self.zr = lsem, cs, cr, xs, dr, nr, zsem, zr
        self.s, self.z, self.c = place()
        self.zs, self.ss, self.co = partners(self.s, self.z, self.c)
        self.col = (self.s,) + plane(self.s)

    @staticmethod
    def bufs(rows, cols):
        v = lambda *n: pltpu.VMEM(n + (rows, cols), BF)
        return [v(16), v(16), v(4), v(2, 4), v(3), DMA((16,)), DMA((16,)), DMA((16,)), DMA((12,)), DMA((4,)), DMA((2, 4)),
                DMA((3,)), DMA((3,))]

    def part(self, m, c):
        return self.g.at[flat(self.col[m // 4], (self.z + m % 4) % NZ, c), :, self.cols]

    def core(self, m):
        return remote(self.part(m, 1 - self.c), self.rc.at[m], self.cs.at[m], self.cr.at[m], self.co)

    def load(self, m):
        return pltpu.make_async_copy(self.part(m, self.c), self.mine.at[m], self.lsem.at[m])

    def to_plane(self, m, via, dst, sem):
        return remote(self.mine.at[m], dst, self.xs.at[m - 4], sem, {"seq": self.col[via], "dp": self.z * NCORE + self.c})

    def to_via(self, kz):
        return self.to_plane(12 + kz, 2 - kz % 2, self.rd.at[kz], self.dr.at[kz])

    def to_next(self, a, kz):
        return self.to_plane(4 * a + kz, a, self.rn.at[a - 1, kz], self.nr.at[a - 1, kz])

    def zz(self, kz):
        return remote(self.mine.at[kz], self.rz.at[kz - 1], self.zsem.at[kz - 1], self.zr.at[kz - 1], self.zs[kz - 1])

    def start(self, which):
        for a in which:
            for kz in (1, 2, 3, 0):
                self.core(4 * a + kz).start()
                self.load(4 * a + kz).start()

    def both(self, m):
        self.load(m).wait()
        self.core(m).wait_recv()
        return self.mine[m].astype(F32) + self.rc[m].astype(F32)

    def away(self, kzs):
        for kz in kzs:
            self.mine[12 + kz] = self.both(12 + kz).astype(BF)
            self.to_via(kz).start()

    def near(self, kzs):
        for kz in kzs:
            plain, joined = 2 - kz % 2, 1 + kz % 2
            self.mine[4 * plain + kz] = self.both(4 * plain + kz).astype(BF)
            self.to_next(plain, kz).start()
            v = self.both(4 * joined + kz)
            self.to_via(kz).wait_recv()
            self.mine[4 * joined + kz] = (v + self.rd[kz].astype(F32)).astype(BF)
            self.to_next(joined, kz).start()

    def line(self, kzs):
        for kz in kzs:
            v = self.both(kz)
            for a in (1, 2):
                self.to_next(a, kz).wait_recv()
                v = v + self.rn[a - 1, kz].astype(F32)
            if kz:
                self.mine[kz] = v.astype(BF)
                self.zz(kz).start()
            else:
                self.put(v)

    def stop(self, out):
        for kz in range(NZ):
            v = self.both(kz)
            for a in (1, 2):
                self.to_next(a, kz).wait_recv()
                v = v + self.rn[a - 1, kz].astype(F32)
            out[kz] = v.astype(BF)
        for m in range(16):
            self.core(m).wait_send()
        for kz in range(NZ):
            self.to_via(kz).wait_send()
            for a in (1, 2):
                self.to_next(a, kz).wait_send()

    def put(self, v):
        at = 0
        for o in self.outs:
            w = o.shape[1]
            o[...] = v[:, at:at + w]
            at += w

    def end(self):
        at = 0
        for kz in (1, 2, 3):
            self.zz(kz).wait_recv()
        for o in self.outs:
            w = o.shape[1]
            v = o[...]
            for kz in (1, 2, 3):
                v = v + self.rz[kz - 1, :, at:at + w].astype(F32)
            o[...] = v
            at += w
        for m in range(16):
            self.core(m).wait_send()
        for kz in range(4):
            self.to_via(kz).wait_send()
            for a in (1, 2):
                self.to_next(a, kz).wait_send()
        for kz in (1, 2, 3):
            self.zz(kz).wait_send()


class LineScatter:
    def __init__(self, part, out, mine, rz, lsem, ss, rs):
        self.part, self.out, self.mine, self.rz, self.lsem, self.ss, self.rs = part, out, mine, rz, lsem, ss, rs
        s, z, c = place()
        self.zs = partners(s, z, c)[0]

    @staticmethod
    def bufs(rows, cols):
        return [pltpu.VMEM((rows, cols), BF), pltpu.VMEM((3, rows, cols), BF), DMA(()), DMA((3,)), DMA((3,))]

    def copy(self, k):
        return remote(self.part.at[k + 1], self.rz.at[k], self.ss.at[k], self.rs.at[k], self.zs[k])

    def local(self):
        return pltpu.make_async_copy(self.part.at[0], self.mine, self.lsem)

    def start(self):
        for k in range(3):
            self.copy(k).start()
        self.local().start()

    def end(self):
        self.local().wait()
        v = self.mine[...].astype(F32)
        for k in range(3):
            self.copy(k).wait_recv()
            v = v + self.rz[k].astype(F32)
        self.out[...] = v
        for k in range(3):
            self.copy(k).wait_send()


def weights_in_kernel(w_ref, wm_ref, x_ref, base_ref, out_ref, zm_ref, xo_ref, bias_h, ga, gb, gc, la, lb, lc, xa, xb, xc, ya, yb, yc, tile, tsem):
    gat = Gather(w_ref, out_ref, ga, gb, gc)
    lin = LineGather(wm_ref, zm_ref, la, lb, lc)
    exc = Exchange(x_ref, xo_ref, xa, xb, xc, (0, 2))
    rest = Exchange(x_ref, xo_ref, ya, yb, yc, (1, 2))
    meet_all()
    gat.start()
    exc.start()

    def flush(h):
        return pltpu.make_async_copy(tile.at[h % 2], bias_h.at[h], tsem.at[h % 2])

    def head(h, carry):
        @pl.when(h >= 2)
        def _():
            flush(h - 2).wait()

        bias_tiles(base_ref, h, tile.at[h % 2])
        flush(h).start()
        return carry

    lax.fori_loop(0, H, head, 0)
    gat.line(1)
    gat.hop(0)
    gat.line(2)
    gat.line(3)
    lin.start()
    gat.diag(0)
    for kz in range(1, NZ):
        gat.hop(kz)
    rest.start()
    for kz in range(1, NZ):
        gat.diag(kz)
    flush(H - 2).wait()
    flush(H - 1).wait()
    gat.end()
    exc.end()
    rest.end()
    lin.end()


def weights_in(w, wm, x, base, cid):
    return pl.pallas_call(
        weights_in_kernel, in_specs=[ANY, ANY, ANY, VM], out_specs=[ANY] * 4,
        out_shape=[sds((ND,) + w.shape, w.dtype), sds((NZ,) + wm.shape, w.dtype), sds(x.shape, x.dtype), sds((H, NBK, BLK, BLK), F32)],
        scratch_shapes=Gather.sems() + LineGather.sems() + Exchange.sems() * 2 + [pltpu.VMEM((2, NBK, BLK, BLK), F32), DMA((2,))],
        compiler_params=params(24, cid), name="weights_in")(w, wm, x, base)


def grads_out_kernel(n, *refs):
    gs, small, gt = refs[:n], refs[n], refs[n + 1]
    outs, osmall, go = refs[n + 2:2 * n + 2], refs[2 * n + 2], refs[2 * n + 3]
    refs = refs[2 * n + 4:]
    nb = len(Scatter.bufs(8, D))
    mc, mx, mz, ms, mr, e1, e2, e3 = refs[:8]
    sca = [Scatter(gs[j], pl.ds(0, D), [outs[j]], *refs[8 + j * nb:8 + (j + 1) * nb]) for j in range(n)]
    s, z, c = place()
    zs, ss, co = partners(s, z, c)
    exc = Exchange(gt, go, e1, e2, e3)
    meet_all()
    first = remote(small, mc, ms.at[0], mr.at[0], co)
    first.start()
    for a in sca:
        a.start((3,))
    for a in sca:
        a.start((2, 1, 0))
    first.wait_recv()
    mx[s] = small[...] + mc[...]
    xy = [remote(mx.at[s], mx.at[s], ms.at[k], mr.at[k], ss[k - 1]) for k in (1, 2, 3)]
    for cp in xy:
        cp.start()
    every = (1, 2, 3, 0)
    for a in sca:
        a.away(every)
    for cp in xy:
        cp.wait_recv()
    mz[z] = (mx[0] + mx[1]) + (mx[2] + mx[3])
    zz = [remote(mz.at[z], mz.at[z], ms.at[3 + k], mr.at[3 + k], zs[k - 1]) for k in (1, 2, 3)]
    for cp in zz:
        cp.start()
    for a in sca:
        a.near(every)
    exc.start()
    for a in sca:
        a.line(every)
    for cp in zz:
        cp.wait_recv()
    osmall[...] = (mz[0] + mz[1]) + (mz[2] + mz[3])
    for a in sca:
        a.end()
    exc.end()
    for cp in [first] + xy + zz:
        cp.wait_send()


def grads_out(gs, small, gt, cid):
    sm = pltpu.VMEM(small.shape, F32)
    sm4 = pltpu.VMEM((4,) + small.shape, F32)
    return pl.pallas_call(
        functools.partial(grads_out_kernel, len(gs)),
        in_specs=[ANY] * len(gs) + [VM, ANY], out_specs=[VM] * (len(gs) + 1) + [ANY],
        out_shape=[sds(g.shape[1:], F32) for g in gs] + [sds(small.shape, F32), sds(gt.shape, BF)],
        scratch_shapes=[sm, sm4, sm4, DMA((7,)), DMA((7,))] + Exchange.sems() + sum([Scatter.bufs(*g.shape[1:]) for g in gs], []),
        compiler_params=params(56, cid), name="grads_out")(*gs, small, gt)


EPS = 1e-6
GATE = 0.7978845608028654


def cst(shape):
    return pl.BlockSpec(shape, lambda *a: (0,) * len(shape), pipeline_mode=pl.Buffered(1))


def col(shape, j):
    return pl.BlockSpec(shape, lambda *a: (0, j), pipeline_mode=pl.Buffered(1))


def rows8(v):
    return jnp.sum(v.reshape(v.shape[0] // 8, 8, v.shape[1]), 0)


def norm(x, g):
    return x * lax.rsqrt(jnp.mean(x * x, -1, keepdims=True) + EPS) * g


def norm_grad(x, g, dn):
    r = lax.rsqrt(jnp.mean(x * x, -1, keepdims=True) + EPS)
    gd = g * dn
    dx = r * gd - x * (r * r * r) * jnp.mean(gd * x, -1, keepdims=True)
    return dx, rows8(dn * x * r)


def gelu_pair(x):
    x2 = x * x
    t = jnp.tanh(x * (GATE + GATE * 0.044715 * x2))
    hp = 0.5 + 0.5 * t
    y = x * hp
    d = hp + 0.5 * x * (1.0 - t * t) * (GATE + 3 * GATE * 0.044715 * x2)
    return y, d


def blocks(n=NBK):
    return [slice(i * BLK, (i + 1) * BLK) for i in range(n)]


HOPS = [("hop", k) for k in range(NZ)]
FWD_PLAN = ((2, [("exc", 0)]), (5, HOPS + [("exc", 1)]))
CROSS_PLAN = ((4, HOPS),)


def self_fwd_kernel(near, st_ref, x_ref, w_ref, gn_ref, bias_ref, mpre_ref, mpost_ref, *refs):
    if near:
        (zm_h, wf_h, enc_h, cot_h, q_ref, k_ref, v_ref, att_ref, gain_ref, p_ref, wo_h, zf_h, eo_h, co_h, acc_ref, lo_ref,
         ags, lgs, ex1, ex2) = split(refs, 16, 3, 3, 3, 3)
        gat = PlaneGather(zm_h, wo_h, *ags)
        lin = LineGather(wf_h, zf_h, *lgs)
        exc = [Exchange(enc_h, eo_h, *ex1), Exchange(cot_h, co_h, *ex2)]
    else:
        q_ref, k_ref, v_ref, att_ref, gain_ref, p_ref, acc_ref, lo_ref = refs
    h = pl.program_id(0)

    if near:
        @pl.when(h == 0)
        def _():
            meet_all()
            gat.start()
            lin.start()

        for hh, todo in FWD_PLAN:
            @pl.when(h == hh)
            def _(todo=todo):
                for name, k in todo:
                    if name == "exc":
                        exc[k].start()
                    else:
                        getattr(gat, name)(k)

    @pl.when(h == 0)
    def _():
        acc_ref[...] = jnp.zeros_like(acc_ref)
        gt = gn_ref[...].astype(F32).T
        gain_ref[...] = gt[:8]
        g = gt[:1]
        for r in blocks():
            n1 = norm(x_ref[r, :].astype(F32), g).astype(BF)
            for j, o in enumerate((q_ref, k_ref, v_ref)):
                o[r, :] = dot(n1, w_ref[:, j * D:(j + 1) * D], 1, 0).astype(BF)
        pos = lax.broadcasted_iota(jnp.int32, (L, 128), 0)
        lo = jnp.zeros((L, 128), jnp.int32)
        for d in range(1, st_ref.shape[0]):
            sd = st_ref[d]
            lo = jnp.where(pos >= sd, sd, lo)
        lo_ref[...] = lo

    mp = mpre_ref[pl.ds(h, 1), :]
    mo = mpost_ref[pl.ds(h, 1), :]

    def scores(i):
        n = (i + 1) * BLK
        qm = (q_ref[i * BLK:n, :].astype(F32) * mp).astype(BF)
        return dot(qm, k_ref[:n, :], 1, 1)

    sc = scores(NBK - 1)
    for i in reversed(range(NBK)):
        nxt = scores(i - 1) if i else None
        n = (i + 1) * BLK
        r = slice(i * BLK, n)
        bias = jnp.concatenate([bias_ref[0, i - j] for j in range(i + 1)], 1) if i else bias_ref[0, 0]
        c = lax.broadcasted_iota(jnp.int32, (BLK, n), 1)
        sc = jnp.where(c >= lo_ref[r, :1], sc + bias, NEG)
        e = jnp.exp(sc - jnp.max(sc, 1, keepdims=True))
        p = (e * (1.0 / jnp.sum(e, 1, keepdims=True))).astype(BF)
        p_ref[0, r, :n] = p
        acc_ref[r, :] += dot(p, v_ref[:n, :], 1, 0) * mo
        sc = nxt

    @pl.when(h == H - 1)
    def _():
        att_ref[...] = acc_ref[...].astype(BF)
        if near:
            lin.end()
            for k in range(NZ):
                gat.diag(k)
            gat.end()
            for e in exc:
                e.end()


def self_fwd(starts, x, w1, bias, mpre, mpost, far=None, cid=None):
    one = cst((L, D))
    near = far is not None
    extra_out = []
    if near:
        extra_out = [sds((ND,) + far[0].shape[1:], BF), sds((NZ,) + far[1].shape, BF)] + [sds(f.shape, BF) for f in far[2:]]
    return pl.pallas_call(
        functools.partial(self_fwd_kernel, near),
        grid_spec=pltpu.PrefetchScalarGridSpec(
            num_scalar_prefetch=1, grid=(H,),
            in_specs=[one, col((D, 3 * D), 0), col((D, 128), 18),
                      pl.BlockSpec((1, NBK, BLK, BLK), lambda h, st: (h, 0, 0, 0)), cst((H, D)), cst((H, D))]
            + [ANY] * (4 * near),
            out_specs=[one] * 4 + [cst((8, D)), pl.BlockSpec((1, L, L), lambda h, st: (h, 0, 0))] + [ANY] * (4 * near),
            scratch_shapes=[pltpu.VMEM((L, D), F32), pltpu.VMEM((L, 128), jnp.int32)]
            + (PlaneGather.sems() + LineGather.sems() + Exchange.sems() * 2 if near else [])),
        out_shape=[sds((L, D), BF)] * 4 + [sds((8, D), F32), sds((H, L, L), BF)] + extra_out,
        compiler_params=params(62, cid),
        cost_estimate=pl.CostEstimate(flops=52_000_000_000, bytes_accessed=45_000_000, transcendentals=8_000_000),
        name="self_fwd")(starts, x, w1, w1, bias, mpre, mpost, *(far or ()))


def cross_fwd_kernel(near, x_ref, att_ref, wo_ref, wq_ref, wk_ref, wv_ref, enc_ref, gain_ref, *refs):
    if near:
        zf_h, h1_ref, n2_ref, q_ref, k_ref, v_ref, catt_ref, p_ref, fo_h, ags = split(refs, 9, 3)
        gat = PlaneGather(zf_h, fo_h, *ags)
    else:
        h1_ref, n2_ref, q_ref, k_ref, v_ref, catt_ref, p_ref = refs
    h = pl.program_id(0)

    if near:
        @pl.when(h == 0)
        def _():
            meet_all()
            gat.start()

        for hh, todo in CROSS_PLAN:
            @pl.when(h == hh)
            def _(todo=todo):
                for name, k in todo:
                    getattr(gat, name)(k)

    @pl.when(h == 0)
    def _():
        g = gain_ref[1:2, :]
        for r in blocks():
            h1 = x_ref[r, :].astype(F32) + dot(att_ref[r, :], wo_ref[...], 1, 0)
            h1_ref[r, :] = h1
            n2 = norm(h1, g).astype(BF)
            n2_ref[r, :] = n2
            q_ref[r, :] = dot(n2, wq_ref[...], 1, 0).astype(BF)
            k_ref[r, :] = dot(enc_ref[r, :], wk_ref[...], 1, 0).astype(BF)
            v_ref[r, :] = dot(enc_ref[r, :], wv_ref[...], 1, 0).astype(BF)

    cols = pl.ds(pl.multiple_of(h * 128, 128), 128)
    first = lax.broadcasted_iota(jnp.int32, (1, 128), 1) < DH
    k = k_ref[:, cols]
    v = v_ref[:, cols]
    steps = [(r, e) for r in blocks() for e in range(2)]

    def scores(r, e):
        q = q_ref[r, cols]
        return dot(jnp.where(first if e == 0 else ~first, q, jnp.zeros_like(q)), k, 1, 1)

    sc = scores(*steps[0])
    keep = None
    for n, (r, e) in enumerate(steps):
        nxt = scores(*steps[n + 1]) if n + 1 < len(steps) else None
        ex = jnp.exp(sc - jnp.max(sc, 1, keepdims=True))
        p = (ex * (1.0 / jnp.sum(ex, 1, keepdims=True))).astype(BF)
        p_ref[e, r, :] = p
        o = dot(p, v, 1, 0)
        if e == 0:
            keep = o
        else:
            catt_ref[r, cols] = jnp.where(first, keep, o).astype(BF)
        sc = nxt

    if near:
        @pl.when(h == H // 2 - 1)
        def _():
            for k in range(NZ):
                gat.diag(k)
            gat.end()


def cross_fwd(x, att, wmid, enc, gains, far=None, cid=None):
    one = cst((L, D))
    near = far is not None
    return pl.pallas_call(
        functools.partial(cross_fwd_kernel, near), grid=(H // 2,),
        in_specs=[one, one] + [col((D, D), j) for j in range(4)] + [one, cst((8, D))] + [ANY] * near,
        out_specs=[one] * 6 + [pl.BlockSpec((2, L, L), lambda h: (h, 0, 0))] + [ANY] * near,
        out_shape=[sds((L, D), F32)] + [sds((L, D), BF)] * 5 + [sds((H, L, L), BF)]
        + ([sds((ND,) + far.shape[1:], BF)] if near else []),
        scratch_shapes=PlaneGather.sems() if near else [],
        compiler_params=params(62, cid),
        cost_estimate=pl.CostEstimate(flops=31_000_000_000, bytes_accessed=50_000_000, transcendentals=12_000_000),
        name="cross_fwd")(x, att, wmid, wmid, wmid, wmid, enc, gains, *([far] if near else []))


def feed_kernel(h1_ref, catt_ref, wco_ref, cot_ref, gain_ref, fi_ref, fo_ref,
                out_ref, bh2_ref, bca_ref, gw_ref, dg_ref,
                n3, n3t, cott, acc, dn, inner, bi):
    a = pl.program_id(0)
    g = gain_ref[2:3, :]

    @pl.when(a == 0)
    def _():
        for r in blocks():
            h2 = h1_ref[r, :] + dot(catt_ref[r, :], wco_ref[...], 1, 0)
            bh2_ref[r, :] = h2
            acc[r, :] = h2
            n3[r, :] = norm(h2, g).astype(BF)
        n3t[...] = n3[...].T
        cott[...] = cot_ref[...].T
        dn[...] = jnp.zeros_like(dn)

    for r in blocks():
        u = dot(n3[r, :], fi_ref[...], 1, 0)
        y, d = gelu_pair(u)
        y = y.astype(BF)
        inner[r, :] = y
        gy = dot(cot_ref[r, :], fo_ref[...], 1, 1)
        b = (gy * d).astype(BF)
        bi[r, :] = b
        acc[r, :] += dot(y, fo_ref[...], 1, 0)
        dn[r, :] += dot(b, fi_ref[...], 1, 1)
    gw_ref[:, :D] = dot(n3t[...], bi[...], 1, 0).astype(BF)
    gw_ref[:, D:] = dot(cott[...], inner[...], 1, 0).T.astype(BF)

    @pl.when(a == pl.num_programs(0) - 1)
    def _():
        dg = jnp.zeros((8, D), F32)
        for r in blocks():
            out_ref[r, :] = acc[r, :].astype(BF)
            dx, s = norm_grad(bh2_ref[r, :], g, dn[r, :])
            dg = dg + s
            b2 = cot_ref[r, :].astype(F32) + dx
            bh2_ref[r, :] = b2
            bca_ref[r, :] = dot(b2.astype(BF), wco_ref[...], 1, 1).astype(BF)
        dg_ref[...] = dg


def feed(h1, catt, wmid, cot, gains, wfeed):
    one = cst((L, D))
    nf = wfeed.shape[1] // (2 * D)
    return pl.pallas_call(
        feed_kernel, grid=(nf,),
        in_specs=[one, one, col((D, D), 4), one, cst((8, D)),
                  pl.BlockSpec((D, D), lambda a: (0, 2 * a)), pl.BlockSpec((D, D), lambda a: (0, 2 * a + 1))],
        out_specs=[one, one, one, pl.BlockSpec((D, 2 * D), lambda a: (0, a)), cst((8, D))],
        out_shape=[sds((L, D), BF), sds((L, D), F32), sds((L, D), BF), sds((D, wfeed.shape[1]), BF), sds((8, D), F32)],
        scratch_shapes=[pltpu.VMEM((L, D), BF), pltpu.VMEM((D, L), BF), pltpu.VMEM((D, L), BF), pltpu.VMEM((L, D), F32),
                        pltpu.VMEM((L, D), F32), pltpu.VMEM((L, D), BF), pltpu.VMEM((L, D), BF)],
        compiler_params=pltpu.CompilerParams(vmem_limit_bytes=62 << 20),
        cost_estimate=pl.CostEstimate(flops=32_000_000_000, bytes_accessed=50_000_000, transcendentals=3_000_000),
        name="feed")(h1, catt, wmid, cot, gains, wfeed, wfeed)


def cross_bwd_kernel(near, q_ref, k_ref, v_ref, do_ref, p_ref, gain_ref, n2_h, enc_h, att_h, catt_h, h1_h, bh2_h, w_h, *refs):
    if near:
        gf_h = refs[0]
        gw_ref, genc_ref, bh1_ref, bat_ref, dg_ref, rf_ref = refs[1:7]
        qt, dot_, ds, dq, dk, dv, n2, enc, att, catt, h1, w, sems, sca = split(refs[7:], 13, len(Scatter.bufs(8, D)))
        sca = Scatter(gf_h, pl.ds(0, gf_h.shape[2]), [], *sca)
    else:
        gw_ref, genc_ref, bh1_ref, bat_ref, dg_ref = refs[:5]
        qt, dot_, ds, dq, dk, dv, n2, enc, att, catt, h1, w, sems = refs[5:]
    h = pl.program_id(0)
    late = [(n2_h, n2), (enc_h, enc), (att_h, att), (catt_h, catt), (h1_h, h1), (bh2_h, bh1_ref)]
    late += [(w_h.at[:, pl.ds(0, 4 * D)], w)]
    copies = [pltpu.make_async_copy(a, b, sems.at[i]) for i, (a, b) in enumerate(late)]

    @pl.when(h == 0)
    def _():
        if near:
            meet_all()
            sca.start((3,))

    @pl.when(h == 3)
    def _():
        for c in copies:
            c.start()

    if near:
        for hh, name, kzs in BWD_PLAN:
            @pl.when(h == hh)
            def _(name=name, kzs=kzs):
                getattr(sca, name)(kzs)

    e = h % 2
    cols = pl.ds(pl.multiple_of((h // 2) * 128, 128), 128)
    fe = (lax.broadcasted_iota(jnp.int32, (1, 128), 1) // DH) == e
    k = k_ref[...]
    v = v_ref[...]

    @pl.when(e == 0)
    def _():
        qt[...] = q_ref[...].T
        dot_[...] = do_ref[...].T

    for r in blocks():
        do = do_ref[r, :]
        dp = dot(jnp.where(fe, do, jnp.zeros_like(do)), v, 1, 1)
        p = p_ref[0, r, :].astype(F32)
        d = (p * (dp - jnp.sum(dp * p, 1, keepdims=True))).astype(BF)
        ds[r, :] = d
        dq[r, cols] = jnp.where(fe, dot(d, k, 1, 0).astype(BF), dq[r, cols])
    x = dot(dot_[...], p_ref[0], 1, 0).T.astype(BF)
    dv[:, cols] = jnp.where(fe, x, dv[:, cols])
    x = dot(qt[...], ds[...], 1, 0).T.astype(BF)
    dk[:, cols] = jnp.where(fe, x, dk[:, cols])

    @pl.when(h == H - 1)
    def _():
        for c in copies:
            c.wait()
        g = gain_ref[1:2, :]
        dg = jnp.zeros((8, D), F32)
        gw_ref[:, D:2 * D] = dot(n2[...], dq[...], 0, 0).astype(BF)
        gw_ref[:, 2 * D:3 * D] = dot(enc[...], dk[...], 0, 0).astype(BF)
        gw_ref[:, 3 * D:4 * D] = dot(enc[...], dv[...], 0, 0).astype(BF)
        for r in blocks():
            genc_ref[r, :] = (dot(dk[r, :], w[:, 2 * D:3 * D], 1, 1) + dot(dv[r, :], w[:, 3 * D:], 1, 1)).astype(genc_ref.dtype)
            dx, s = norm_grad(h1[r, :], g, dot(dq[r, :], w[:, D:2 * D], 1, 1))
            dg = dg + s
            b2 = bh1_ref[r, :]
            b1 = b2 + dx
            bh1_ref[r, :] = b1
            b1 = b1.astype(BF)
            n2[r, :] = b1
            enc[r, :] = b2.astype(BF)
            bat_ref[r, :] = dot(b1, w[:, :D], 1, 1).astype(BF)
        gw_ref[:, :D] = dot(att[...], n2[...], 0, 0).astype(BF)
        gw_ref[:, 4 * D:] = dot(catt[...], enc[...], 0, 0).astype(BF)
        dg_ref[...] = dg
        if near:
            sca.stop(rf_ref)


EVERY = (1, 2, 3, 0)
BWD_PLAN = ((1, "away", EVERY), (1, "start", (2, 1)), (3, "start", (0,)), (6, "near", EVERY))


def cross_bwd(q, k, v, do, p, gains, n2, enc, att, catt, h1, bh2, wmid, far=None, cid=None):
    one = cst((L, D))
    near = far is not None
    pair = pl.BlockSpec((L, 128), lambda h: (0, h // 2))
    act = pltpu.VMEM((L, D), BF)
    more = [(NZ,) + far.shape[1:]] if near else []
    return pl.pallas_call(
        functools.partial(cross_bwd_kernel, near), grid=(H,),
        in_specs=[pair] * 4 + [pl.BlockSpec((1, L, L), lambda h: (h, 0, 0)), cst((8, D))] + [ANY] * (7 + near),
        out_specs=[cst((D, 5 * D)), one, one, one, cst((8, D))] + [cst(s) for s in more],
        out_shape=[sds((D, 5 * D), BF), sds((L, D), BF), sds((L, D), F32), sds((L, D), BF), sds((8, D), F32)]
        + [sds(s, BF) for s in more],
        scratch_shapes=[pltpu.VMEM((128, L), BF)] * 2 + [pltpu.VMEM((L, L), BF)] + [act] * 7
        + [pltpu.VMEM((L, D), F32), pltpu.VMEM((D, 4 * D), BF), DMA((7,))] + sum([Scatter.bufs(*s[1:]) for s in more], []),
        compiler_params=params(62, cid),
        cost_estimate=pl.CostEstimate(flops=37_000_000_000, bytes_accessed=70_000_000, transcendentals=0),
        name="cross_bwd")(q, k, v, do, p, gains, n2, enc, att, catt, h1, bh2, wmid, *([far] if near else []))


SELF_PLAN = ((1, "away", EVERY), (1, "start", (2, 1, 0)), (3, "near", EVERY), (3, "exc", 0), (6, "exc", 1), (8, "line", EVERY))


def self_bwd_kernel(near, q_ref, k_ref, v_ref, ba_ref, p_ref, mpre_ref, mpost_ref, gain_ref, x_h, bh1_h, w_h, *refs):
    if near:
        gm_h, zf_h, out_h, ge_h = refs[:4]
        gq_ref, gk_ref, gv_ref, gtok_ref, gpre_ref, gpost_ref, diag_ref, dg_ref = refs[4:12]
        rms, (rf_ref, oo_h, go_h) = refs[12:17], refs[17:20]
        qt, bat, dqa, dkt, dvt, dm, x, bh1, w, sems, sca, lin, ex1, ex2 = split(refs[20:], 10, len(Scatter.bufs(8, D)), 5, 3, 3)
        lin = LineScatter(zf_h, rf_ref, *lin)
        sca = Scatter(gm_h, pl.ds(0, gm_h.shape[2]), rms, *sca)
        exc = [Exchange(out_h, oo_h, *ex1), Exchange(ge_h, go_h, *ex2)]
    else:
        gq_ref, gk_ref, gv_ref, gtok_ref, gpre_ref, gpost_ref, diag_ref, dg_ref = refs[:8]
        qt, bat, dqa, dkt, dvt, dm, x, bh1, w, sems = refs[8:]
    h = pl.program_id(0)

    if near:
        @pl.when(h == 0)
        def _():
            meet_all()
            sca.start((3,))
            lin.start()

        for hh, name, kzs in SELF_PLAN:
            @pl.when(h == hh)
            def _(name=name, kzs=kzs):
                if name == "exc":
                    exc[kzs].start()
                else:
                    getattr(sca, name)(kzs)

    late = [(x_h, x), (bh1_h, bh1), (w_h.at[:, pl.ds(0, 3 * D)], w)]
    copies = [pltpu.make_async_copy(a, b, sems.at[i]) for i, (a, b) in enumerate(late)]

    @pl.when(h == 0)
    def _():
        for c in copies:
            c.start()
        qt[...] = q_ref[...].T
        bat[...] = ba_ref[...].T
        dqa[...] = jnp.zeros_like(dqa)
        dkt[...] = jnp.zeros_like(dkt)
        dvt[...] = jnp.zeros_like(dvt)

    mp = mpre_ref[pl.ds(h, 1), :]
    mo = mpost_ref[pl.ds(h, 1), :]
    gp = jnp.zeros((8, D), F32)
    dacc = [None] * NBK
    for i, r in enumerate(blocks()):
        n = (i + 1) * BLK
        bam = (ba_ref[r, :].astype(F32) * mo).astype(BF)
        dp = dot(bam, v_ref[:n, :], 1, 1)
        p = p_ref[0, r, :n].astype(F32)
        d = p * (dp - jnp.sum(dp * p, 1, keepdims=True))
        for j in range(i + 1):
            t = d[:, j * BLK:(j + 1) * BLK]
            dacc[i - j] = t if dacc[i - j] is None else dacc[i - j] + t
        db = d.astype(BF)
        dm[r, :n] = db
        rr = dot(db, k_ref[:n, :], 1, 0)
        dqa[r, :] += rr * mp
        gp = gp + rows8(rr * q_ref[r, :].astype(F32))
    gpre_ref[pl.ds(h, 1), :] = jnp.sum(gp, 0, keepdims=True)
    for t in range(NBK):
        y = jnp.concatenate([jnp.zeros((BLK, BLK), F32), dacc[t]], 1)
        n = BLK // 2
        while n >= 1:
            y = y[:n] + pltpu.roll(y[n:], 2 * BLK - n, 1)
            n //= 2
        diag_ref[0, t] = y
    mpc = jnp.broadcast_to(mp, (8, D)).T[:, :1]
    moc = jnp.broadcast_to(mo, (8, D)).T[:, :1]
    gq = jnp.zeros((8, D), F32)
    for c in blocks():
        i0 = c.start
        t = dot(bat[:, i0:], p_ref[0, i0:, c], 1, 0)
        dvt[:, c] += t * moc
        gq = gq + rows8(t.T * v_ref[c, :].astype(F32))
        u = dot(qt[:, i0:], dm[i0:, c], 1, 0)
        dkt[:, c] += u * mpc
    gpost_ref[pl.ds(h, 1), :] = jnp.sum(gq, 0, keepdims=True)

    @pl.when(h == H - 1)
    def _():
        for c in copies:
            c.wait()
        g = gain_ref[:1, :]
        dg = jnp.zeros((8, D), F32)
        for r in blocks():
            xr = x[r, :].astype(F32)
            n1 = norm(xr, g).astype(BF)
            dk = dkt[:, r].T.astype(BF)
            dv = dvt[:, r].T.astype(BF)
            dq = dqa[r, :].astype(BF)
            bat[:, r] = n1.T
            dm[r, :D] = dq
            dqa[r, :] = dk.astype(F32)
            back = dot(dq, w[:, :D], 1, 1) + dot(dk, w[:, D:2 * D], 1, 1) + dot(dv, w[:, 2 * D:], 1, 1)
            dx, s = norm_grad(xr, g, back)
            dg = dg + s
            gtok_ref[r, :] = (bh1[r, :] + dx).astype(gtok_ref.dtype)
        gq_ref[...] = dot(bat[...], dm[:, :D], 1, 0).astype(BF)
        gk_ref[...] = dot(bat[...], dqa[...].astype(BF), 1, 0).astype(BF)
        gv_ref[...] = dot(bat[...], dvt[...].astype(BF), 1, 1).astype(BF)
        dg_ref[...] = dg
        if near:
            lin.end()
            sca.end()
            for e in exc:
                e.end()


def self_bwd(q, k, v, ba, p, mpre, mpost, gains, x, bh1, w1, far=None, cid=None):
    one = cst((L, D))
    near = far is not None
    rows = far[0].shape[1] if near else 0
    more = [cst((rows, D))] * 5 + [cst(far[1].shape[1:]), ANY, ANY] if near else []
    more_out = []
    if near:
        more_out = [sds((rows, D), F32)] * 5 + [sds(far[1].shape[1:], F32)] + [sds(f.shape, BF) for f in far[2:]]
    return pl.pallas_call(
        functools.partial(self_bwd_kernel, near), grid=(H,),
        in_specs=[one] * 4 + [pl.BlockSpec((1, L, L), lambda h: (h, 0, 0)), cst((H, D)), cst((H, D)), cst((8, D))] + [ANY] * (3 + 4 * near),
        out_specs=[cst((D, D))] * 3 + [one, cst((H, D)), cst((H, D)),
                   pl.BlockSpec((1, NBK, 1, 2 * BLK), lambda h: (h, 0, 0, 0)), cst((8, D))] + more,
        out_shape=[sds((D, D), BF)] * 3 + [sds((L, D), BF), sds((H, D), F32), sds((H, D), F32),
                   sds((H, NBK, 1, 2 * BLK), F32), sds((8, D), F32)] + more_out,
        scratch_shapes=[pltpu.VMEM((D, L), BF)] * 2 + [pltpu.VMEM((L, D), F32)] + [pltpu.VMEM((D, L), F32)] * 2
        + [pltpu.VMEM((L, L), BF), pltpu.VMEM((L, D), BF), pltpu.VMEM((L, D), F32), pltpu.VMEM((D, 3 * D), BF), DMA((3,))]
        + (Scatter.bufs(*far[0].shape[1:]) + LineScatter.bufs(*far[1].shape[1:]) + Exchange.sems() * 2 if near else []),
        compiler_params=params(62, cid),
        cost_estimate=pl.CostEstimate(flops=128_000_000_000, bytes_accessed=50_000_000, transcendentals=0),
        name="self_bwd")(q, k, v, ba, p, mpre, mpost, gains, x, bh1, w1, *(far or ()))


AX = ("seq", "dp")


def gather(w):
    return lax.all_gather(w, AX, axis=0, tiled=True)


def scatter(g):
    return lax.psum_scatter(g, AX, scatter_dimension=0, tiled=True).astype(F32)


def per_device(tokens, encoded, cotangent, doc_starts, rel_bucket, sq, sk, sv, so, cq, ck, cv, co, fi, fo,
               gs, gc, gf, mix_pre, mix_post, rel_table):
    nseq, ndp = lax.axis_size("seq"), lax.axis_size("dp")
    rows = sq.shape[0]
    nf = fo.shape[0] // rows
    ndev = nseq * ndp
    buckets = rel_table.shape[0]
    near = nseq == NS and ndp == NZ * NCORE and rows % 8 == 0
    to_stream = lambda x: lax.all_to_all(x, "seq", 0, 1, tiled=True).reshape(L, D)
    from_stream = lambda x: lax.all_to_all(x.reshape(1, L, D), "seq", 1, 0, tiled=True)
    hot = (rel_bucket[:, None] == jnp.arange(buckets)[None, :]).astype(F32)
    trow = lax.dot_general(rel_table, hot, (((0,), (1,)), ((), ())), precision=lax.Precision.HIGHEST)
    base = make_base(trow)
    gains = jnp.pad(jnp.stack([gs, gc, gf], 1), ((0, 0), (0, 125)))
    w1 = jnp.concatenate([sq, sk, sv, gains], 1)
    wmid = jnp.concatenate([so, cq, ck, cv, co], 1)
    wfeed = jnp.stack([fi.reshape(rows, D, nf).transpose(0, 2, 1), fo.reshape(rows, nf, D)], 2).reshape(rows, 2 * nf * D)
    if near:
        w1, zmid, x, bias = weights_in(w1, wmid, tokens, base, 1)
        w1 = w1.reshape(D, -1)
        x = x.reshape(L, D)
    else:
        w1 = gather(w1)
        x = to_stream(tokens)
        bias = toeplitz(base)
        wmid = gather(wmid)
        wfeed = gather(wfeed)
        enc = to_stream(encoded)
        cot = to_stream(cotangent)
    starts = lax.dynamic_index_in_dim(doc_starts, lax.axis_index("seq"), 0, keepdims=False)
    mpre = jnp.repeat(mix_pre.T, DH, axis=1)
    mpost = jnp.repeat(mix_post, DH, axis=1)
    if near:
        q, k, v, att, gain, p, wmid, zfeed, enc, cot = self_fwd(starts, x, w1, bias, mpre, mpost, (zmid, wfeed, encoded, cotangent), 2)
        wmid = wmid.reshape(D, -1)
        enc = enc.reshape(L, D)
        h1, n2, cqx, ckx, cvx, catt, cp, wfeed = cross_fwd(x, att, wmid, enc, gain, zfeed, 3)
        cot = cot.reshape(L, D)
        wfeed = wfeed.reshape(D, -1)
    else:
        q, k, v, att, gain, p = self_fwd(starts, x, w1, bias, mpre, mpost)
        h1, n2, cqx, ckx, cvx, catt, cp = cross_fwd(x, att, wmid, enc, gain)
    out, bh2, bca, gw_feed, dgf = feed(h1, catt, wmid, cot, gain, wfeed)
    back = (cqx, ckx, cvx, bca, cp, gain, n2, enc, att, catt, h1, bh2, wmid)
    if near:
        gw_mid, g_enc, bh1, bat, dgc, zfeed = cross_bwd(*back, gw_feed.reshape(ndev, rows, -1), 6)
    else:
        gw_mid, g_enc, bh1, bat, dgc = cross_bwd(*back)
        r_feed = scatter(gw_feed)
    blk = lambda a: a.reshape(nseq, L // nseq, D)
    if near:
        far = (gw_mid.reshape(ndev, rows, -1), zfeed, blk(out), blk(g_enc))
        gw_q, gw_k, gw_v, g_tok, gpre, gpost, diag, dgs, *r_mid, r_feed, out, g_enc = self_bwd(
            q, k, v, bat, p, mpre, mpost, gain, x, bh1, w1, far, 4)
    else:
        gw_q, gw_k, gw_v, g_tok, gpre, gpost, diag, dgs = self_bwd(q, k, v, bat, p, mpre, mpost, gain, x, bh1, w1)
    gpre = gpre.reshape(H, H, DH).sum(-1).T
    gpost = gpost.reshape(H, H, DH).sum(-1)
    dg = diag[:, :, 0, ::-1]
    gt = 0.0
    for d in range(NBK):
        gt = gt + jnp.pad(dg[:, d], ((0, 0), (d * BLK + 1, L - d * BLK - 1)))
    gt = gt[:, BLK:BLK + L]
    gtab = lax.dot_general(hot, gt, (((0,), (1,)), ((), ())), precision=lax.Precision.HIGHEST)
    dgain = jnp.stack([dgs.sum(0), dgc.sum(0), dgf.sum(0)])
    if near:
        parts = [dgain, gpre, gpost, gtab]
        vec = jnp.concatenate([a.reshape(-1) for a in parts])
        vec = jnp.pad(vec, (0, 3072 - vec.shape[0])).reshape(24, 128)
        r_q, r_k, r_v, vec, g_tok = grads_out([a.reshape(ndev, rows, -1) for a in (gw_q, gw_k, gw_v)], vec, blk(g_tok), 5)
        vec = vec.reshape(-1)
        o = 0
        got = []
        for a in parts:
            got.append(vec[o:o + a.size].reshape(a.shape))
            o += a.size
        dgain, gpre, gpost, gtab = got
    else:
        r_mid = jnp.split(scatter(gw_mid), 5, 1)
        r_q, r_k, r_v = scatter(gw_q), scatter(gw_k), scatter(gw_v)
        out, g_tok, g_enc = from_stream(out), from_stream(g_tok), from_stream(g_enc)
        dgain, gpre, gpost, gtab = lax.psum((dgain, gpre, gpost, gtab), AX)
    r_feed = r_feed.reshape(rows, nf, 2, D)
    me = lax.axis_index("seq") * ndp + lax.axis_index("dp")
    dgain = lax.dynamic_slice_in_dim(dgain, me * rows, rows, 1)
    return (out, g_tok.astype(F32), g_enc.astype(F32),
            r_q, r_k, r_v, *r_mid,
            r_feed[:, :, 0].transpose(0, 2, 1).reshape(rows, nf * D), r_feed[:, :, 1].reshape(rows * nf, D),
            dgain[0], dgain[1], dgain[2], gpre, gpost, gtab)


def solution(mesh):
    act = P("dp", "seq", None)
    w = P(AX, None)
    g = P(AX)
    return jax.shard_map(
        per_device, mesh=mesh, in_specs=(act, act, act, P("dp", None), P()) + (w,) * 10 + (g,) * 3 + (P(),) * 3,
        out_specs=(act,) * 3 + (w,) * 10 + (g,) * 3 + (P(),) * 3, check_vma=False)
```

```python
import functools

import jax
import jax.numpy as jnp
from jax import lax
from jax.experimental import pallas as pl
from jax.experimental.pallas import tpu as pltpu
from jax.sharding import PartitionSpec as P

F32 = jnp.float32
BF = jnp.bfloat16
NEG = -1e30
H, DH, D, L = 12, 64, 768, 1024
BLK = 256
NBK = L // BLK


def dot(a, b, ca, cb):
    return lax.dot_general(a, b, (((ca,), (cb,)), ((), ())), preferred_element_type=F32)


def bias_tiles(base_ref, h, out_ref):
    for d in range(NBK):
        row = jnp.broadcast_to(base_ref[h, d], (BLK, 2 * BLK))
        t = pltpu.roll(row, 0, 1, stride=1, stride_axis=0)[:, :BLK]
        if d == 0:
            a = lax.broadcasted_iota(jnp.int32, (BLK, BLK), 0)
            b = lax.broadcasted_iota(jnp.int32, (BLK, BLK), 1)
            t = jnp.where(a >= b, t, NEG)
        out_ref[d] = t


def toeplitz(base):
    def kernel(base_ref, out_ref):
        bias_tiles(base_ref, 0, out_ref.at[0])

    return pl.pallas_call(
        kernel, grid=(H,), in_specs=[pl.BlockSpec((1, NBK, 1, 2 * BLK), lambda h: (h, 0, 0, 0))],
        out_specs=pl.BlockSpec((1, NBK, BLK, BLK), lambda h: (h, 0, 0, 0)),
        out_shape=jax.ShapeDtypeStruct((H, NBK, BLK, BLK), F32), name="bias_tiles")(base)


def make_base(trow):
    rows = []
    for d in range(NBK):
        lo = d * BLK
        a = trow[:, max(lo - BLK + 1, 0):lo + 1][:, ::-1]
        if d == 0:
            a = jnp.concatenate([a, jnp.zeros((H, BLK - 1), F32)], 1)
        b = trow[:, lo + 1:lo + BLK][:, ::-1]
        rows.append(jnp.concatenate([a, jnp.zeros((H, 1), F32), b], 1))
    return jnp.stack(rows, 1)[:, :, None, :]


ANY = pl.BlockSpec(memory_space=pl.ANY)
VM = pl.BlockSpec(memory_space=pltpu.VMEM)
DMA = pltpu.SemaphoreType.DMA
MESH = pl.DeviceIdType.MESH
NS, NZ, NCORE = 4, 4, 2
ND = NS * NZ * NCORE


def sds(shape, dt):
    return jax.ShapeDtypeStruct(shape, dt)


def hbm(shape, dt):
    return pltpu.HBM(shape, dt)


def params(mib, cid):
    if cid is None:
        return pltpu.CompilerParams(vmem_limit_bytes=mib << 20)
    return pltpu.CompilerParams(vmem_limit_bytes=mib << 20, collective_id=cid, has_side_effects=True)


def split(refs, n, *groups):
    out = list(refs[:n])
    for g in groups:
        out.append(refs[n:n + g])
        n += g
    return out


def place():
    s = lax.axis_index("seq")
    d = lax.axis_index("dp")
    return s, d // NCORE, d % NCORE


def flat(s, z, c):
    return (s * NZ + z) * NCORE + c


def partners(s, z, c):
    zs = [{"seq": s, "dp": ((z + k) % NZ) * NCORE + c} for k in (1, 2, 3)]
    ss = [{"seq": (s + k) % NS, "dp": z * NCORE + c} for k in (1, 2, 3)]
    return zs, ss, {"seq": s, "dp": z * NCORE + 1 - c}


def plane(s):
    return s + 1 - 2 * (s % 2), (s + 2) % NS, NS - 1 - s


def meet(devices):
    bar = pltpu.get_barrier_semaphore()
    for p in devices:
        pl.semaphore_signal(bar, inc=1, device_id=p, device_id_type=MESH)
    pl.semaphore_wait(bar, len(devices))


def meet_all():
    zs, ss, co = partners(*place())
    meet(zs + ss + [co])


def meet_seq():
    meet(partners(*place())[1])


def remote(src, dst, ssem, rsem, dev):
    return pltpu.make_async_remote_copy(src, dst, ssem, rsem, device_id=dev, device_id_type=MESH)


class Exchange:
    def __init__(self, src, dst, ss, rs, ls, part=(0, 1)):
        self.s, z, c = place()
        self.src, self.dst, self.ss, self.rs, self.ls = src, dst, ss, rs, ls
        n = src.shape[1] // part[1]
        self.rows = pl.ds(part[0] * n, n)
        self.to = partners(self.s, z, c)[1]

    @staticmethod
    def sems():
        return [DMA((3,)), DMA((3,)), DMA(())]

    def local(self):
        return pltpu.make_async_copy(self.src.at[self.s, self.rows], self.dst.at[self.s, self.rows], self.ls)

    def copy(self, k):
        return remote(self.src.at[(self.s + k) % NS, self.rows], self.dst.at[self.s, self.rows], self.ss.at[k - 1], self.rs.at[k - 1], self.to[k - 1])

    def start(self):
        for k in (2, 1, 3):
            self.copy(k).start()
        self.local().start()

    def end(self):
        for k in (1, 2, 3):
            self.copy(k).wait_recv()
            self.copy(k).wait_send()
        self.local().wait()


class Gather:
    def __init__(self, w, out, ssem, rsem, lsem):
        self.w, self.out, self.ssem, self.rsem, self.lsem = w, out, ssem, rsem, lsem
        self.s, self.z, self.c = place()
        self.zs, self.ss, self.co = partners(self.s, self.z, self.c)
        self.px, self.py, self.pd = plane(self.s)

    @staticmethod
    def sems():
        return [DMA((ND - 1,)), DMA((ND,)), DMA(())]

    def slot(self, i):
        return self.out.at[i]

    def at(self, s, kz, c):
        return flat(s, (self.z + NZ - kz) % NZ, c)

    def there(self, s):
        return {"seq": s, "dp": self.z * NCORE + self.c}

    def send(self, i, dev, n, src=None):
        remote(self.slot(i) if src is None else src, self.slot(i), self.ssem.at[n], self.rsem.at[i], dev).start()

    def got(self, i):
        remote(self.slot(i), self.slot(i), self.ssem.at[0], self.rsem.at[i], self.co).wait_recv()

    def local(self):
        return pltpu.make_async_copy(self.w, self.slot(self.at(self.s, 0, self.c)), self.lsem)

    def start(self):
        own = self.at(self.s, 0, self.c)
        for k in range(3):
            self.send(own, self.zs[k], k, self.w)
        self.send(own, self.there(self.px), 3, self.w)
        self.send(own, self.there(self.py), 4, self.w)
        self.send(own, self.co, 5, self.w)
        self.local().start()

    def line(self, k):
        i = self.at(self.s, k, self.c)
        self.got(i)
        self.send(i, self.there(self.px), 3 * k + 3)
        self.send(i, self.there(self.py), 3 * k + 4)
        self.send(i, self.co, 3 * k + 5)

    def hop(self, kz):
        for j, (a, b) in enumerate(((self.px, self.py), (self.py, self.px))):
            i = self.at(a, kz, self.c)
            self.got(i)
            if kz % 2 == j:
                self.send(i, self.there(b), 15 + kz)
            self.send(i, self.co, 19 + 3 * kz + j)

    def diag(self, kz):
        i = self.at(self.pd, kz, self.c)
        self.got(i)
        self.send(i, self.co, 21 + 3 * kz)

    def end(self):
        for kz in range(NZ):
            for k in range(NS):
                self.got(self.at((self.s + k) % NS, kz, 1 - self.c))
        for n in range(ND - 1):
            remote(self.w, self.slot(0), self.ssem.at[n], self.rsem.at[0], self.co).wait_send()
        self.local().wait()


class LineGather:
    def __init__(self, w, out, ss, rs, ls):
        self.w, self.out, self.ss, self.rs, self.ls = w, out, ss, rs, ls
        s, self.z, c = place()
        self.zs = partners(s, self.z, c)[0]

    @staticmethod
    def sems():
        return [DMA((3,)), DMA((3,)), DMA(())]

    def local(self):
        return pltpu.make_async_copy(self.w, self.out.at[self.z], self.ls)

    def copy(self, k):
        return remote(self.w, self.out.at[self.z], self.ss.at[k], self.rs.at[k], self.zs[k])

    def start(self):
        for k in range(3):
            self.copy(k).start()
        self.local().start()

    def end(self):
        for k in range(3):
            self.copy(k).wait_recv()
            self.copy(k).wait_send()
        self.local().wait()


class PlaneGather:
    def __init__(self, w, out, ss, rx, rd, rc, ls):
        self.w, self.out, self.ss, self.rx, self.rd, self.rc, self.ls = w, out, ss, rx, rd, rc, ls
        self.s, self.z, self.c = place()
        self.co = partners(self.s, self.z, self.c)[2]
        self.col = (self.s,) + plane(self.s)

    @staticmethod
    def sems():
        return [DMA((9,)), DMA((2,)), DMA((2,)), DMA((4,)), DMA(())]

    def at(self, a):
        return self.out.at[self.col[a], :, self.c]

    def half(self, a, j):
        return self.out.at[self.col[a], pl.ds(2 * j, 2), self.c]

    def to(self, a):
        return {"seq": self.col[a], "dp": self.z * NCORE + self.c}

    def local(self):
        return pltpu.make_async_copy(self.w, self.at(0), self.ls)

    def direct(self, a):
        return remote(self.w, self.at(0), self.ss.at[a], self.rx.at[a - 1], self.to(a))

    def core(self, a):
        return remote(self.at(a) if a else self.w, self.at(a), self.ss.at[5 + a], self.rc.at[a], self.co)

    def on(self, a):
        return remote(self.half(a, a - 1), self.half(a, a - 1), self.ss.at[2 + a], self.rd.at[a - 1], self.to(3 - a))

    def start(self):
        self.direct(1).start()
        self.direct(2).start()
        self.core(0).start()
        self.local().start()

    def hop(self):
        for a in (1, 2):
            self.direct(a).wait_recv()
            self.on(a).start()
            self.core(a).start()

    def diag(self):
        self.on(1).wait_recv()
        self.on(2).wait_recv()
        self.core(3).start()

    def end(self):
        for a in range(4):
            self.core(a).wait_recv()
            self.core(a).wait_send()
        for a in (1, 2):
            self.direct(a).wait_send()
            self.on(a).wait_send()
        self.local().wait()


class Scatter:
    def __init__(self, g, outs, mine, rc, rd, rn, rz, lsem, cs, cr, xs, ds, dr, nr, zsem, zr):
        self.g, self.outs = g, outs
        self.mine, self.rc, self.rd, self.rn, self.rz = mine, rc, rd, rn, rz
        self.lsem, self.cs, self.cr, self.xs, self.ds, self.dr, self.nr, self.zsem, self.zr = lsem, cs, cr, xs, ds, dr, nr, zsem, zr
        self.s, self.z, self.c = place()
        self.zs, self.ss, self.co = partners(self.s, self.z, self.c)
        self.col = (self.s,) + plane(self.s)

    @staticmethod
    def bufs(rows, cols):
        v = lambda *n: pltpu.VMEM(n + (rows, cols), BF)
        return [v(4, NZ), v(4, NZ), v(2, 2), v(2, NZ), v(3), DMA((4,)), DMA((4,)), DMA((4,)), DMA((2,)), DMA((2,)), DMA((2,)), DMA((2,)),
                DMA((3,)), DMA((3,))]

    def core(self, a):
        return remote(self.g.at[self.col[a], :, 1 - self.c], self.rc.at[a], self.cs.at[a], self.cr.at[a], self.co)

    def load(self, a):
        return pltpu.make_async_copy(self.g.at[self.col[a], :, self.c], self.mine.at[a], self.lsem.at[a])

    def to(self, a):
        return {"seq": self.col[a], "dp": self.z * NCORE + self.c}

    def via(self, a):
        return remote(self.mine.at[3, pl.ds(2 * (a - 1), 2)], self.rd.at[a - 1], self.ds.at[a - 1], self.dr.at[a - 1], self.to(a))

    def last(self, a):
        return remote(self.mine.at[a], self.rn.at[a - 1], self.xs.at[a - 1], self.nr.at[a - 1], self.to(a))

    def zz(self, k):
        return remote(self.mine.at[0, (self.z + k) % NZ], self.rz.at[k - 1], self.zsem.at[k - 1], self.zr.at[k - 1], self.zs[k - 1])

    def start(self, which):
        for a in which:
            self.core(a).start()
            self.load(a).start()

    def both(self, a, j, ready=True):
        if ready:
            self.load(a).wait()
            self.core(a).wait_recv()
        return None if j is None else self.mine[a, j].astype(F32) + self.rc[a, j].astype(F32)

    def away(self):
        self.both(3, None)
        for a in (1, 2):
            for j in range(2 * (a - 1), 2 * a):
                self.mine[3, j] = self.both(3, j, False).astype(BF)
            self.via(a).start()

    def near(self):
        for a in (1, 2):
            self.both(a, None)
            self.via(3 - a).wait_recv()
            for j in range(NZ):
                v = self.both(a, j, False)
                if j // 2 == 2 - a:
                    v = v + self.rd[2 - a, j % 2].astype(F32)
                self.mine[a, j] = v.astype(BF)
            self.last(a).start()

    def total(self, j):
        v = self.mine[0, j].astype(F32) + self.rc[0, j].astype(F32)
        return v + (self.rn[0, j].astype(F32) + self.rn[1, j].astype(F32))

    def come(self):
        self.both(0, None)
        self.last(1).wait_recv()
        self.last(2).wait_recv()

    def line(self):
        self.come()
        for k in (1, 2, 3):
            j = (self.z + k) % NZ
            self.mine[0, j] = self.total(j).astype(BF)
            self.zz(k).start()

    def sent(self):
        for a in range(4):
            self.core(a).wait_send()
        for a in (1, 2):
            self.via(a).wait_send()
            self.last(a).wait_send()

    def stop(self, out):
        self.come()
        for j in range(NZ):
            out[j] = self.total(j).astype(BF)
        self.sent()

    def end(self):
        v = self.total(self.z)
        for k in (1, 2, 3):
            self.zz(k).wait_recv()
            v = v + self.rz[k - 1].astype(F32)
        at = 0
        for o in self.outs:
            o[...] = v[:, at:at + o.shape[1]]
            at += o.shape[1]
        self.sent()
        for k in (1, 2, 3):
            self.zz(k).wait_send()


class LineScatter:
    def __init__(self, part, out, mine, rz, lsem, ss, rs):
        self.part, self.out, self.mine, self.rz, self.lsem, self.ss, self.rs = part, out, mine, rz, lsem, ss, rs
        s, self.z, c = place()
        self.zs = partners(s, self.z, c)[0]

    @staticmethod
    def bufs(rows, cols):
        return [pltpu.VMEM((rows, cols), BF), pltpu.VMEM((3, rows, cols), BF), DMA(()), DMA((3,)), DMA((3,))]

    def copy(self, k):
        return remote(self.part.at[(self.z + k + 1) % NZ], self.rz.at[k], self.ss.at[k], self.rs.at[k], self.zs[k])

    def local(self):
        return pltpu.make_async_copy(self.part.at[self.z], self.mine, self.lsem)

    def start(self):
        for k in range(3):
            self.copy(k).start()
        self.local().start()

    def end(self):
        self.local().wait()
        v = self.mine[...].astype(F32)
        for k in range(3):
            self.copy(k).wait_recv()
            v = v + self.rz[k].astype(F32)
        self.out[...] = v
        for k in range(3):
            self.copy(k).wait_send()


def weights_in_kernel(w_ref, wm_ref, x_ref, base_ref, out_ref, zm_ref, xo_ref, bias_h, ga, gb, gc, la, lb, lc, xa, xb, xc, ya, yb, yc, tile, tsem):
    gat = Gather(w_ref, out_ref, ga, gb, gc)
    lin = LineGather(wm_ref, zm_ref, la, lb, lc)
    exc = Exchange(x_ref, xo_ref, xa, xb, xc, (0, 2))
    rest = Exchange(x_ref, xo_ref, ya, yb, yc, (1, 2))
    meet_all()
    gat.start()
    exc.start()

    def flush(h):
        return pltpu.make_async_copy(tile.at[h % 2], bias_h.at[h], tsem.at[h % 2])

    def head(h, carry):
        @pl.when(h >= 2)
        def _():
            flush(h - 2).wait()

        bias_tiles(base_ref, h, tile.at[h % 2])
        flush(h).start()
        return carry

    lax.fori_loop(0, H, head, 0)
    gat.line(1)
    gat.hop(0)
    gat.line(2)
    gat.line(3)
    lin.start()
    gat.diag(0)
    for kz in range(1, NZ):
        gat.hop(kz)
    rest.start()
    for kz in range(1, NZ):
        gat.diag(kz)
    flush(H - 2).wait()
    flush(H - 1).wait()
    gat.end()
    exc.end()
    rest.end()
    lin.end()


def weights_in(w, wm, x, base, cid):
    return pl.pallas_call(
        weights_in_kernel, in_specs=[ANY, ANY, ANY, VM], out_specs=[ANY] * 4,
        out_shape=[hbm((ND,) + w.shape, w.dtype), hbm((NZ,) + wm.shape, w.dtype), hbm(x.shape, x.dtype), hbm((H, NBK, BLK, BLK), F32)],
        scratch_shapes=Gather.sems() + LineGather.sems() + Exchange.sems() * 2 + [pltpu.VMEM((2, NBK, BLK, BLK), F32), DMA((2,))],
        compiler_params=params(24, cid), name="weights_in")(w, wm, x, base)


def hsum(sel, v):
    return lax.dot_general(sel, v, (((1,), (1,)), ((), ())), precision=lax.Precision.HIGHEST, preferred_element_type=F32)


def grads_out_kernel(g, dgs, dgc, dgf, gpre, gpost, diag, bucket, gt, oq, ok, ov, o_gain, o_pre, o_post, o_tab, gt_o,
                     mc, mx, mz, ms, mr, small, e1, e2, e3, *bufs):
    sca = Scatter(g, [oq, ok, ov], *bufs)
    s, z, c = place()
    zs, ss, co = partners(s, z, c)
    exc = Exchange(gt, gt_o, e1, e2, e3)
    meet_all()
    sca.start((3, 2, 1, 0))
    nbk = o_tab.shape[1]
    small[...] = jnp.zeros_like(small)
    for i, d in enumerate((dgs, dgc, dgf)):
        v = jnp.sum(d[...], 0, keepdims=True)
        for j in range(D // 128):
            small[6 * i + j:6 * i + j + 1, :] = v[:, j * 128:(j + 1) * 128]
    sel = (lax.broadcasted_iota(jnp.int32, (H, D), 1) // DH == lax.broadcasted_iota(jnp.int32, (H, D), 0)).astype(F32)
    small[24:24 + H, :H] = hsum(sel, gpre[...])
    small[24:24 + H, 16:16 + H] = hsum(gpost[...], sel)
    tab = jnp.zeros((H, nbk), F32)
    for d in range(NBK):
        hot = (lax.broadcasted_iota(jnp.int32, (nbk, 2 * BLK), 0) == bucket[d:d + 1, :]).astype(F32)
        tab = tab + hsum(diag[:, d, 0, :], hot)
    small[24:24 + H, 32:32 + nbk] = tab
    first = remote(small, mc, ms.at[0], mr.at[0], co)
    first.start()
    sca.away()
    first.wait_recv()
    mx[s] = small[...] + mc[...]
    xy = [remote(mx.at[s], mx.at[s], ms.at[k], mr.at[k], ss[k - 1]) for k in (1, 2, 3)]
    for cp in xy:
        cp.start()
    sca.near()
    exc.start()
    for cp in xy:
        cp.wait_recv()
    mz[z] = (mx[0] + mx[1]) + (mx[2] + mx[3])
    zz = [remote(mz.at[z], mz.at[z], ms.at[3 + k], mr.at[3 + k], zs[k - 1]) for k in (1, 2, 3)]
    for cp in zz:
        cp.start()
    sca.line()
    for cp in zz:
        cp.wait_recv()
    v = (mz[0] + mz[1]) + (mz[2] + mz[3])
    o_pre[...] = v[24:24 + H, :H]
    o_post[...] = v[24:24 + H, 16:16 + H]
    o_tab[...] = v[24:24 + H, 32:32 + nbk]
    o_gain[...] = v[:24]
    exc.end()
    sca.end()
    for cp in [first] + xy + zz:
        cp.wait_send()


def grads_out(g, small, gt, nbk, cid):
    sm = (40, 128)
    rows = g.shape[3]
    return pl.pallas_call(
        grads_out_kernel,
        in_specs=[ANY] + [VM] * len(small) + [ANY], out_specs=[VM] * 7 + [ANY],
        out_shape=[sds((rows, D), F32)] * 3
        + [sds((24, 128), F32), sds((H, H), F32), sds((H, H), F32), sds((H, nbk), F32), sds(gt.shape, BF)],
        scratch_shapes=[pltpu.VMEM(sm, F32), pltpu.VMEM((4,) + sm, F32), pltpu.VMEM((4,) + sm, F32), DMA((7,)), DMA((7,)),
                        pltpu.VMEM(sm, F32)] + Exchange.sems() + Scatter.bufs(*g.shape[3:]),
        compiler_params=params(56, cid), name="grads_out")(g, *small, gt)


def finish_kernel(n, *refs):
    acts, plain, rf = refs[:3], refs[3:3 + n], refs[3 + n]
    o_acts, o_plain, o_fo, o_fi = refs[4 + n:7 + n], refs[7 + n:7 + 2 * n], refs[7 + 2 * n], refs[8 + 2 * n]
    for a, b in zip(acts, o_acts):
        b[...] = a[...].astype(b.dtype)

    @pl.when(pl.program_id(0) == 0)
    def _():
        for a, b in zip(plain, o_plain):
            b[...] = a[...]
        nf = o_fi.shape[0]
        for j in range(nf):
            o_fi[j] = rf[:, 2 * j * D:(2 * j + 1) * D]
            o_fo[:, j, :] = rf[:, (2 * j + 1) * D:(2 * j + 2) * D]


def finish(acts, plain, rf):
    rows = rf.shape[0]
    nf = rf.shape[1] // (2 * D)
    blk = pl.BlockSpec((1,) + acts[0].shape[1:], lambda i: (i, 0, 0))
    whole = [pl.BlockSpec(p.shape, lambda i: (0, 0)) for p in plain]
    return pl.pallas_call(
        functools.partial(finish_kernel, len(plain)), grid=(acts[0].shape[0],),
        in_specs=[blk] * 3 + whole + [pl.BlockSpec(rf.shape, lambda i: (0, 0))],
        out_specs=[blk] * 3 + whole + [pl.BlockSpec((rows, nf, D), lambda i: (0, 0, 0)), pl.BlockSpec((nf, rows, D), lambda i: (0, 0, 0))],
        out_shape=[sds(a.shape, t) for a, t in zip(acts, (BF, F32, F32))] + [sds(p.shape, F32) for p in plain]
        + [sds((rows, nf, D), F32), sds((nf, rows, D), F32)],
        name="finish")(*acts, *plain, rf)


EPS = 1e-6
GATE = 0.7978845608028654


def cst(shape):
    return pl.BlockSpec(shape, lambda *a: (0,) * len(shape), pipeline_mode=pl.Buffered(1))


def col(shape, j):
    return pl.BlockSpec(shape, lambda *a: (0, j), pipeline_mode=pl.Buffered(1))


def each(f):
    def step(i, carry):
        f(pl.ds(pl.multiple_of(i * BLK, BLK), BLK))
        return carry

    lax.fori_loop(0, NBK, step, 0)


def rows8(v):
    return jnp.sum(v.reshape(v.shape[0] // 8, 8, v.shape[1]), 0)


def norm(x, g):
    return x * lax.rsqrt(jnp.mean(x * x, -1, keepdims=True) + EPS) * g


def norm_grad(x, g, dn):
    r = lax.rsqrt(jnp.mean(x * x, -1, keepdims=True) + EPS)
    gd = g * dn
    dx = r * gd - x * (r * r * r) * jnp.mean(gd * x, -1, keepdims=True)
    return dx, rows8(dn * x * r)


def gelu_pair(x):
    x2 = x * x
    t = jnp.tanh(x * (GATE + GATE * 0.044715 * x2))
    hp = 0.5 + 0.5 * t
    y = x * hp
    d = hp + 0.5 * x * (1.0 - t * t) * (GATE + 3 * GATE * 0.044715 * x2)
    return y, d


def blocks(n=NBK):
    return [slice(i * BLK, (i + 1) * BLK) for i in range(n)]


FWD_PLAN = ((2, "exc", 0), (5, "hop", 0), (5, "exc", 1), (9, "diag", 0))
CROSS_PLAN = ((4, "hop"),)


def self_fwd_kernel(near, st_ref, x_ref, w_ref, gn_ref, bias_ref, pre_ref, post_ref, *refs):
    if near:
        (zm_h, wf_h, enc_h, cot_h, q_ref, k_ref, v_ref, att_ref, gain_ref, mpre_ref, mpost_ref, p_ref, wo_h, zf_h, eo_h, co_h, acc_ref, lo_ref,
         ags, lgs, ex1, ex2) = split(refs, 18, 5, 3, 3, 3)
        gat = PlaneGather(zm_h, wo_h, *ags)
        lin = LineGather(wf_h, zf_h, *lgs)
        exc = [Exchange(enc_h, eo_h, *ex1), Exchange(cot_h, co_h, *ex2)]
    else:
        q_ref, k_ref, v_ref, att_ref, gain_ref, mpre_ref, mpost_ref, p_ref, acc_ref, lo_ref = refs
    h = pl.program_id(0)

    if near:
        @pl.when(h == 0)
        def _():
            meet_all()
            gat.start()
            lin.start()

        for hh, name, k in FWD_PLAN:
            @pl.when(h == hh)
            def _(name=name, k=k):
                if name == "exc":
                    exc[k].start()
                else:
                    getattr(gat, name)()

    @pl.when(h == 0)
    def _():
        acc_ref[...] = jnp.zeros_like(acc_ref)
        gt = gn_ref[...].astype(F32).T
        gain_ref[...] = gt[:8]
        g = gt[:1]

        def project(r):
            n1 = norm(x_ref[r, :].astype(F32), g).astype(BF)
            for j, o in enumerate((q_ref, k_ref, v_ref)):
                o[r, :] = dot(n1, w_ref[:, j * D:(j + 1) * D], 1, 0).astype(BF)

        each(project)
        pos = lax.broadcasted_iota(jnp.int32, (L, 128), 0)
        lo = jnp.zeros((L, 128), jnp.int32)
        me = lax.axis_index("seq")
        for d in range(1, st_ref.shape[1]):
            sd = st_ref[me, d]
            lo = jnp.where(pos >= sd, sd, lo)
        lo_ref[...] = lo
        sel = (lax.broadcasted_iota(jnp.int32, (H, D), 1) // DH == lax.broadcasted_iota(jnp.int32, (H, D), 0)).astype(F32)
        wide = lambda m, k: lax.dot_general(m[...], sel, (((k,), (0,)), ((), ())), precision=lax.Precision.HIGHEST,
                                            preferred_element_type=F32)
        mpre_ref[...] = wide(pre_ref, 0)
        mpost_ref[...] = wide(post_ref, 1)

    mp = mpre_ref[pl.ds(h, 1), :]
    mo = mpost_ref[pl.ds(h, 1), :]

    def scores(i):
        n = (i + 1) * BLK
        qm = (q_ref[i * BLK:n, :].astype(F32) * mp).astype(BF)
        return dot(qm, k_ref[:n, :], 1, 1)

    sc = scores(NBK - 1)
    for i in reversed(range(NBK)):
        nxt = scores(i - 1) if i else None
        n = (i + 1) * BLK
        r = slice(i * BLK, n)
        bias = jnp.concatenate([bias_ref[0, i - j] for j in range(i + 1)], 1) if i else bias_ref[0, 0]
        c = lax.broadcasted_iota(jnp.int32, (BLK, n), 1)
        sc = jnp.where(c >= lo_ref[r, :1], sc + bias, NEG)
        e = jnp.exp(sc - jnp.max(sc, 1, keepdims=True))
        p = (e * (1.0 / jnp.sum(e, 1, keepdims=True))).astype(BF)
        p_ref[0, r, :n] = p
        acc_ref[r, :] += dot(p, v_ref[:n, :], 1, 0) * mo
        sc = nxt

    @pl.when(h == H - 1)
    def _():
        att_ref[...] = acc_ref[...].astype(BF)
        if near:
            lin.end()
            gat.end()
            for e in exc:
                e.end()


def self_fwd(starts, x, w1, bias, mpre, mpost, far=None, cid=None):
    one = cst((L, D))
    near = far is not None
    extra_out = []
    if near:
        extra_out = [sds((NS, NZ, NCORE) + far[0].shape[1:], BF), sds((NZ,) + far[1].shape, BF)] + [sds(f.shape, BF) for f in far[2:]]
    return pl.pallas_call(
        functools.partial(self_fwd_kernel, near),
        grid_spec=pltpu.PrefetchScalarGridSpec(
            num_scalar_prefetch=1, grid=(H,),
            in_specs=[one, col((D, 3 * D), 0), col((D, 128), 18),
                      pl.BlockSpec((1, NBK, BLK, BLK), lambda h, st: (h, 0, 0, 0)), cst((H, H)), cst((H, H))]
            + [ANY] * (4 * near),
            out_specs=[one] * 4 + [cst((8, D)), cst((H, D)), cst((H, D)), pl.BlockSpec((1, L, L), lambda h, st: (h, 0, 0))] + [ANY] * (4 * near),
            scratch_shapes=[pltpu.VMEM((L, D), F32), pltpu.VMEM((L, 128), jnp.int32)]
            + (PlaneGather.sems() + LineGather.sems() + Exchange.sems() * 2 if near else [])),
        out_shape=[sds((L, D), BF)] * 4 + [sds((8, D), F32), sds((H, D), F32), sds((H, D), F32), sds((H, L, L), BF)] + extra_out,
        compiler_params=params(62, cid),
        cost_estimate=pl.CostEstimate(flops=52_000_000_000, bytes_accessed=45_000_000, transcendentals=8_000_000),
        name="self_fwd")(starts, x, w1, w1, bias, mpre, mpost, *(far or ()))


def cross_fwd_kernel(near, x_ref, att_ref, wo_ref, wq_ref, wk_ref, wv_ref, enc_ref, gain_ref, *refs):
    if near:
        zf_h, h1_ref, n2_ref, q_ref, k_ref, v_ref, catt_ref, p_ref, fo_h, ags = split(refs, 9, 5)
        gat = PlaneGather(zf_h, fo_h, *ags)
    else:
        h1_ref, n2_ref, q_ref, k_ref, v_ref, catt_ref, p_ref = refs
    h = pl.program_id(0)

    if near:
        @pl.when(h == 0)
        def _():
            meet_all()
            gat.start()

        for hh, name in CROSS_PLAN:
            @pl.when(h == hh)
            def _(name=name):
                getattr(gat, name)()

    @pl.when(h == 0)
    def _():
        g = gain_ref[1:2, :]

        def project(r):
            h1 = x_ref[r, :].astype(F32) + dot(att_ref[r, :], wo_ref[...], 1, 0)
            h1_ref[r, :] = h1
            n2 = norm(h1, g).astype(BF)
            n2_ref[r, :] = n2
            q_ref[r, :] = dot(n2, wq_ref[...], 1, 0).astype(BF)
            k_ref[r, :] = dot(enc_ref[r, :], wk_ref[...], 1, 0).astype(BF)
            v_ref[r, :] = dot(enc_ref[r, :], wv_ref[...], 1, 0).astype(BF)

        each(project)

    cols = pl.ds(pl.multiple_of(h * 128, 128), 128)
    first = lax.broadcasted_iota(jnp.int32, (1, 128), 1) < DH
    k = k_ref[:, cols]
    v = v_ref[:, cols]
    steps = [(r, e) for r in blocks() for e in range(2)]

    def scores(r, e):
        q = q_ref[r, cols]
        return dot(jnp.where(first if e == 0 else ~first, q, jnp.zeros_like(q)), k, 1, 1)

    sc = scores(*steps[0])
    keep = None
    for n, (r, e) in enumerate(steps):
        nxt = scores(*steps[n + 1]) if n + 1 < len(steps) else None
        ex = jnp.exp(sc - jnp.max(sc, 1, keepdims=True))
        p = (ex * (1.0 / jnp.sum(ex, 1, keepdims=True))).astype(BF)
        p_ref[e, r, :] = p
        o = dot(p, v, 1, 0)
        if e == 0:
            keep = o
        else:
            catt_ref[r, cols] = jnp.where(first, keep, o).astype(BF)
        sc = nxt

    if near:
        @pl.when(h == H // 2 - 1)
        def _():
            gat.diag()
            gat.end()


def cross_fwd(x, att, wmid, enc, gains, far=None, cid=None):
    one = cst((L, D))
    near = far is not None
    return pl.pallas_call(
        functools.partial(cross_fwd_kernel, near), grid=(H // 2,),
        in_specs=[one, one] + [col((D, D), j) for j in range(4)] + [one, cst((8, D))] + [ANY] * near,
        out_specs=[one] * 6 + [pl.BlockSpec((2, L, L), lambda h: (h, 0, 0))] + [ANY] * near,
        out_shape=[sds((L, D), F32)] + [sds((L, D), BF)] * 5 + [sds((H, L, L), BF)]
        + ([sds((NS, NZ, NCORE) + far.shape[1:], BF)] if near else []),
        scratch_shapes=PlaneGather.sems() if near else [],
        compiler_params=params(62, cid),
        cost_estimate=pl.CostEstimate(flops=31_000_000_000, bytes_accessed=50_000_000, transcendentals=12_000_000),
        name="cross_fwd")(x, att, wmid, wmid, wmid, wmid, enc, gains, *([far] if near else []))


def feed_kernel(h1_ref, catt_ref, wco_ref, cot_ref, gain_ref, fi_ref, fo_ref,
                out_ref, bh2_ref, bca_ref, gw_ref, dg_ref,
                n3, n3t, cott, acc, dn, inner, bi):
    a = pl.program_id(0)
    g = gain_ref[2:3, :]

    @pl.when(a == 0)
    def _():

        def enter(r):
            h2 = h1_ref[r, :] + dot(catt_ref[r, :], wco_ref[...], 1, 0)
            bh2_ref[r, :] = h2
            acc[r, :] = h2
            n3[r, :] = norm(h2, g).astype(BF)

        each(enter)
        n3t[...] = n3[...].T
        cott[...] = cot_ref[...].T
        dn[...] = jnp.zeros_like(dn)

    for r in blocks():
        u = dot(n3[r, :], fi_ref[...], 1, 0)
        y, d = gelu_pair(u)
        y = y.astype(BF)
        inner[r, :] = y
        gy = dot(cot_ref[r, :], fo_ref[...], 1, 1)
        b = (gy * d).astype(BF)
        bi[r, :] = b
        acc[r, :] += dot(y, fo_ref[...], 1, 0)
        dn[r, :] += dot(b, fi_ref[...], 1, 1)
    gw_ref[:, :D] = dot(n3t[...], bi[...], 1, 0).astype(BF)
    gw_ref[:, D:] = dot(cott[...], inner[...], 1, 0).T.astype(BF)

    @pl.when(a == pl.num_programs(0) - 1)
    def _():
        dg_ref[...] = jnp.zeros_like(dg_ref)

        def leave(r):
            out_ref[r, :] = acc[r, :].astype(BF)
            dx, s = norm_grad(bh2_ref[r, :], g, dn[r, :])
            dg_ref[...] += s
            b2 = cot_ref[r, :].astype(F32) + dx
            bh2_ref[r, :] = b2
            bca_ref[r, :] = dot(b2.astype(BF), wco_ref[...], 1, 1).astype(BF)

        each(leave)


def feed(h1, catt, wmid, cot, gains, wfeed):
    one = cst((L, D))
    nf = wfeed.shape[1] // (2 * D)
    return pl.pallas_call(
        feed_kernel, grid=(nf,),
        in_specs=[one, one, col((D, D), 4), one, cst((8, D)),
                  pl.BlockSpec((D, D), lambda a: (0, 2 * a)), pl.BlockSpec((D, D), lambda a: (0, 2 * a + 1))],
        out_specs=[one, one, one, pl.BlockSpec((D, 2 * D), lambda a: (0, a)), cst((8, D))],
        out_shape=[sds((L, D), BF), sds((L, D), F32), sds((L, D), BF), sds((D, wfeed.shape[1]), BF), sds((8, D), F32)],
        scratch_shapes=[pltpu.VMEM((L, D), BF), pltpu.VMEM((D, L), BF), pltpu.VMEM((D, L), BF), pltpu.VMEM((L, D), F32),
                        pltpu.VMEM((L, D), F32), pltpu.VMEM((L, D), BF), pltpu.VMEM((L, D), BF)],
        compiler_params=pltpu.CompilerParams(vmem_limit_bytes=62 << 20),
        cost_estimate=pl.CostEstimate(flops=32_000_000_000, bytes_accessed=50_000_000, transcendentals=3_000_000),
        name="feed")(h1, catt, wmid, cot, gains, wfeed, wfeed)


def cross_bwd_kernel(near, q_ref, k_ref, v_ref, do_ref, p_ref, gain_ref, n2_h, enc_h, att_h, catt_h, h1_h, bh2_h, w_h, *refs):
    if near:
        gf_h = refs[0]
        gw_ref, genc_ref, bh1_ref, bat_ref, dg_ref, rf_ref = refs[1:7]
        qt, dot_, ds, dq, dk, dv, n2, enc, att, catt, h1, w, sems, sca = split(refs[7:], 13, len(Scatter.bufs(8, D)))
        sca = Scatter(gf_h, [], *sca)
    else:
        gw_ref, genc_ref, bh1_ref, bat_ref, dg_ref = refs[:5]
        qt, dot_, ds, dq, dk, dv, n2, enc, att, catt, h1, w, sems = refs[5:]
    h = pl.program_id(0)
    late = [(n2_h, n2), (enc_h, enc), (att_h, att), (catt_h, catt), (h1_h, h1), (bh2_h, bh1_ref)]
    late += [(w_h.at[:, pl.ds(0, 4 * D)], w)]
    copies = [pltpu.make_async_copy(a, b, sems.at[i]) for i, (a, b) in enumerate(late)]

    @pl.when(h == 0)
    def _():
        if near:
            meet_all()
            sca.start((3,))

    @pl.when(h == 3)
    def _():
        for c in copies:
            c.start()

    if near:
        for hh, name, *more in BWD_PLAN:
            @pl.when(h == hh)
            def _(name=name, more=more):
                getattr(sca, name)(*more)

    e = h % 2
    cols = pl.ds(pl.multiple_of((h // 2) * 128, 128), 128)
    fe = (lax.broadcasted_iota(jnp.int32, (1, 128), 1) // DH) == e
    k = k_ref[...]
    v = v_ref[...]

    @pl.when(e == 0)
    def _():
        qt[...] = q_ref[...].T
        dot_[...] = do_ref[...].T

    for r in blocks():
        do = do_ref[r, :]
        dp = dot(jnp.where(fe, do, jnp.zeros_like(do)), v, 1, 1)
        p = p_ref[0, r, :].astype(F32)
        d = (p * (dp - jnp.sum(dp * p, 1, keepdims=True))).astype(BF)
        ds[r, :] = d
        dq[r, cols] = jnp.where(fe, dot(d, k, 1, 0).astype(BF), dq[r, cols])
    x = dot(dot_[...], p_ref[0], 1, 0).T.astype(BF)
    dv[:, cols] = jnp.where(fe, x, dv[:, cols])
    x = dot(qt[...], ds[...], 1, 0).T.astype(BF)
    dk[:, cols] = jnp.where(fe, x, dk[:, cols])

    @pl.when(h == H - 1)
    def _():
        for c in copies:
            c.wait()
        g = gain_ref[1:2, :]
        dg_ref[...] = jnp.zeros_like(dg_ref)
        gw_ref[:, D:2 * D] = dot(n2[...], dq[...], 0, 0).astype(BF)
        gw_ref[:, 2 * D:3 * D] = dot(enc[...], dk[...], 0, 0).astype(BF)
        gw_ref[:, 3 * D:4 * D] = dot(enc[...], dv[...], 0, 0).astype(BF)

        def leave(r):
            genc_ref[r, :] = (dot(dk[r, :], w[:, 2 * D:3 * D], 1, 1) + dot(dv[r, :], w[:, 3 * D:], 1, 1)).astype(genc_ref.dtype)
            dx, s = norm_grad(h1[r, :], g, dot(dq[r, :], w[:, D:2 * D], 1, 1))
            dg_ref[...] += s
            b2 = bh1_ref[r, :]
            b1 = b2 + dx
            bh1_ref[r, :] = b1
            b1 = b1.astype(BF)
            n2[r, :] = b1
            enc[r, :] = b2.astype(BF)
            bat_ref[r, :] = dot(b1, w[:, :D], 1, 1).astype(BF)

        each(leave)
        gw_ref[:, :D] = dot(att[...], n2[...], 0, 0).astype(BF)
        gw_ref[:, 4 * D:] = dot(catt[...], enc[...], 0, 0).astype(BF)
        if near:
            sca.stop(rf_ref)


BWD_PLAN = ((1, "away"), (1, "start", (2, 1)), (3, "start", (0,)), (6, "near"))


def cross_bwd(q, k, v, do, p, gains, n2, enc, att, catt, h1, bh2, wmid, far=None, cid=None):
    one = cst((L, D))
    near = far is not None
    pair = pl.BlockSpec((L, 128), lambda h: (0, h // 2))
    act = pltpu.VMEM((L, D), BF)
    more = [(NZ,) + far.shape[3:]] if near else []
    return pl.pallas_call(
        functools.partial(cross_bwd_kernel, near), grid=(H,),
        in_specs=[pair] * 4 + [pl.BlockSpec((1, L, L), lambda h: (h, 0, 0)), cst((8, D))] + [ANY] * (7 + near),
        out_specs=[cst((D, 5 * D)), one, one, one, cst((8, D))] + [cst(s) for s in more],
        out_shape=[sds((D, 5 * D), BF), sds((L, D), BF), sds((L, D), F32), sds((L, D), BF), sds((8, D), F32)]
        + [sds(s, BF) for s in more],
        scratch_shapes=[pltpu.VMEM((128, L), BF)] * 2 + [pltpu.VMEM((L, L), BF)] + [act] * 7
        + [pltpu.VMEM((L, D), F32), pltpu.VMEM((D, 4 * D), BF), DMA((7,))] + sum([Scatter.bufs(*s[1:]) for s in more], []),
        compiler_params=params(62, cid),
        cost_estimate=pl.CostEstimate(flops=37_000_000_000, bytes_accessed=70_000_000, transcendentals=0),
        name="cross_bwd")(q, k, v, do, p, gains, n2, enc, att, catt, h1, bh2, wmid, *([far] if near else []))


SELF_PLAN = ((1, "away"), (1, "start", (2, 1, 0)), (3, "near"), (3, "exc", 0), (6, "exc", 1), (8, "line"))


def self_bwd_kernel(near, q_ref, k_ref, v_ref, ba_ref, p_ref, mpre_ref, mpost_ref, gain_ref, x_h, bh1_h, w_h, *refs):
    if near:
        gm_h, zf_h, out_h, ge_h = refs[:4]
        gw_ref, gtok_ref, gpre_ref, gpost_ref, diag_ref, dg_ref = refs[4:10]
        rms, (rf_ref, oo_h, go_h) = refs[10:15], refs[15:18]
        qt, bat, dqa, dkt, dvt, dm, x, bh1, w, sems, sca, lin, ex1, ex2 = split(refs[18:], 10, len(Scatter.bufs(8, D)), 5, 3, 3)
        lin = LineScatter(zf_h, rf_ref, *lin)
        sca = Scatter(gm_h, rms, *sca)
        exc = [Exchange(out_h, oo_h, *ex1), Exchange(ge_h, go_h, *ex2)]
    else:
        gw_ref, gtok_ref, gpre_ref, gpost_ref, diag_ref, dg_ref = refs[:6]
        qt, bat, dqa, dkt, dvt, dm, x, bh1, w, sems = refs[6:]
    h = pl.program_id(0)

    if near:
        @pl.when(h == 0)
        def _():
            meet_all()
            sca.start((3,))
            lin.start()

        for hh, name, *more in SELF_PLAN:
            @pl.when(h == hh)
            def _(name=name, more=more):
                if name == "exc":
                    exc[more[0]].start()
                else:
                    getattr(sca, name)(*more)

    late = [(x_h, x), (bh1_h, bh1), (w_h.at[:, pl.ds(0, 3 * D)], w)]
    copies = [pltpu.make_async_copy(a, b, sems.at[i]) for i, (a, b) in enumerate(late)]

    @pl.when(h == 0)
    def _():
        for c in copies:
            c.start()
        qt[...] = q_ref[...].T
        bat[...] = ba_ref[...].T
        dqa[...] = jnp.zeros_like(dqa)
        dkt[...] = jnp.zeros_like(dkt)
        dvt[...] = jnp.zeros_like(dvt)

    mp = mpre_ref[pl.ds(h, 1), :]
    mo = mpost_ref[pl.ds(h, 1), :]
    gp = jnp.zeros((8, D), F32)
    dacc = [None] * NBK
    for i, r in enumerate(blocks()):
        n = (i + 1) * BLK
        bam = (ba_ref[r, :].astype(F32) * mo).astype(BF)
        dp = dot(bam, v_ref[:n, :], 1, 1)
        p = p_ref[0, r, :n].astype(F32)
        d = p * (dp - jnp.sum(dp * p, 1, keepdims=True))
        for j in range(i + 1):
            t = d[:, j * BLK:(j + 1) * BLK]
            dacc[i - j] = t if dacc[i - j] is None else dacc[i - j] + t
        db = d.astype(BF)
        dm[r, :n] = db
        rr = dot(db, k_ref[:n, :], 1, 0)
        dqa[r, :] += rr * mp
        gp = gp + rows8(rr * q_ref[r, :].astype(F32))
    gpre_ref[pl.ds(h, 1), :] = jnp.sum(gp, 0, keepdims=True)
    for t in range(NBK):
        y = jnp.concatenate([jnp.zeros((BLK, BLK), F32), dacc[t]], 1)
        n = BLK // 2
        while n >= 1:
            y = y[:n] + pltpu.roll(y[n:], 2 * BLK - n, 1)
            n //= 2
        diag_ref[0, t] = y
    mpc = jnp.broadcast_to(mp, (8, D)).T[:, :1]
    moc = jnp.broadcast_to(mo, (8, D)).T[:, :1]
    gq = jnp.zeros((8, D), F32)
    for c in blocks():
        i0 = c.start
        t = dot(bat[:, i0:], p_ref[0, i0:, c], 1, 0)
        dvt[:, c] += t * moc
        gq = gq + rows8(t.T * v_ref[c, :].astype(F32))
        u = dot(qt[:, i0:], dm[i0:, c], 1, 0)
        dkt[:, c] += u * mpc
    gpost_ref[pl.ds(h, 1), :] = jnp.sum(gq, 0, keepdims=True)

    @pl.when(h == H - 1)
    def _():
        for c in copies:
            c.wait()
        g = gain_ref[:1, :]
        dg_ref[...] = jnp.zeros_like(dg_ref)

        def leave(r):
            xr = x[r, :].astype(F32)
            n1 = norm(xr, g).astype(BF)
            dk = dkt[:, r].T.astype(BF)
            dv = dvt[:, r].T.astype(BF)
            dq = dqa[r, :].astype(BF)
            bat[:, r] = n1.T
            dm[r, :D] = dq
            dqa[r, :] = dk.astype(F32)
            back = dot(dq, w[:, :D], 1, 1) + dot(dk, w[:, D:2 * D], 1, 1) + dot(dv, w[:, 2 * D:], 1, 1)
            dx, s = norm_grad(xr, g, back)
            dg_ref[...] += s
            gtok_ref[r, :] = (bh1[r, :] + dx).astype(gtok_ref.dtype)

        each(leave)
        gw_ref[:, :D] = dot(bat[...], dm[:, :D], 1, 0).astype(BF)
        gw_ref[:, D:2 * D] = dot(bat[...], dqa[...].astype(BF), 1, 0).astype(BF)
        gw_ref[:, 2 * D:] = dot(bat[...], dvt[...].astype(BF), 1, 1).astype(BF)
        if near:
            lin.end()
            sca.end()
            for e in exc:
                e.end()


def self_bwd(q, k, v, ba, p, mpre, mpost, gains, x, bh1, w1, far=None, cid=None):
    one = cst((L, D))
    near = far is not None
    rows = far[0].shape[3] if near else 0
    more = [cst((rows, D))] * 5 + [cst(far[1].shape[1:]), ANY, ANY] if near else []
    more_out = []
    if near:
        more_out = [sds((rows, D), F32)] * 5 + [sds(far[1].shape[1:], F32)] + [sds(f.shape, BF) for f in far[2:]]
    return pl.pallas_call(
        functools.partial(self_bwd_kernel, near), grid=(H,),
        in_specs=[one] * 4 + [pl.BlockSpec((1, L, L), lambda h: (h, 0, 0)), cst((H, D)), cst((H, D)), cst((8, D))] + [ANY] * (3 + 4 * near),
        out_specs=[cst((D, 3 * D))] + [one, cst((H, D)), cst((H, D)),
                   pl.BlockSpec((1, NBK, 1, 2 * BLK), lambda h: (h, 0, 0, 0)), cst((8, D))] + more,
        out_shape=[sds((D, 3 * D), BF)] + [sds((L, D), BF), sds((H, D), F32), sds((H, D), F32),
                   sds((H, NBK, 1, 2 * BLK), F32), sds((8, D), F32)] + more_out,
        scratch_shapes=[pltpu.VMEM((D, L), BF)] * 2 + [pltpu.VMEM((L, D), F32)] + [pltpu.VMEM((D, L), F32)] * 2
        + [pltpu.VMEM((L, L), BF), pltpu.VMEM((L, D), BF), pltpu.VMEM((L, D), F32), pltpu.VMEM((D, 3 * D), BF), DMA((3,))]
        + (Scatter.bufs(*far[0].shape[3:]) + LineScatter.bufs(*far[1].shape[1:]) + Exchange.sems() * 2 if near else []),
        compiler_params=params(62, cid),
        cost_estimate=pl.CostEstimate(flops=128_000_000_000, bytes_accessed=50_000_000, transcendentals=0),
        name="self_bwd")(q, k, v, ba, p, mpre, mpost, gains, x, bh1, w1, *(far or ()))


AX = ("seq", "dp")


def gather(w):
    return lax.all_gather(w, AX, axis=0, tiled=True)


def scatter(g):
    return lax.psum_scatter(g, AX, scatter_dimension=0, tiled=True).astype(F32)


def per_device(tokens, encoded, cotangent, doc_starts, rel_bucket, sq, sk, sv, so, cq, ck, cv, co, fi, fo,
               gs, gc, gf, mix_pre, mix_post, rel_table):
    nseq, ndp = lax.axis_size("seq"), lax.axis_size("dp")
    rows = sq.shape[0]
    nf = fo.shape[0] // rows
    ndev = nseq * ndp
    buckets = rel_table.shape[0]
    near = nseq == NS and ndp == NZ * NCORE and rows % 8 == 0
    to_stream = lambda x: lax.all_to_all(x, "seq", 0, 1, tiled=True).reshape(L, D)
    from_stream = lambda x: lax.all_to_all(x.reshape(1, L, D), "seq", 1, 0, tiled=True)
    hot = (rel_bucket[:, None] == jnp.arange(buckets)[None, :]).astype(F32)
    trow = lax.dot_general(rel_table, hot, (((0,), (1,)), ((), ())), precision=lax.Precision.HIGHEST)
    base = make_base(trow)
    gains = jnp.pad(jnp.stack([gs, gc, gf], 1), ((0, 0), (0, 125)))
    w1 = jnp.concatenate([sq, sk, sv, gains], 1)
    wmid = jnp.concatenate([so, cq, ck, cv, co], 1)
    wfeed = jnp.stack([fi.reshape(rows, D, nf).transpose(0, 2, 1), fo.reshape(rows, nf, D)], 2).reshape(rows, 2 * nf * D)
    if near:
        w1, zmid, x, bias = weights_in(w1, wmid, tokens, base, 1)
        w1 = w1.reshape(D, -1)
        x = x.reshape(L, D)
    else:
        w1 = gather(w1)
        x = to_stream(tokens)
        bias = toeplitz(base)
        wmid = gather(wmid)
        wfeed = gather(wfeed)
        enc = to_stream(encoded)
        cot = to_stream(cotangent)
    if near:
        q, k, v, att, gain, mpre, mpost, p, wmid, zfeed, enc, cot = self_fwd(doc_starts, x, w1, bias, mix_pre, mix_post, (zmid, wfeed, encoded, cotangent), 2)
        wmid = wmid.reshape(D, -1)
        enc = enc.reshape(L, D)
        h1, n2, cqx, ckx, cvx, catt, cp, wfeed = cross_fwd(x, att, wmid, enc, gain, zfeed, 3)
        cot = cot.reshape(L, D)
        wfeed = wfeed.reshape(D, -1)
    else:
        q, k, v, att, gain, mpre, mpost, p = self_fwd(doc_starts, x, w1, bias, mix_pre, mix_post)
        h1, n2, cqx, ckx, cvx, catt, cp = cross_fwd(x, att, wmid, enc, gain)
    out, bh2, bca, gw_feed, dgf = feed(h1, catt, wmid, cot, gain, wfeed)
    by_dev = lambda a: a.reshape(NS, NZ, NCORE, rows, -1)
    back = (cqx, ckx, cvx, bca, cp, gain, n2, enc, att, catt, h1, bh2, wmid)
    if near:
        gw_mid, g_enc, bh1, bat, dgc, zfeed = cross_bwd(*back, by_dev(gw_feed), 6)
    else:
        gw_mid, g_enc, bh1, bat, dgc = cross_bwd(*back)
        r_feed = scatter(gw_feed)
    blk = lambda a: a.reshape(nseq, L // nseq, D)
    if near:
        far = (by_dev(gw_mid), zfeed, blk(out), blk(g_enc))
        gw_qkv, g_tok, gpre, gpost, diag, dgs, *r_mid, r_feed, out, g_enc = self_bwd(
            q, k, v, bat, p, mpre, mpost, gain, x, bh1, w1, far, 4)
    else:
        gw_qkv, g_tok, gpre, gpost, diag, dgs = self_bwd(q, k, v, bat, p, mpre, mpost, gain, x, bh1, w1)
    if near:
        pad = jnp.pad(rel_bucket[::-1], (BLK, BLK), constant_values=-1)
        bucket = jnp.stack([lax.slice(pad, (L + BLK - 1 - (d * BLK + BLK),), (L + BLK - 1 - (d * BLK + BLK) + 2 * BLK,))
                            for d in range(NBK)])
        r_q, r_k, r_v, dgain, gpre, gpost, gtab, g_tok = grads_out(
            by_dev(gw_qkv), [dgs, dgc, dgf, gpre, gpost, diag, bucket], blk(g_tok), buckets, 5)
        out, g_tok, g_enc, *plain, g_fo, g_fi = finish([out, g_tok, g_enc], [r_q, r_k, r_v, *r_mid, dgain, gpre, gpost, gtab], r_feed)
        r_q, r_k, r_v = plain[:3]
        r_mid, (dgain, gpre, gpost, gtab) = plain[3:8], plain[8:]
        gtab = gtab.T
        dgain = dgain[:18].reshape(3, D)
    else:
        gpre = gpre.reshape(H, H, DH).sum(-1).T
        gpost = gpost.reshape(H, H, DH).sum(-1)
        dg = diag[:, :, 0, ::-1]
        gt = 0.0
        for d in range(NBK):
            gt = gt + jnp.pad(dg[:, d], ((0, 0), (d * BLK + 1, L - d * BLK - 1)))
        gt = gt[:, BLK:BLK + L]
        gtab = lax.dot_general(hot, gt, (((0,), (1,)), ((), ())), precision=lax.Precision.HIGHEST)
        dgain = jnp.stack([dgs.sum(0), dgc.sum(0), dgf.sum(0)])
        r_mid = jnp.split(scatter(gw_mid), 5, 1)
        r_q, r_k, r_v = jnp.split(scatter(gw_qkv), 3, 1)
        out, g_tok, g_enc = from_stream(out), from_stream(g_tok).astype(F32), from_stream(g_enc).astype(F32)
        dgain, gpre, gpost, gtab = lax.psum((dgain, gpre, gpost, gtab), AX)
        r_feed = r_feed.reshape(rows, nf, 2, D)
        g_fi, g_fo = r_feed[:, :, 0].transpose(1, 0, 2), r_feed[:, :, 1].reshape(rows * nf, D)
    g_fi = g_fi.transpose(1, 2, 0).reshape(rows, nf * D)
    g_fo = g_fo.reshape(rows * nf, D)
    me = lax.axis_index("seq") * ndp + lax.axis_index("dp")
    dgain = lax.dynamic_slice_in_dim(dgain, me * rows, rows, 1)
    return (out, g_tok, g_enc,
            r_q, r_k, r_v, *r_mid,
            g_fi, g_fo,
            dgain[0], dgain[1], dgain[2], gpre, gpost, gtab)


def solution(mesh):
    act = P("dp", "seq", None)
    w = P(AX, None)
    g = P(AX)
    return jax.shard_map(
        per_device, mesh=mesh, in_specs=(act, act, act, P("dp", None), P()) + (w,) * 10 + (g,) * 3 + (P(),) * 3,
        out_specs=(act,) * 3 + (w,) * 10 + (g,) * 3 + (P(),) * 3, check_vma=False)
```

```python
import functools

import jax
import jax.numpy as jnp
from jax import lax
from jax.experimental import pallas as pl
from jax.experimental.pallas import tpu as pltpu
from jax.sharding import PartitionSpec as P

F32 = jnp.float32
BF = jnp.bfloat16
NEG = -1e30
H, DH, D, L = 12, 64, 768, 1024
BLK = 256
NBK = L // BLK


def dot(a, b, ca, cb):
    return lax.dot_general(a, b, (((ca,), (cb,)), ((), ())), preferred_element_type=F32)


def bias_tiles(base_ref, h, out_ref):
    for d in range(NBK):
        row = jnp.broadcast_to(base_ref[h, d], (BLK, 2 * BLK))
        t = pltpu.roll(row, 0, 1, stride=1, stride_axis=0)[:, :BLK]
        if d == 0:
            a = lax.broadcasted_iota(jnp.int32, (BLK, BLK), 0)
            b = lax.broadcasted_iota(jnp.int32, (BLK, BLK), 1)
            t = jnp.where(a >= b, t, NEG)
        out_ref[d] = t


def toeplitz(base):
    def kernel(base_ref, out_ref):
        bias_tiles(base_ref, 0, out_ref.at[0])

    return pl.pallas_call(
        kernel, grid=(H,), in_specs=[pl.BlockSpec((1, NBK, 1, 2 * BLK), lambda h: (h, 0, 0, 0))],
        out_specs=pl.BlockSpec((1, NBK, BLK, BLK), lambda h: (h, 0, 0, 0)),
        out_shape=jax.ShapeDtypeStruct((H, NBK, BLK, BLK), F32), name="bias_tiles")(base)


def make_base(trow):
    rows = []
    for d in range(NBK):
        lo = d * BLK
        a = trow[:, max(lo - BLK + 1, 0):lo + 1][:, ::-1]
        if d == 0:
            a = jnp.concatenate([a, jnp.zeros((H, BLK - 1), F32)], 1)
        b = trow[:, lo + 1:lo + BLK][:, ::-1]
        rows.append(jnp.concatenate([a, jnp.zeros((H, 1), F32), b], 1))
    return jnp.stack(rows, 1)[:, :, None, :]


ANY = pl.BlockSpec(memory_space=pl.ANY)
VM = pl.BlockSpec(memory_space=pltpu.VMEM)
DMA = pltpu.SemaphoreType.DMA
MESH = pl.DeviceIdType.MESH
NS, NZ, NCORE = 4, 4, 2
ND = NS * NZ * NCORE


def sds(shape, dt):
    return jax.ShapeDtypeStruct(shape, dt)


def hbm(shape, dt):
    return pltpu.HBM(shape, dt)


def params(mib, cid):
    if cid is None:
        return pltpu.CompilerParams(vmem_limit_bytes=mib << 20)
    return pltpu.CompilerParams(vmem_limit_bytes=mib << 20, collective_id=cid, has_side_effects=True)


def split(refs, n, *groups):
    out = list(refs[:n])
    for g in groups:
        out.append(refs[n:n + g])
        n += g
    return out


def place():
    s = lax.axis_index("seq")
    d = lax.axis_index("dp")
    return s, d // NCORE, d % NCORE


def flat(s, z, c):
    return (s * NZ + z) * NCORE + c


def partners(s, z, c):
    zs = [{"seq": s, "dp": ((z + k) % NZ) * NCORE + c} for k in (1, 2, 3)]
    ss = [{"seq": (s + k) % NS, "dp": z * NCORE + c} for k in (1, 2, 3)]
    return zs, ss, {"seq": s, "dp": z * NCORE + 1 - c}


def plane(s):
    return s + 1 - 2 * (s % 2), (s + 2) % NS, NS - 1 - s


def meet(devices):
    bar = pltpu.get_barrier_semaphore()
    for p in devices:
        pl.semaphore_signal(bar, inc=1, device_id=p, device_id_type=MESH)
    pl.semaphore_wait(bar, len(devices))


def meet_all():
    zs, ss, co = partners(*place())
    meet(zs + ss + [co])


def meet_seq():
    meet(partners(*place())[1])


def remote(src, dst, ssem, rsem, dev):
    return pltpu.make_async_remote_copy(src, dst, ssem, rsem, device_id=dev, device_id_type=MESH)


class Exchange:
    def __init__(self, src, dst, ss, rs, ls, part=(0, 1)):
        self.s, z, c = place()
        self.src, self.dst, self.ss, self.rs, self.ls = src, dst, ss, rs, ls
        n = src.shape[1] // part[1]
        self.rows = pl.ds(part[0] * n, n)
        self.to = partners(self.s, z, c)[1]

    @staticmethod
    def sems():
        return [DMA((3,)), DMA((3,)), DMA(())]

    def local(self):
        return pltpu.make_async_copy(self.src.at[self.s, self.rows], self.dst.at[self.s, self.rows], self.ls)

    def copy(self, k):
        return remote(self.src.at[(self.s + k) % NS, self.rows], self.dst.at[self.s, self.rows], self.ss.at[k - 1], self.rs.at[k - 1], self.to[k - 1])

    def start(self):
        for k in (2, 1, 3):
            self.copy(k).start()
        self.local().start()

    def end(self):
        for k in (1, 2, 3):
            self.copy(k).wait_recv()
            self.copy(k).wait_send()
        self.local().wait()


class Gather:
    def __init__(self, w, out, ssem, rsem, lsem):
        self.w, self.out, self.ssem, self.rsem, self.lsem = w, out, ssem, rsem, lsem
        self.s, self.z, self.c = place()
        self.zs, self.ss, self.co = partners(self.s, self.z, self.c)
        self.px, self.py, self.pd = plane(self.s)

    @staticmethod
    def sems():
        return [DMA((ND - 1,)), DMA((ND,)), DMA(())]

    def slot(self, i):
        return self.out.at[i]

    def at(self, s, kz, c):
        return flat(s, (self.z + NZ - kz) % NZ, c)

    def there(self, s):
        return {"seq": s, "dp": self.z * NCORE + self.c}

    def send(self, i, dev, n, src=None):
        remote(self.slot(i) if src is None else src, self.slot(i), self.ssem.at[n], self.rsem.at[i], dev).start()

    def got(self, i):
        remote(self.slot(i), self.slot(i), self.ssem.at[0], self.rsem.at[i], self.co).wait_recv()

    def local(self):
        return pltpu.make_async_copy(self.w, self.slot(self.at(self.s, 0, self.c)), self.lsem)

    def start(self):
        own = self.at(self.s, 0, self.c)
        for k in range(3):
            self.send(own, self.zs[k], k, self.w)
        self.send(own, self.there(self.px), 3, self.w)
        self.send(own, self.there(self.py), 4, self.w)
        self.send(own, self.co, 5, self.w)
        self.local().start()

    def line(self, k):
        i = self.at(self.s, k, self.c)
        self.got(i)
        self.send(i, self.there(self.px), 3 * k + 3)
        self.send(i, self.there(self.py), 3 * k + 4)
        self.send(i, self.co, 3 * k + 5)

    def hop(self, kz):
        for j, (a, b) in enumerate(((self.px, self.py), (self.py, self.px))):
            i = self.at(a, kz, self.c)
            self.got(i)
            if kz % 2 == j:
                self.send(i, self.there(b), 15 + kz)
            self.send(i, self.co, 19 + 3 * kz + j)

    def diag(self, kz):
        i = self.at(self.pd, kz, self.c)
        self.got(i)
        self.send(i, self.co, 21 + 3 * kz)

    def end(self):
        for kz in range(NZ):
            for k in range(NS):
                self.got(self.at((self.s + k) % NS, kz, 1 - self.c))
        for n in range(ND - 1):
            remote(self.w, self.slot(0), self.ssem.at[n], self.rsem.at[0], self.co).wait_send()
        self.local().wait()


class LineGather:
    def __init__(self, w, out, ss, rs, ls):
        self.w, self.out, self.ss, self.rs, self.ls = w, out, ss, rs, ls
        s, self.z, c = place()
        self.zs = partners(s, self.z, c)[0]

    @staticmethod
    def sems():
        return [DMA((3,)), DMA((3,)), DMA(())]

    def local(self):
        return pltpu.make_async_copy(self.w, self.out.at[self.z], self.ls)

    def copy(self, k):
        return remote(self.w, self.out.at[self.z], self.ss.at[k], self.rs.at[k], self.zs[k])

    def start(self):
        for k in range(3):
            self.copy(k).start()
        self.local().start()

    def end(self):
        for k in range(3):
            self.copy(k).wait_recv()
            self.copy(k).wait_send()
        self.local().wait()


class PlaneGather:
    def __init__(self, w, out, ss, rx, rd, rc, ls):
        self.w, self.out, self.ss, self.rx, self.rd, self.rc, self.ls = w, out, ss, rx, rd, rc, ls
        self.s, self.z, self.c = place()
        self.co = partners(self.s, self.z, self.c)[2]
        self.col = (self.s,) + plane(self.s)

    @staticmethod
    def sems():
        return [DMA((9,)), DMA((2,)), DMA((2,)), DMA((4,)), DMA(())]

    def at(self, a):
        return self.out.at[self.col[a], :, self.c]

    def half(self, a, j):
        return self.out.at[self.col[a], pl.ds(2 * j, 2), self.c]

    def to(self, a):
        return {"seq": self.col[a], "dp": self.z * NCORE + self.c}

    def local(self):
        return pltpu.make_async_copy(self.w, self.at(0), self.ls)

    def direct(self, a):
        return remote(self.w, self.at(0), self.ss.at[a], self.rx.at[a - 1], self.to(a))

    def core(self, a):
        return remote(self.at(a) if a else self.w, self.at(a), self.ss.at[5 + a], self.rc.at[a], self.co)

    def on(self, a):
        return remote(self.half(a, a - 1), self.half(a, a - 1), self.ss.at[2 + a], self.rd.at[a - 1], self.to(3 - a))

    def start(self):
        self.direct(1).start()
        self.direct(2).start()
        self.core(0).start()
        self.local().start()

    def hop(self):
        for a in (1, 2):
            self.direct(a).wait_recv()
            self.on(a).start()
            self.core(a).start()

    def diag(self):
        self.on(1).wait_recv()
        self.on(2).wait_recv()
        self.core(3).start()

    def end(self):
        for a in range(4):
            self.core(a).wait_recv()
            self.core(a).wait_send()
        for a in (1, 2):
            self.direct(a).wait_send()
            self.on(a).wait_send()
        self.local().wait()


class Scatter:
    def __init__(self, g, outs, mine, rc, rd, rn, rz, lsem, cs, cr, xs, ds, dr, nr, zsem, zr):
        self.g, self.outs = g, outs
        self.mine, self.rc, self.rd, self.rn, self.rz = mine, rc, rd, rn, rz
        self.lsem, self.cs, self.cr, self.xs, self.ds, self.dr, self.nr, self.zsem, self.zr = lsem, cs, cr, xs, ds, dr, nr, zsem, zr
        self.s, self.z, self.c = place()
        self.zs, self.ss, self.co = partners(self.s, self.z, self.c)
        self.col = (self.s,) + plane(self.s)

    @staticmethod
    def bufs(rows, cols):
        v = lambda *n: pltpu.VMEM(n + (rows, cols), BF)
        return [v(4, NZ), v(4, NZ), v(2, 2), v(2, NZ), v(3), DMA((4,)), DMA((4,)), DMA((4,)), DMA((2,)), DMA((2,)), DMA((2,)), DMA((2,)),
                DMA((3,)), DMA((3,))]

    def core(self, a):
        return remote(self.g.at[self.col[a], :, 1 - self.c], self.rc.at[a], self.cs.at[a], self.cr.at[a], self.co)

    def load(self, a):
        return pltpu.make_async_copy(self.g.at[self.col[a], :, self.c], self.mine.at[a], self.lsem.at[a])

    def to(self, a):
        return {"seq": self.col[a], "dp": self.z * NCORE + self.c}

    def via(self, a):
        return remote(self.mine.at[3, pl.ds(2 * (a - 1), 2)], self.rd.at[a - 1], self.ds.at[a - 1], self.dr.at[a - 1], self.to(a))

    def last(self, a):
        return remote(self.mine.at[a], self.rn.at[a - 1], self.xs.at[a - 1], self.nr.at[a - 1], self.to(a))

    def zz(self, k):
        return remote(self.mine.at[0, (self.z + k) % NZ], self.rz.at[k - 1], self.zsem.at[k - 1], self.zr.at[k - 1], self.zs[k - 1])

    def start(self, which):
        for a in which:
            self.core(a).start()
            self.load(a).start()

    def both(self, a, j, ready=True):
        if ready:
            self.load(a).wait()
            self.core(a).wait_recv()
        return None if j is None else self.mine[a, j].astype(F32) + self.rc[a, j].astype(F32)

    def away(self):
        self.both(3, None)
        for a in (1, 2):
            for j in range(2 * (a - 1), 2 * a):
                self.mine[3, j] = self.both(3, j, False).astype(BF)
            self.via(a).start()

    def near(self):
        for a in (1, 2):
            self.both(a, None)
            self.via(3 - a).wait_recv()
            for j in range(NZ):
                v = self.both(a, j, False)
                if j // 2 == 2 - a:
                    v = v + self.rd[2 - a, j % 2].astype(F32)
                self.mine[a, j] = v.astype(BF)
            self.last(a).start()

    def total(self, j):
        v = self.mine[0, j].astype(F32) + self.rc[0, j].astype(F32)
        return v + (self.rn[0, j].astype(F32) + self.rn[1, j].astype(F32))

    def come(self):
        self.both(0, None)
        self.last(1).wait_recv()
        self.last(2).wait_recv()

    def line(self):
        self.come()
        for k in (1, 2, 3):
            j = (self.z + k) % NZ
            self.mine[0, j] = self.total(j).astype(BF)
            self.zz(k).start()

    def sent(self):
        for a in range(4):
            self.core(a).wait_send()
        for a in (1, 2):
            self.via(a).wait_send()
            self.last(a).wait_send()

    def stop(self, out):
        self.come()
        for j in range(NZ):
            out[j] = self.total(j).astype(BF)
        self.sent()

    def end(self):
        v = self.total(self.z)
        for k in (1, 2, 3):
            self.zz(k).wait_recv()
            v = v + self.rz[k - 1].astype(F32)
        at = 0
        for o in self.outs:
            o[...] = v[:, at:at + o.shape[1]]
            at += o.shape[1]
        self.sent()
        for k in (1, 2, 3):
            self.zz(k).wait_send()


class LineScatter:
    def __init__(self, part, out, mine, rz, lsem, ss, rs):
        self.part, self.out, self.mine, self.rz, self.lsem, self.ss, self.rs = part, out, mine, rz, lsem, ss, rs
        s, self.z, c = place()
        self.zs = partners(s, self.z, c)[0]

    @staticmethod
    def bufs(rows, cols):
        return [pltpu.VMEM((rows, cols), BF), pltpu.VMEM((3, rows, cols), BF), DMA(()), DMA((3,)), DMA((3,))]

    def copy(self, k):
        return remote(self.part.at[(self.z + k + 1) % NZ], self.rz.at[k], self.ss.at[k], self.rs.at[k], self.zs[k])

    def local(self):
        return pltpu.make_async_copy(self.part.at[self.z], self.mine, self.lsem)

    def start(self):
        for k in range(3):
            self.copy(k).start()
        self.local().start()

    def end(self):
        self.local().wait()
        v = self.mine[...].astype(F32)
        for k in range(3):
            self.copy(k).wait_recv()
            v = v + self.rz[k].astype(F32)
        self.out[...] = v
        for k in range(3):
            self.copy(k).wait_send()


def weights_in_kernel(w_ref, wm_ref, x_ref, base_ref, out_ref, zm_ref, xo_ref, bias_h, ga, gb, gc, la, lb, lc, xa, xb, xc, ya, yb, yc, tile, tsem):
    gat = Gather(w_ref, out_ref, ga, gb, gc)
    lin = LineGather(wm_ref, zm_ref, la, lb, lc)
    exc = Exchange(x_ref, xo_ref, xa, xb, xc, (0, 2))
    rest = Exchange(x_ref, xo_ref, ya, yb, yc, (1, 2))
    meet_all()
    gat.start()
    exc.start()

    def flush(h):
        return pltpu.make_async_copy(tile.at[h % 2], bias_h.at[h], tsem.at[h % 2])

    def head(h, carry):
        @pl.when(h >= 2)
        def _():
            flush(h - 2).wait()

        bias_tiles(base_ref, h, tile.at[h % 2])
        flush(h).start()
        return carry

    lax.fori_loop(0, H, head, 0)
    gat.line(1)
    gat.hop(0)
    gat.line(2)
    gat.line(3)
    rest.start()
    lin.start()
    gat.diag(0)
    for kz in range(1, NZ):
        gat.hop(kz)
    for kz in range(1, NZ):
        gat.diag(kz)
    flush(H - 2).wait()
    flush(H - 1).wait()
    gat.end()
    exc.end()
    rest.end()
    lin.end()


def weights_in(w, wm, x, base, cid):
    return pl.pallas_call(
        weights_in_kernel, in_specs=[ANY, ANY, ANY, VM], out_specs=[ANY] * 4,
        out_shape=[hbm((ND,) + w.shape, w.dtype), hbm((NZ,) + wm.shape, w.dtype), hbm(x.shape, x.dtype), hbm((H, NBK, BLK, BLK), F32)],
        scratch_shapes=Gather.sems() + LineGather.sems() + Exchange.sems() * 2 + [pltpu.VMEM((2, NBK, BLK, BLK), F32), DMA((2,))],
        compiler_params=params(24, cid), name="weights_in")(w, wm, x, base)


def hsum(sel, v):
    return lax.dot_general(sel, v, (((1,), (1,)), ((), ())), precision=lax.Precision.HIGHEST, preferred_element_type=F32)


def grads_out_kernel(g, dgs, dgc, dgf, gpre, gpost, diag, bucket, gt, oq, ok, ov, o_gain, o_pre, o_post, o_tab, gt_o,
                     mc, mx, mz, ms, mr, small, e1, e2, e3, *bufs):
    sca = Scatter(g, [oq, ok, ov], *bufs)
    s, z, c = place()
    zs, ss, co = partners(s, z, c)
    exc = Exchange(gt, gt_o, e1, e2, e3)
    meet_all()
    sca.start((3, 2, 1, 0))
    nbk = o_tab.shape[1]
    small[...] = jnp.zeros_like(small)
    for i, d in enumerate((dgs, dgc, dgf)):
        v = jnp.sum(d[...], 0, keepdims=True)
        for j in range(D // 128):
            small[6 * i + j:6 * i + j + 1, :] = v[:, j * 128:(j + 1) * 128]
    sel = (lax.broadcasted_iota(jnp.int32, (H, D), 1) // DH == lax.broadcasted_iota(jnp.int32, (H, D), 0)).astype(F32)
    small[24:24 + H, :H] = hsum(sel, gpre[...])
    small[24:24 + H, 16:16 + H] = hsum(gpost[...], sel)
    tab = jnp.zeros((H, nbk), F32)
    for d in range(NBK):
        hot = (lax.broadcasted_iota(jnp.int32, (nbk, 2 * BLK), 0) == bucket[d:d + 1, :]).astype(F32)
        tab = tab + hsum(diag[:, d, 0, :], hot)
    small[24:24 + H, 32:32 + nbk] = tab
    first = remote(small, mc, ms.at[0], mr.at[0], co)
    first.start()
    sca.away()
    first.wait_recv()
    mx[s] = small[...] + mc[...]
    xy = [remote(mx.at[s], mx.at[s], ms.at[k], mr.at[k], ss[k - 1]) for k in (1, 2, 3)]
    for cp in xy:
        cp.start()
    sca.near()
    exc.start()
    for cp in xy:
        cp.wait_recv()
    mz[z] = (mx[0] + mx[1]) + (mx[2] + mx[3])
    zz = [remote(mz.at[z], mz.at[z], ms.at[3 + k], mr.at[3 + k], zs[k - 1]) for k in (1, 2, 3)]
    for cp in zz:
        cp.start()
    sca.line()
    for cp in zz:
        cp.wait_recv()
    v = (mz[0] + mz[1]) + (mz[2] + mz[3])
    o_pre[...] = v[24:24 + H, :H]
    o_post[...] = v[24:24 + H, 16:16 + H]
    o_tab[...] = v[24:24 + H, 32:32 + nbk]
    o_gain[...] = v[:24]
    exc.end()
    sca.end()
    for cp in [first] + xy + zz:
        cp.wait_send()


def grads_out(g, small, gt, nbk, cid):
    sm = (40, 128)
    rows = g.shape[3]
    return pl.pallas_call(
        grads_out_kernel,
        in_specs=[ANY] + [VM] * len(small) + [ANY], out_specs=[VM] * 7 + [ANY],
        out_shape=[sds((rows, D), F32)] * 3
        + [sds((24, 128), F32), sds((H, H), F32), sds((H, H), F32), sds((H, nbk), F32), sds(gt.shape, BF)],
        scratch_shapes=[pltpu.VMEM(sm, F32), pltpu.VMEM((4,) + sm, F32), pltpu.VMEM((4,) + sm, F32), DMA((7,)), DMA((7,)),
                        pltpu.VMEM(sm, F32)] + Exchange.sems() + Scatter.bufs(*g.shape[3:]),
        compiler_params=params(56, cid), name="grads_out")(g, *small, gt)


def finish_kernel(n, *refs):
    acts, plain, rf = refs[:3], refs[3:3 + n], refs[3 + n]
    o_acts, o_plain, o_fo, o_fi = refs[4 + n:7 + n], refs[7 + n:7 + 2 * n], refs[7 + 2 * n], refs[8 + 2 * n]
    for a, b in zip(acts, o_acts):
        b[...] = a[...].astype(b.dtype)

    @pl.when(pl.program_id(0) == 0)
    def _():
        for a, b in zip(plain, o_plain):
            b[...] = a[...]
        nf = o_fi.shape[0]
        for j in range(nf):
            o_fi[j] = rf[:, 2 * j * D:(2 * j + 1) * D]
            o_fo[:, j, :] = rf[:, (2 * j + 1) * D:(2 * j + 2) * D]


def finish(acts, plain, rf):
    rows = rf.shape[0]
    nf = rf.shape[1] // (2 * D)
    blk = pl.BlockSpec((1,) + acts[0].shape[1:], lambda i: (i, 0, 0))
    whole = [pl.BlockSpec(p.shape, lambda i: (0, 0)) for p in plain]
    return pl.pallas_call(
        functools.partial(finish_kernel, len(plain)), grid=(acts[0].shape[0],),
        in_specs=[blk] * 3 + whole + [pl.BlockSpec(rf.shape, lambda i: (0, 0))],
        out_specs=[blk] * 3 + whole + [pl.BlockSpec((rows, nf, D), lambda i: (0, 0, 0)), pl.BlockSpec((nf, rows, D), lambda i: (0, 0, 0))],
        out_shape=[sds(a.shape, t) for a, t in zip(acts, (BF, F32, F32))] + [sds(p.shape, F32) for p in plain]
        + [sds((rows, nf, D), F32), sds((nf, rows, D), F32)],
        name="finish")(*acts, *plain, rf)


EPS = 1e-6
GATE = 0.7978845608028654


def cst(shape):
    return pl.BlockSpec(shape, lambda *a: (0,) * len(shape), pipeline_mode=pl.Buffered(1))


def col(shape, j):
    return pl.BlockSpec(shape, lambda *a: (0, j), pipeline_mode=pl.Buffered(1))


def each(f):
    def step(i, carry):
        f(pl.ds(pl.multiple_of(i * BLK, BLK), BLK))
        return carry

    lax.fori_loop(0, NBK, step, 0)


def rows8(v):
    return jnp.sum(v.reshape(v.shape[0] // 8, 8, v.shape[1]), 0)


def norm(x, g):
    return x * lax.rsqrt(jnp.mean(x * x, -1, keepdims=True) + EPS) * g


def norm_grad(x, g, dn):
    r = lax.rsqrt(jnp.mean(x * x, -1, keepdims=True) + EPS)
    gd = g * dn
    dx = r * gd - x * (r * r * r) * jnp.mean(gd * x, -1, keepdims=True)
    return dx, rows8(dn * x * r)


def gelu_pair(x):
    x2 = x * x
    t = jnp.tanh(x * (GATE + GATE * 0.044715 * x2))
    hp = 0.5 + 0.5 * t
    y = x * hp
    d = hp + 0.5 * x * (1.0 - t * t) * (GATE + 3 * GATE * 0.044715 * x2)
    return y, d


def blocks(n=NBK):
    return [slice(i * BLK, (i + 1) * BLK) for i in range(n)]


FWD_PLAN = ((3, "exc", 0), (4, "hop", 0), (5, "exc", 1), (8, "diag", 0))
CROSS_PLAN = ((4, "hop"),)


def self_fwd_kernel(near, st_ref, x_ref, w_ref, gn_ref, bias_ref, pre_ref, post_ref, *refs):
    if near:
        (zm_h, wf_h, enc_h, cot_h, q_ref, k_ref, v_ref, att_ref, gain_ref, mpre_ref, mpost_ref, p_ref, wo_h, zf_h, eo_h, co_h, acc_ref, lo_ref,
         ags, lgs, ex1, ex2) = split(refs, 18, 5, 3, 3, 3)
        gat = PlaneGather(zm_h, wo_h, *ags)
        lin = LineGather(wf_h, zf_h, *lgs)
        exc = [Exchange(enc_h, eo_h, *ex1), Exchange(cot_h, co_h, *ex2)]
    else:
        q_ref, k_ref, v_ref, att_ref, gain_ref, mpre_ref, mpost_ref, p_ref, acc_ref, lo_ref = refs
    h = pl.program_id(0)

    if near:
        @pl.when(h == 0)
        def _():
            meet_all()
            gat.start()
            lin.start()

        for hh, name, k in FWD_PLAN:
            @pl.when(h == hh)
            def _(name=name, k=k):
                if name == "exc":
                    exc[k].start()
                else:
                    getattr(gat, name)()

    @pl.when(h == 0)
    def _():
        acc_ref[...] = jnp.zeros_like(acc_ref)
        gt = gn_ref[...].astype(F32).T
        gain_ref[...] = gt[:8]
        g = gt[:1]

        def project(r):
            n1 = norm(x_ref[r, :].astype(F32), g).astype(BF)
            for j, o in enumerate((q_ref, k_ref, v_ref)):
                o[r, :] = dot(n1, w_ref[:, j * D:(j + 1) * D], 1, 0).astype(BF)

        each(project)
        pos = lax.broadcasted_iota(jnp.int32, (L, 128), 0)
        lo = jnp.zeros((L, 128), jnp.int32)
        me = lax.axis_index("seq")
        for d in range(1, st_ref.shape[1]):
            sd = st_ref[me, d]
            lo = jnp.where(pos >= sd, sd, lo)
        lo_ref[...] = lo
        sel = (lax.broadcasted_iota(jnp.int32, (H, D), 1) // DH == lax.broadcasted_iota(jnp.int32, (H, D), 0)).astype(F32)
        wide = lambda m, k: lax.dot_general(m[...], sel, (((k,), (0,)), ((), ())), precision=lax.Precision.HIGHEST,
                                            preferred_element_type=F32)
        mpre_ref[...] = wide(pre_ref, 0)
        mpost_ref[...] = wide(post_ref, 1)

    mp = mpre_ref[pl.ds(h, 1), :]
    mo = mpost_ref[pl.ds(h, 1), :]

    def scores(i):
        n = (i + 1) * BLK
        qm = (q_ref[i * BLK:n, :].astype(F32) * mp).astype(BF)
        return dot(qm, k_ref[:n, :], 1, 1)

    sc = scores(NBK - 1)
    for i in reversed(range(NBK)):
        nxt = scores(i - 1) if i else None
        n = (i + 1) * BLK
        r = slice(i * BLK, n)
        bias = jnp.concatenate([bias_ref[0, i - j] for j in range(i + 1)], 1) if i else bias_ref[0, 0]
        c = lax.broadcasted_iota(jnp.int32, (BLK, n), 1)
        sc = jnp.where(c >= lo_ref[r, :1], sc + bias, NEG)
        e = jnp.exp(sc - jnp.max(sc, 1, keepdims=True))
        p = (e * (1.0 / jnp.sum(e, 1, keepdims=True))).astype(BF)
        p_ref[0, r, :n] = p
        acc_ref[r, :] += dot(p, v_ref[:n, :], 1, 0) * mo
        sc = nxt

    @pl.when(h == H - 1)
    def _():
        att_ref[...] = acc_ref[...].astype(BF)
        if near:
            lin.end()
            gat.end()
            for e in exc:
                e.end()


def self_fwd(starts, x, w1, bias, mpre, mpost, far=None, cid=None):
    one = cst((L, D))
    near = far is not None
    extra_out = []
    if near:
        extra_out = [sds((NS, NZ, NCORE) + far[0].shape[1:], BF), sds((NZ,) + far[1].shape, BF)] + [sds(f.shape, BF) for f in far[2:]]
    return pl.pallas_call(
        functools.partial(self_fwd_kernel, near),
        grid_spec=pltpu.PrefetchScalarGridSpec(
            num_scalar_prefetch=1, grid=(H,),
            in_specs=[one, col((D, 3 * D), 0), col((D, 128), 18),
                      pl.BlockSpec((1, NBK, BLK, BLK), lambda h, st: (h, 0, 0, 0)), cst((H, H)), cst((H, H))]
            + [ANY] * (4 * near),
            out_specs=[one] * 4 + [cst((8, D)), cst((H, D)), cst((H, D)), pl.BlockSpec((1, L, L), lambda h, st: (h, 0, 0))] + [ANY] * (4 * near),
            scratch_shapes=[pltpu.VMEM((L, D), F32), pltpu.VMEM((L, 128), jnp.int32)]
            + (PlaneGather.sems() + LineGather.sems() + Exchange.sems() * 2 if near else [])),
        out_shape=[sds((L, D), BF)] * 4 + [sds((8, D), F32), sds((H, D), F32), sds((H, D), F32), sds((H, L, L), BF)] + extra_out,
        compiler_params=params(62, cid),
        cost_estimate=pl.CostEstimate(flops=52_000_000_000, bytes_accessed=45_000_000, transcendentals=8_000_000),
        name="self_fwd")(starts, x, w1, w1, bias, mpre, mpost, *(far or ()))


def cross_fwd_kernel(near, x_ref, att_ref, wo_ref, wq_ref, wk_ref, wv_ref, enc_ref, gain_ref, *refs):
    if near:
        zf_h, h1_ref, n2_ref, q_ref, k_ref, v_ref, catt_ref, p_ref, fo_h, ags = split(refs, 9, 5)
        gat = PlaneGather(zf_h, fo_h, *ags)
    else:
        h1_ref, n2_ref, q_ref, k_ref, v_ref, catt_ref, p_ref = refs
    h = pl.program_id(0)

    if near:
        @pl.when(h == 0)
        def _():
            meet_all()
            gat.start()

        for hh, name in CROSS_PLAN:
            @pl.when(h == hh)
            def _(name=name):
                getattr(gat, name)()

    @pl.when(h == 0)
    def _():
        g = gain_ref[1:2, :]

        def project(r):
            h1 = x_ref[r, :].astype(F32) + dot(att_ref[r, :], wo_ref[...], 1, 0)
            h1_ref[r, :] = h1
            n2 = norm(h1, g).astype(BF)
            n2_ref[r, :] = n2
            q_ref[r, :] = dot(n2, wq_ref[...], 1, 0).astype(BF)
            k_ref[r, :] = dot(enc_ref[r, :], wk_ref[...], 1, 0).astype(BF)
            v_ref[r, :] = dot(enc_ref[r, :], wv_ref[...], 1, 0).astype(BF)

        each(project)

    cols = pl.ds(pl.multiple_of(h * 128, 128), 128)
    first = lax.broadcasted_iota(jnp.int32, (1, 128), 1) < DH
    k = k_ref[:, cols]
    v = v_ref[:, cols]
    steps = [(r, e) for r in blocks() for e in range(2)]

    def scores(r, e):
        q = q_ref[r, cols]
        return dot(jnp.where(first if e == 0 else ~first, q, jnp.zeros_like(q)), k, 1, 1)

    sc = scores(*steps[0])
    keep = None
    for n, (r, e) in enumerate(steps):
        nxt = scores(*steps[n + 1]) if n + 1 < len(steps) else None
        ex = jnp.exp(sc - jnp.max(sc, 1, keepdims=True))
        p = (ex * (1.0 / jnp.sum(ex, 1, keepdims=True))).astype(BF)
        p_ref[e, r, :] = p
        o = dot(p, v, 1, 0)
        if e == 0:
            keep = o
        else:
            catt_ref[r, cols] = jnp.where(first, keep, o).astype(BF)
        sc = nxt

    if near:
        @pl.when(h == H // 2 - 1)
        def _():
            gat.diag()
            gat.end()


def cross_fwd(x, att, wmid, enc, gains, far=None, cid=None):
    one = cst((L, D))
    near = far is not None
    return pl.pallas_call(
        functools.partial(cross_fwd_kernel, near), grid=(H // 2,),
        in_specs=[one, one] + [col((D, D), j) for j in range(4)] + [one, cst((8, D))] + [ANY] * near,
        out_specs=[one] * 6 + [pl.BlockSpec((2, L, L), lambda h: (h, 0, 0))] + [ANY] * near,
        out_shape=[sds((L, D), F32)] + [sds((L, D), BF)] * 5 + [sds((H, L, L), BF)]
        + ([sds((NS, NZ, NCORE) + far.shape[1:], BF)] if near else []),
        scratch_shapes=PlaneGather.sems() if near else [],
        compiler_params=params(62, cid),
        cost_estimate=pl.CostEstimate(flops=31_000_000_000, bytes_accessed=50_000_000, transcendentals=12_000_000),
        name="cross_fwd")(x, att, wmid, wmid, wmid, wmid, enc, gains, *([far] if near else []))


def feed_kernel(h1_ref, catt_ref, wco_ref, cot_ref, gain_ref, fi_ref, fo_ref,
                out_ref, bh2_ref, bca_ref, gw_ref, dg_ref,
                n3, n3t, cott, acc, dn, inner, bi):
    a = pl.program_id(0)
    g = gain_ref[2:3, :]

    @pl.when(a == 0)
    def _():

        def enter(r):
            h2 = h1_ref[r, :] + dot(catt_ref[r, :], wco_ref[...], 1, 0)
            bh2_ref[r, :] = h2
            acc[r, :] = h2
            n3[r, :] = norm(h2, g).astype(BF)

        each(enter)
        n3t[...] = n3[...].T
        cott[...] = cot_ref[...].T
        dn[...] = jnp.zeros_like(dn)

    for r in blocks():
        u = dot(n3[r, :], fi_ref[...], 1, 0)
        y, d = gelu_pair(u)
        y = y.astype(BF)
        inner[r, :] = y
        gy = dot(cot_ref[r, :], fo_ref[...], 1, 1)
        b = (gy * d).astype(BF)
        bi[r, :] = b
        acc[r, :] += dot(y, fo_ref[...], 1, 0)
        dn[r, :] += dot(b, fi_ref[...], 1, 1)
    gw_ref[:, :D] = dot(n3t[...], bi[...], 1, 0).astype(BF)
    gw_ref[:, D:] = dot(cott[...], inner[...], 1, 0).T.astype(BF)

    @pl.when(a == pl.num_programs(0) - 1)
    def _():
        dg_ref[...] = jnp.zeros_like(dg_ref)

        def leave(r):
            out_ref[r, :] = acc[r, :].astype(BF)
            dx, s = norm_grad(bh2_ref[r, :], g, dn[r, :])
            dg_ref[...] += s
            b2 = cot_ref[r, :].astype(F32) + dx
            bh2_ref[r, :] = b2
            bca_ref[r, :] = dot(b2.astype(BF), wco_ref[...], 1, 1).astype(BF)

        each(leave)


def feed(h1, catt, wmid, cot, gains, wfeed):
    one = cst((L, D))
    nf = wfeed.shape[1] // (2 * D)
    return pl.pallas_call(
        feed_kernel, grid=(nf,),
        in_specs=[one, one, col((D, D), 4), one, cst((8, D)),
                  pl.BlockSpec((D, D), lambda a: (0, 2 * a)), pl.BlockSpec((D, D), lambda a: (0, 2 * a + 1))],
        out_specs=[one, one, one, pl.BlockSpec((D, 2 * D), lambda a: (0, a)), cst((8, D))],
        out_shape=[sds((L, D), BF), sds((L, D), F32), sds((L, D), BF), sds((D, wfeed.shape[1]), BF), sds((8, D), F32)],
        scratch_shapes=[pltpu.VMEM((L, D), BF), pltpu.VMEM((D, L), BF), pltpu.VMEM((D, L), BF), pltpu.VMEM((L, D), F32),
                        pltpu.VMEM((L, D), F32), pltpu.VMEM((L, D), BF), pltpu.VMEM((L, D), BF)],
        compiler_params=pltpu.CompilerParams(vmem_limit_bytes=62 << 20),
        cost_estimate=pl.CostEstimate(flops=32_000_000_000, bytes_accessed=50_000_000, transcendentals=3_000_000),
        name="feed")(h1, catt, wmid, cot, gains, wfeed, wfeed)


def cross_bwd_kernel(near, q_ref, k_ref, v_ref, do_ref, p_ref, gain_ref, n2_h, enc_h, att_h, catt_h, h1_h, bh2_h, w_h, *refs):
    if near:
        gf_h = refs[0]
        gw_ref, genc_ref, bh1_ref, bat_ref, dg_ref, rf_ref = refs[1:7]
        qt, dot_, ds, dq, dk, dv, n2, enc, att, catt, h1, w, sems, sca = split(refs[7:], 13, len(Scatter.bufs(8, D)))
        sca = Scatter(gf_h, [], *sca)
    else:
        gw_ref, genc_ref, bh1_ref, bat_ref, dg_ref = refs[:5]
        qt, dot_, ds, dq, dk, dv, n2, enc, att, catt, h1, w, sems = refs[5:]
    h = pl.program_id(0)
    late = [(n2_h, n2), (enc_h, enc), (att_h, att), (catt_h, catt), (h1_h, h1), (bh2_h, bh1_ref)]
    late += [(w_h.at[:, pl.ds(0, 4 * D)], w)]
    copies = [pltpu.make_async_copy(a, b, sems.at[i]) for i, (a, b) in enumerate(late)]

    @pl.when(h == 0)
    def _():
        if near:
            meet_all()
            sca.start((3,))

    @pl.when(h == 3)
    def _():
        for c in copies:
            c.start()

    if near:
        for hh, name, *more in BWD_PLAN:
            @pl.when(h == hh)
            def _(name=name, more=more):
                getattr(sca, name)(*more)

    e = h % 2
    cols = pl.ds(pl.multiple_of((h // 2) * 128, 128), 128)
    fe = (lax.broadcasted_iota(jnp.int32, (1, 128), 1) // DH) == e
    k = k_ref[...]
    v = v_ref[...]

    @pl.when(e == 0)
    def _():
        qt[...] = q_ref[...].T
        dot_[...] = do_ref[...].T

    for r in blocks():
        do = do_ref[r, :]
        dp = dot(jnp.where(fe, do, jnp.zeros_like(do)), v, 1, 1)
        p = p_ref[0, r, :].astype(F32)
        d = (p * (dp - jnp.sum(dp * p, 1, keepdims=True))).astype(BF)
        ds[r, :] = d
        dq[r, cols] = jnp.where(fe, dot(d, k, 1, 0).astype(BF), dq[r, cols])
    x = dot(dot_[...], p_ref[0], 1, 0).T.astype(BF)
    dv[:, cols] = jnp.where(fe, x, dv[:, cols])
    x = dot(qt[...], ds[...], 1, 0).T.astype(BF)
    dk[:, cols] = jnp.where(fe, x, dk[:, cols])

    @pl.when(h == H - 1)
    def _():
        for c in copies:
            c.wait()
        g = gain_ref[1:2, :]
        dg_ref[...] = jnp.zeros_like(dg_ref)
        gw_ref[:, D:2 * D] = dot(n2[...], dq[...], 0, 0).astype(BF)
        gw_ref[:, 2 * D:3 * D] = dot(enc[...], dk[...], 0, 0).astype(BF)
        gw_ref[:, 3 * D:4 * D] = dot(enc[...], dv[...], 0, 0).astype(BF)

        def leave(r):
            genc_ref[r, :] = (dot(dk[r, :], w[:, 2 * D:3 * D], 1, 1) + dot(dv[r, :], w[:, 3 * D:], 1, 1)).astype(genc_ref.dtype)
            dx, s = norm_grad(h1[r, :], g, dot(dq[r, :], w[:, D:2 * D], 1, 1))
            dg_ref[...] += s
            b2 = bh1_ref[r, :]
            b1 = b2 + dx
            bh1_ref[r, :] = b1
            b1 = b1.astype(BF)
            n2[r, :] = b1
            enc[r, :] = b2.astype(BF)
            bat_ref[r, :] = dot(b1, w[:, :D], 1, 1).astype(BF)

        each(leave)
        gw_ref[:, :D] = dot(att[...], n2[...], 0, 0).astype(BF)
        gw_ref[:, 4 * D:] = dot(catt[...], enc[...], 0, 0).astype(BF)
        if near:
            sca.stop(rf_ref)


BWD_PLAN = ((2, "away"), (2, "start", (2, 1)), (3, "start", (0,)), (6, "near"))


def cross_bwd(q, k, v, do, p, gains, n2, enc, att, catt, h1, bh2, wmid, far=None, cid=None):
    one = cst((L, D))
    near = far is not None
    pair = pl.BlockSpec((L, 128), lambda h: (0, h // 2))
    act = pltpu.VMEM((L, D), BF)
    more = [(NZ,) + far.shape[3:]] if near else []
    return pl.pallas_call(
        functools.partial(cross_bwd_kernel, near), grid=(H,),
        in_specs=[pair] * 4 + [pl.BlockSpec((1, L, L), lambda h: (h, 0, 0)), cst((8, D))] + [ANY] * (7 + near),
        out_specs=[cst((D, 5 * D)), one, one, one, cst((8, D))] + [cst(s) for s in more],
        out_shape=[sds((D, 5 * D), BF), sds((L, D), BF), sds((L, D), F32), sds((L, D), BF), sds((8, D), F32)]
        + [sds(s, BF) for s in more],
        scratch_shapes=[pltpu.VMEM((128, L), BF)] * 2 + [pltpu.VMEM((L, L), BF)] + [act] * 7
        + [pltpu.VMEM((L, D), F32), pltpu.VMEM((D, 4 * D), BF), DMA((7,))] + sum([Scatter.bufs(*s[1:]) for s in more], []),
        compiler_params=params(62, cid),
        cost_estimate=pl.CostEstimate(flops=37_000_000_000, bytes_accessed=70_000_000, transcendentals=0),
        name="cross_bwd")(q, k, v, do, p, gains, n2, enc, att, catt, h1, bh2, wmid, *([far] if near else []))


SELF_PLAN = ((1, "away"), (1, "start", (2, 1, 0)), (3, "near"), (3, "exc", 0), (6, "exc", 1), (8, "line"))


def self_bwd_kernel(near, q_ref, k_ref, v_ref, ba_ref, p_ref, mpre_ref, mpost_ref, gain_ref, x_h, bh1_h, w_h, *refs):
    if near:
        gm_h, zf_h, out_h, ge_h = refs[:4]
        gw_ref, gtok_ref, gpre_ref, gpost_ref, diag_ref, dg_ref = refs[4:10]
        rms, (rf_ref, oo_h, go_h) = refs[10:15], refs[15:18]
        qt, bat, dqa, dkt, dvt, dm, x, bh1, w, sems, sca, lin, ex1, ex2 = split(refs[18:], 10, len(Scatter.bufs(8, D)), 5, 3, 3)
        lin = LineScatter(zf_h, rf_ref, *lin)
        sca = Scatter(gm_h, rms, *sca)
        exc = [Exchange(out_h, oo_h, *ex1), Exchange(ge_h, go_h, *ex2)]
    else:
        gw_ref, gtok_ref, gpre_ref, gpost_ref, diag_ref, dg_ref = refs[:6]
        qt, bat, dqa, dkt, dvt, dm, x, bh1, w, sems = refs[6:]
    h = pl.program_id(0)

    if near:
        @pl.when(h == 0)
        def _():
            meet_all()
            sca.start((3,))
            lin.start()

        for hh, name, *more in SELF_PLAN:
            @pl.when(h == hh)
            def _(name=name, more=more):
                if name == "exc":
                    exc[more[0]].start()
                else:
                    getattr(sca, name)(*more)

    late = [(x_h, x), (bh1_h, bh1), (w_h.at[:, pl.ds(0, 3 * D)], w)]
    copies = [pltpu.make_async_copy(a, b, sems.at[i]) for i, (a, b) in enumerate(late)]

    @pl.when(h == 0)
    def _():
        for c in copies:
            c.start()
        qt[...] = q_ref[...].T
        bat[...] = ba_ref[...].T
        dqa[...] = jnp.zeros_like(dqa)
        dkt[...] = jnp.zeros_like(dkt)
        dvt[...] = jnp.zeros_like(dvt)

    mp = mpre_ref[pl.ds(h, 1), :]
    mo = mpost_ref[pl.ds(h, 1), :]
    gp = jnp.zeros((8, D), F32)
    dacc = [None] * NBK
    for i, r in enumerate(blocks()):
        n = (i + 1) * BLK
        bam = (ba_ref[r, :].astype(F32) * mo).astype(BF)
        dp = dot(bam, v_ref[:n, :], 1, 1)
        p = p_ref[0, r, :n].astype(F32)
        d = p * (dp - jnp.sum(dp * p, 1, keepdims=True))
        for j in range(i + 1):
            t = d[:, j * BLK:(j + 1) * BLK]
            dacc[i - j] = t if dacc[i - j] is None else dacc[i - j] + t
        db = d.astype(BF)
        dm[r, :n] = db
        rr = dot(db, k_ref[:n, :], 1, 0)
        dqa[r, :] += rr * mp
        gp = gp + rows8(rr * q_ref[r, :].astype(F32))
    gpre_ref[pl.ds(h, 1), :] = jnp.sum(gp, 0, keepdims=True)
    for t in range(NBK):
        y = jnp.concatenate([jnp.zeros((BLK, BLK), F32), dacc[t]], 1)
        n = BLK // 2
        while n >= 1:
            y = y[:n] + pltpu.roll(y[n:], 2 * BLK - n, 1)
            n //= 2
        diag_ref[0, t] = y
    mpc = jnp.broadcast_to(mp, (8, D)).T[:, :1]
    moc = jnp.broadcast_to(mo, (8, D)).T[:, :1]
    gq = jnp.zeros((8, D), F32)
    for c in blocks():
        i0 = c.start
        t = dot(bat[:, i0:], p_ref[0, i0:, c], 1, 0)
        dvt[:, c] += t * moc
        gq = gq + rows8(t.T * v_ref[c, :].astype(F32))
        u = dot(qt[:, i0:], dm[i0:, c], 1, 0)
        dkt[:, c] += u * mpc
    gpost_ref[pl.ds(h, 1), :] = jnp.sum(gq, 0, keepdims=True)

    @pl.when(h == H - 1)
    def _():
        for c in copies:
            c.wait()
        g = gain_ref[:1, :]
        dg_ref[...] = jnp.zeros_like(dg_ref)

        def leave(r):
            xr = x[r, :].astype(F32)
            n1 = norm(xr, g).astype(BF)
            dk = dkt[:, r].T.astype(BF)
            dv = dvt[:, r].T.astype(BF)
            dq = dqa[r, :].astype(BF)
            bat[:, r] = n1.T
            dm[r, :D] = dq
            dqa[r, :] = dk.astype(F32)
            back = dot(dq, w[:, :D], 1, 1) + dot(dk, w[:, D:2 * D], 1, 1) + dot(dv, w[:, 2 * D:], 1, 1)
            dx, s = norm_grad(xr, g, back)
            dg_ref[...] += s
            gtok_ref[r, :] = (bh1[r, :] + dx).astype(gtok_ref.dtype)

        each(leave)
        gw_ref[:, :D] = dot(bat[...], dm[:, :D], 1, 0).astype(BF)
        gw_ref[:, D:2 * D] = dot(bat[...], dqa[...].astype(BF), 1, 0).astype(BF)
        gw_ref[:, 2 * D:] = dot(bat[...], dvt[...].astype(BF), 1, 1).astype(BF)
        if near:
            lin.end()
            sca.end()
            for e in exc:
                e.end()


def self_bwd(q, k, v, ba, p, mpre, mpost, gains, x, bh1, w1, far=None, cid=None):
    one = cst((L, D))
    near = far is not None
    rows = far[0].shape[3] if near else 0
    more = [cst((rows, D))] * 5 + [cst(far[1].shape[1:]), ANY, ANY] if near else []
    more_out = []
    if near:
        more_out = [sds((rows, D), F32)] * 5 + [sds(far[1].shape[1:], F32)] + [sds(f.shape, BF) for f in far[2:]]
    return pl.pallas_call(
        functools.partial(self_bwd_kernel, near), grid=(H,),
        in_specs=[one] * 4 + [pl.BlockSpec((1, L, L), lambda h: (h, 0, 0)), cst((H, D)), cst((H, D)), cst((8, D))] + [ANY] * (3 + 4 * near),
        out_specs=[cst((D, 3 * D))] + [one, cst((H, D)), cst((H, D)),
                   pl.BlockSpec((1, NBK, 1, 2 * BLK), lambda h: (h, 0, 0, 0)), cst((8, D))] + more,
        out_shape=[sds((D, 3 * D), BF)] + [sds((L, D), BF), sds((H, D), F32), sds((H, D), F32),
                   sds((H, NBK, 1, 2 * BLK), F32), sds((8, D), F32)] + more_out,
        scratch_shapes=[pltpu.VMEM((D, L), BF)] * 2 + [pltpu.VMEM((L, D), F32)] + [pltpu.VMEM((D, L), F32)] * 2
        + [pltpu.VMEM((L, L), BF), pltpu.VMEM((L, D), BF), pltpu.VMEM((L, D), F32), pltpu.VMEM((D, 3 * D), BF), DMA((3,))]
        + (Scatter.bufs(*far[0].shape[3:]) + LineScatter.bufs(*far[1].shape[1:]) + Exchange.sems() * 2 if near else []),
        compiler_params=params(62, cid),
        cost_estimate=pl.CostEstimate(flops=128_000_000_000, bytes_accessed=50_000_000, transcendentals=0),
        name="self_bwd")(q, k, v, ba, p, mpre, mpost, gains, x, bh1, w1, *(far or ()))


AX = ("seq", "dp")


def gather(w):
    return lax.all_gather(w, AX, axis=0, tiled=True)


def scatter(g):
    return lax.psum_scatter(g, AX, scatter_dimension=0, tiled=True).astype(F32)


def per_device(tokens, encoded, cotangent, doc_starts, rel_bucket, sq, sk, sv, so, cq, ck, cv, co, fi, fo,
               gs, gc, gf, mix_pre, mix_post, rel_table):
    nseq, ndp = lax.axis_size("seq"), lax.axis_size("dp")
    rows = sq.shape[0]
    nf = fo.shape[0] // rows
    ndev = nseq * ndp
    buckets = rel_table.shape[0]
    near = nseq == NS and ndp == NZ * NCORE and rows % 8 == 0
    to_stream = lambda x: lax.all_to_all(x, "seq", 0, 1, tiled=True).reshape(L, D)
    from_stream = lambda x: lax.all_to_all(x.reshape(1, L, D), "seq", 1, 0, tiled=True)
    hot = (rel_bucket[:, None] == jnp.arange(buckets)[None, :]).astype(F32)
    trow = lax.dot_general(rel_table, hot, (((0,), (1,)), ((), ())), precision=lax.Precision.HIGHEST)
    base = make_base(trow)
    gains = jnp.pad(jnp.stack([gs, gc, gf], 1), ((0, 0), (0, 125)))
    w1 = jnp.concatenate([sq, sk, sv, gains], 1)
    wmid = jnp.concatenate([so, cq, ck, cv, co], 1)
    wfeed = jnp.stack([fi.reshape(rows, D, nf).transpose(0, 2, 1), fo.reshape(rows, nf, D)], 2).reshape(rows, 2 * nf * D)
    if near:
        w1, zmid, x, bias = weights_in(w1, wmid, tokens, base, 1)
        w1 = w1.reshape(D, -1)
        x = x.reshape(L, D)
    else:
        w1 = gather(w1)
        x = to_stream(tokens)
        bias = toeplitz(base)
        wmid = gather(wmid)
        wfeed = gather(wfeed)
        enc = to_stream(encoded)
        cot = to_stream(cotangent)
    if near:
        q, k, v, att, gain, mpre, mpost, p, wmid, zfeed, enc, cot = self_fwd(doc_starts, x, w1, bias, mix_pre, mix_post, (zmid, wfeed, encoded, cotangent), 2)
        wmid = wmid.reshape(D, -1)
        enc = enc.reshape(L, D)
        h1, n2, cqx, ckx, cvx, catt, cp, wfeed = cross_fwd(x, att, wmid, enc, gain, zfeed, 3)
        cot = cot.reshape(L, D)
        wfeed = wfeed.reshape(D, -1)
    else:
        q, k, v, att, gain, mpre, mpost, p = self_fwd(doc_starts, x, w1, bias, mix_pre, mix_post)
        h1, n2, cqx, ckx, cvx, catt, cp = cross_fwd(x, att, wmid, enc, gain)
    out, bh2, bca, gw_feed, dgf = feed(h1, catt, wmid, cot, gain, wfeed)
    by_dev = lambda a: a.reshape(NS, NZ, NCORE, rows, -1)
    back = (cqx, ckx, cvx, bca, cp, gain, n2, enc, att, catt, h1, bh2, wmid)
    if near:
        gw_mid, g_enc, bh1, bat, dgc, zfeed = cross_bwd(*back, by_dev(gw_feed), 6)
    else:
        gw_mid, g_enc, bh1, bat, dgc = cross_bwd(*back)
        r_feed = scatter(gw_feed)
    blk = lambda a: a.reshape(nseq, L // nseq, D)
    if near:
        far = (by_dev(gw_mid), zfeed, blk(out), blk(g_enc))
        gw_qkv, g_tok, gpre, gpost, diag, dgs, *r_mid, r_feed, out, g_enc = self_bwd(
            q, k, v, bat, p, mpre, mpost, gain, x, bh1, w1, far, 4)
    else:
        gw_qkv, g_tok, gpre, gpost, diag, dgs = self_bwd(q, k, v, bat, p, mpre, mpost, gain, x, bh1, w1)
    if near:
        pad = jnp.pad(rel_bucket[::-1], (BLK, BLK), constant_values=-1)
        bucket = jnp.stack([lax.slice(pad, (L + BLK - 1 - (d * BLK + BLK),), (L + BLK - 1 - (d * BLK + BLK) + 2 * BLK,))
                            for d in range(NBK)])
        r_q, r_k, r_v, dgain, gpre, gpost, gtab, g_tok = grads_out(
            by_dev(gw_qkv), [dgs, dgc, dgf, gpre, gpost, diag, bucket], blk(g_tok), buckets, 5)
        out, g_tok, g_enc, *plain, g_fo, g_fi = finish([out, g_tok, g_enc], [r_q, r_k, r_v, *r_mid, dgain, gpre, gpost, gtab], r_feed)
        r_q, r_k, r_v = plain[:3]
        r_mid, (dgain, gpre, gpost, gtab) = plain[3:8], plain[8:]
        gtab = gtab.T
        dgain = dgain[:18].reshape(3, D)
    else:
        gpre = gpre.reshape(H, H, DH).sum(-1).T
        gpost = gpost.reshape(H, H, DH).sum(-1)
        dg = diag[:, :, 0, ::-1]
        gt = 0.0
        for d in range(NBK):
            gt = gt + jnp.pad(dg[:, d], ((0, 0), (d * BLK + 1, L - d * BLK - 1)))
        gt = gt[:, BLK:BLK + L]
        gtab = lax.dot_general(hot, gt, (((0,), (1,)), ((), ())), precision=lax.Precision.HIGHEST)
        dgain = jnp.stack([dgs.sum(0), dgc.sum(0), dgf.sum(0)])
        r_mid = jnp.split(scatter(gw_mid), 5, 1)
        r_q, r_k, r_v = jnp.split(scatter(gw_qkv), 3, 1)
        out, g_tok, g_enc = from_stream(out), from_stream(g_tok).astype(F32), from_stream(g_enc).astype(F32)
        dgain, gpre, gpost, gtab = lax.psum((dgain, gpre, gpost, gtab), AX)
        r_feed = r_feed.reshape(rows, nf, 2, D)
        g_fi, g_fo = r_feed[:, :, 0].transpose(1, 0, 2), r_feed[:, :, 1].reshape(rows * nf, D)
    g_fi = g_fi.transpose(1, 2, 0).reshape(rows, nf * D)
    g_fo = g_fo.reshape(rows * nf, D)
    me = lax.axis_index("seq") * ndp + lax.axis_index("dp")
    dgain = lax.dynamic_slice_in_dim(dgain, me * rows, rows, 1)
    return (out, g_tok, g_enc,
            r_q, r_k, r_v, *r_mid,
            g_fi, g_fo,
            dgain[0], dgain[1], dgain[2], gpre, gpost, gtab)


def solution(mesh):
    act = P("dp", "seq", None)
    w = P(AX, None)
    g = P(AX)
    return jax.shard_map(
        per_device, mesh=mesh, in_specs=(act, act, act, P("dp", None), P()) + (w,) * 10 + (g,) * 3 + (P(),) * 3,
        out_specs=(act,) * 3 + (w,) * 10 + (g,) * 3 + (P(),) * 3, check_vma=False)
```

```python
import functools

import jax
import jax.numpy as jnp
from jax import lax
from jax.experimental import pallas as pl
from jax.experimental.pallas import tpu as pltpu
from jax.sharding import PartitionSpec as P

F32 = jnp.float32
BF = jnp.bfloat16
NEG = -1e30
H, DH, D, L = 12, 64, 768, 1024
BLK = 256
NBK = L // BLK


def dot(a, b, ca, cb):
    return lax.dot_general(a, b, (((ca,), (cb,)), ((), ())), preferred_element_type=F32)


def bias_tiles(base_ref, h, out_ref):
    for d in range(NBK):
        row = jnp.broadcast_to(base_ref[h, d], (BLK, 2 * BLK))
        t = pltpu.roll(row, 0, 1, stride=1, stride_axis=0)[:, :BLK]
        if d == 0:
            a = lax.broadcasted_iota(jnp.int32, (BLK, BLK), 0)
            b = lax.broadcasted_iota(jnp.int32, (BLK, BLK), 1)
            t = jnp.where(a >= b, t, NEG)
        out_ref[d] = t


def toeplitz(base):
    def kernel(base_ref, out_ref):
        bias_tiles(base_ref, 0, out_ref.at[0])

    return pl.pallas_call(
        kernel, grid=(H,), in_specs=[pl.BlockSpec((1, NBK, 1, 2 * BLK), lambda h: (h, 0, 0, 0))],
        out_specs=pl.BlockSpec((1, NBK, BLK, BLK), lambda h: (h, 0, 0, 0)),
        out_shape=jax.ShapeDtypeStruct((H, NBK, BLK, BLK), F32), name="bias_tiles")(base)


def make_base(trow):
    rows = []
    for d in range(NBK):
        lo = d * BLK
        a = trow[:, max(lo - BLK + 1, 0):lo + 1][:, ::-1]
        if d == 0:
            a = jnp.concatenate([a, jnp.zeros((H, BLK - 1), F32)], 1)
        b = trow[:, lo + 1:lo + BLK][:, ::-1]
        rows.append(jnp.concatenate([a, jnp.zeros((H, 1), F32), b], 1))
    return jnp.stack(rows, 1)[:, :, None, :]


ANY = pl.BlockSpec(memory_space=pl.ANY)
VM = pl.BlockSpec(memory_space=pltpu.VMEM)
DMA = pltpu.SemaphoreType.DMA
MESH = pl.DeviceIdType.MESH
NS, NZ, NCORE = 4, 4, 2
ND = NS * NZ * NCORE


def sds(shape, dt):
    return jax.ShapeDtypeStruct(shape, dt)


def hbm(shape, dt):
    return pltpu.HBM(shape, dt)


def params(mib, cid):
    if cid is None:
        return pltpu.CompilerParams(vmem_limit_bytes=mib << 20)
    return pltpu.CompilerParams(vmem_limit_bytes=mib << 20, collective_id=cid, has_side_effects=True)


def split(refs, n, *groups):
    out = list(refs[:n])
    for g in groups:
        out.append(refs[n:n + g])
        n += g
    return out


def place():
    s = lax.axis_index("seq")
    d = lax.axis_index("dp")
    return s, d // NCORE, d % NCORE


def flat(s, z, c):
    return (s * NZ + z) * NCORE + c


def partners(s, z, c):
    zs = [{"seq": s, "dp": ((z + k) % NZ) * NCORE + c} for k in (1, 2, 3)]
    ss = [{"seq": (s + k) % NS, "dp": z * NCORE + c} for k in (1, 2, 3)]
    return zs, ss, {"seq": s, "dp": z * NCORE + 1 - c}


def plane(s):
    return s + 1 - 2 * (s % 2), (s + 2) % NS, NS - 1 - s


def meet(devices):
    bar = pltpu.get_barrier_semaphore()
    for p in devices:
        pl.semaphore_signal(bar, inc=1, device_id=p, device_id_type=MESH)
    pl.semaphore_wait(bar, len(devices))


def meet_all():
    zs, ss, co = partners(*place())
    meet(zs + ss + [co])


def meet_seq():
    meet(partners(*place())[1])


def remote(src, dst, ssem, rsem, dev):
    return pltpu.make_async_remote_copy(src, dst, ssem, rsem, device_id=dev, device_id_type=MESH)


class Exchange:
    def __init__(self, src, dst, ss, rs, ls, part=(0, 1)):
        self.s, z, c = place()
        self.src, self.dst, self.ss, self.rs, self.ls = src, dst, ss, rs, ls
        n = src.shape[1] // part[1]
        self.rows = pl.ds(part[0] * n, n)
        self.to = partners(self.s, z, c)[1]

    @staticmethod
    def sems():
        return [DMA((3,)), DMA((3,)), DMA(())]

    def local(self):
        return pltpu.make_async_copy(self.src.at[self.s, self.rows], self.dst.at[self.s, self.rows], self.ls)

    def copy(self, k):
        return remote(self.src.at[(self.s + k) % NS, self.rows], self.dst.at[self.s, self.rows], self.ss.at[k - 1], self.rs.at[k - 1], self.to[k - 1])

    def start(self):
        for k in (2, 1, 3):
            self.copy(k).start()
        self.local().start()

    def end(self):
        for k in (1, 2, 3):
            self.copy(k).wait_recv()
            self.copy(k).wait_send()
        self.local().wait()


class Gather:
    def __init__(self, w, out, ssem, rsem, lsem):
        self.w, self.out, self.ssem, self.rsem, self.lsem = w, out, ssem, rsem, lsem
        self.s, self.z, self.c = place()
        self.zs, self.ss, self.co = partners(self.s, self.z, self.c)
        self.px, self.py, self.pd = plane(self.s)

    @staticmethod
    def sems():
        return [DMA((ND - 1,)), DMA((ND,)), DMA(())]

    def slot(self, i):
        return self.out.at[i]

    def at(self, s, kz, c):
        return flat(s, (self.z + NZ - kz) % NZ, c)

    def there(self, s):
        return {"seq": s, "dp": self.z * NCORE + self.c}

    def send(self, i, dev, n, src=None):
        remote(self.slot(i) if src is None else src, self.slot(i), self.ssem.at[n], self.rsem.at[i], dev).start()

    def got(self, i):
        remote(self.slot(i), self.slot(i), self.ssem.at[0], self.rsem.at[i], self.co).wait_recv()

    def local(self):
        return pltpu.make_async_copy(self.w, self.slot(self.at(self.s, 0, self.c)), self.lsem)

    def start(self):
        own = self.at(self.s, 0, self.c)
        for k in range(3):
            self.send(own, self.zs[k], k, self.w)
        self.send(own, self.there(self.px), 3, self.w)
        self.send(own, self.there(self.py), 4, self.w)
        self.send(own, self.co, 5, self.w)
        self.local().start()

    def line(self, k):
        i = self.at(self.s, k, self.c)
        self.got(i)
        self.send(i, self.there(self.px), 3 * k + 3)
        self.send(i, self.there(self.py), 3 * k + 4)
        self.send(i, self.co, 3 * k + 5)

    def hop(self, kz):
        for j, (a, b) in enumerate(((self.px, self.py), (self.py, self.px))):
            i = self.at(a, kz, self.c)
            self.got(i)
            if kz % 2 == j:
                self.send(i, self.there(b), 15 + kz)
            self.send(i, self.co, 19 + 3 * kz + j)

    def diag(self, kz):
        i = self.at(self.pd, kz, self.c)
        self.got(i)
        self.send(i, self.co, 21 + 3 * kz)

    def end(self):
        for kz in range(NZ):
            for k in range(NS):
                self.got(self.at((self.s + k) % NS, kz, 1 - self.c))
        for n in range(ND - 1):
            remote(self.w, self.slot(0), self.ssem.at[n], self.rsem.at[0], self.co).wait_send()
        self.local().wait()


class LineGather:
    def __init__(self, w, out, ss, rs, ls):
        self.w, self.out, self.ss, self.rs, self.ls = w, out, ss, rs, ls
        s, self.z, c = place()
        self.zs = partners(s, self.z, c)[0]

    @staticmethod
    def sems():
        return [DMA((3,)), DMA((3,)), DMA(())]

    def local(self):
        return pltpu.make_async_copy(self.w, self.out.at[self.z], self.ls)

    def copy(self, k):
        return remote(self.w, self.out.at[self.z], self.ss.at[k], self.rs.at[k], self.zs[k])

    def start(self):
        for k in range(3):
            self.copy(k).start()
        self.local().start()

    def end(self):
        for k in range(3):
            self.copy(k).wait_recv()
            self.copy(k).wait_send()
        self.local().wait()


class PlaneGather:
    def __init__(self, w, out, ss, rx, rd, rc, ls):
        self.w, self.out, self.ss, self.rx, self.rd, self.rc, self.ls = w, out, ss, rx, rd, rc, ls
        self.s, self.z, self.c = place()
        self.co = partners(self.s, self.z, self.c)[2]
        self.col = (self.s,) + plane(self.s)

    @staticmethod
    def sems():
        return [DMA((9,)), DMA((2,)), DMA((2,)), DMA((4,)), DMA(())]

    def at(self, a):
        return self.out.at[self.col[a], :, self.c]

    def half(self, a, j):
        return self.out.at[self.col[a], pl.ds(2 * j, 2), self.c]

    def to(self, a):
        return {"seq": self.col[a], "dp": self.z * NCORE + self.c}

    def local(self):
        return pltpu.make_async_copy(self.w, self.at(0), self.ls)

    def direct(self, a):
        return remote(self.w, self.at(0), self.ss.at[a], self.rx.at[a - 1], self.to(a))

    def core(self, a):
        return remote(self.at(a) if a else self.w, self.at(a), self.ss.at[5 + a], self.rc.at[a], self.co)

    def on(self, a):
        return remote(self.half(a, a - 1), self.half(a, a - 1), self.ss.at[2 + a], self.rd.at[a - 1], self.to(3 - a))

    def start(self):
        self.direct(1).start()
        self.direct(2).start()
        self.core(0).start()
        self.local().start()

    def hop(self):
        for a in (1, 2):
            self.direct(a).wait_recv()
            self.on(a).start()
            self.core(a).start()

    def diag(self):
        self.on(1).wait_recv()
        self.on(2).wait_recv()
        self.core(3).start()

    def end(self):
        for a in range(4):
            self.core(a).wait_recv()
            self.core(a).wait_send()
        for a in (1, 2):
            self.direct(a).wait_send()
            self.on(a).wait_send()
        self.local().wait()


class Scatter:
    def __init__(self, g, outs, mine, rc, rd, rn, rz, lsem, cs, cr, xs, ds, dr, nr, zsem, zr):
        self.g, self.outs = g, outs
        self.mine, self.rc, self.rd, self.rn, self.rz = mine, rc, rd, rn, rz
        self.lsem, self.cs, self.cr, self.xs, self.ds, self.dr, self.nr, self.zsem, self.zr = lsem, cs, cr, xs, ds, dr, nr, zsem, zr
        self.s, self.z, self.c = place()
        self.zs, self.ss, self.co = partners(self.s, self.z, self.c)
        self.col = (self.s,) + plane(self.s)

    @staticmethod
    def bufs(rows, cols):
        v = lambda *n: pltpu.VMEM(n + (rows, cols), BF)
        return [v(4, NZ), v(4, NZ), v(2, 2), v(2, NZ), v(3), DMA((4,)), DMA((4,)), DMA((4,)), DMA((2,)), DMA((2,)), DMA((2,)), DMA((2,)),
                DMA((3,)), DMA((3,))]

    def core(self, a):
        return remote(self.g.at[self.col[a], :, 1 - self.c], self.rc.at[a], self.cs.at[a], self.cr.at[a], self.co)

    def load(self, a):
        return pltpu.make_async_copy(self.g.at[self.col[a], :, self.c], self.mine.at[a], self.lsem.at[a])

    def to(self, a):
        return {"seq": self.col[a], "dp": self.z * NCORE + self.c}

    def via(self, a):
        return remote(self.mine.at[3, pl.ds(2 * (a - 1), 2)], self.rd.at[a - 1], self.ds.at[a - 1], self.dr.at[a - 1], self.to(a))

    def last(self, a):
        return remote(self.mine.at[a], self.rn.at[a - 1], self.xs.at[a - 1], self.nr.at[a - 1], self.to(a))

    def zz(self, k):
        return remote(self.mine.at[0, (self.z + k) % NZ], self.rz.at[k - 1], self.zsem.at[k - 1], self.zr.at[k - 1], self.zs[k - 1])

    def start(self, which):
        for a in which:
            self.core(a).start()
            self.load(a).start()

    def both(self, a, j, ready=True):
        if ready:
            self.load(a).wait()
            self.core(a).wait_recv()
        return None if j is None else self.mine[a, j].astype(F32) + self.rc[a, j].astype(F32)

    def away(self):
        self.both(3, None)
        for a in (1, 2):
            for j in range(2 * (a - 1), 2 * a):
                self.mine[3, j] = self.both(3, j, False).astype(BF)
            self.via(a).start()

    def near(self):
        for a in (1, 2):
            self.both(a, None)
            self.via(3 - a).wait_recv()
            for j in range(NZ):
                v = self.both(a, j, False)
                if j // 2 == 2 - a:
                    v = v + self.rd[2 - a, j % 2].astype(F32)
                self.mine[a, j] = v.astype(BF)
            self.last(a).start()

    def total(self, j):
        v = self.mine[0, j].astype(F32) + self.rc[0, j].astype(F32)
        return v + (self.rn[0, j].astype(F32) + self.rn[1, j].astype(F32))

    def come(self):
        self.both(0, None)
        self.last(1).wait_recv()
        self.last(2).wait_recv()

    def line(self):
        self.come()
        for k in (1, 2, 3):
            j = (self.z + k) % NZ
            self.mine[0, j] = self.total(j).astype(BF)
            self.zz(k).start()

    def sent(self):
        for a in range(4):
            self.core(a).wait_send()
        for a in (1, 2):
            self.via(a).wait_send()
            self.last(a).wait_send()

    def stop(self, out):
        self.come()
        for j in range(NZ):
            out[j] = self.total(j).astype(BF)
        self.sent()

    def end(self):
        v = self.total(self.z)
        for k in (1, 2, 3):
            self.zz(k).wait_recv()
            v = v + self.rz[k - 1].astype(F32)
        at = 0
        for o in self.outs:
            o[...] = v[:, at:at + o.shape[1]]
            at += o.shape[1]
        self.sent()
        for k in (1, 2, 3):
            self.zz(k).wait_send()


class LineScatter:
    def __init__(self, part, out, mine, rz, lsem, ss, rs):
        self.part, self.out, self.mine, self.rz, self.lsem, self.ss, self.rs = part, out, mine, rz, lsem, ss, rs
        s, self.z, c = place()
        self.zs = partners(s, self.z, c)[0]

    @staticmethod
    def bufs(rows, cols):
        return [pltpu.VMEM((rows, cols), BF), pltpu.VMEM((3, rows, cols), BF), DMA(()), DMA((3,)), DMA((3,))]

    def copy(self, k):
        return remote(self.part.at[(self.z + k + 1) % NZ], self.rz.at[k], self.ss.at[k], self.rs.at[k], self.zs[k])

    def local(self):
        return pltpu.make_async_copy(self.part.at[self.z], self.mine, self.lsem)

    def start(self):
        for k in range(3):
            self.copy(k).start()
        self.local().start()

    def end(self):
        self.local().wait()
        v = self.mine[...].astype(F32)
        for k in range(3):
            self.copy(k).wait_recv()
            v = v + self.rz[k].astype(F32)
        self.out[...] = v
        for k in range(3):
            self.copy(k).wait_send()


def weights_in_kernel(w_ref, wm_ref, x_ref, base_ref, out_ref, zm_ref, xo_ref, bias_h, ga, gb, gc, la, lb, lc, xa, xb, xc, ya, yb, yc, tile, tsem):
    gat = Gather(w_ref, out_ref, ga, gb, gc)
    lin = LineGather(wm_ref, zm_ref, la, lb, lc)
    exc = Exchange(x_ref, xo_ref, xa, xb, xc, (0, 2))
    rest = Exchange(x_ref, xo_ref, ya, yb, yc, (1, 2))
    meet_all()
    gat.start()
    exc.start()

    def flush(h):
        return pltpu.make_async_copy(tile.at[h % 2], bias_h.at[h], tsem.at[h % 2])

    def head(h, carry):
        @pl.when(h >= 2)
        def _():
            flush(h - 2).wait()

        bias_tiles(base_ref, h, tile.at[h % 2])
        flush(h).start()
        return carry

    lax.fori_loop(0, H, head, 0)
    gat.line(1)
    gat.hop(0)
    gat.line(2)
    gat.line(3)
    rest.start()
    lin.start()
    gat.diag(0)
    for kz in range(1, NZ):
        gat.hop(kz)
    for kz in range(1, NZ):
        gat.diag(kz)
    flush(H - 2).wait()
    flush(H - 1).wait()
    gat.end()
    exc.end()
    rest.end()
    lin.end()


def weights_in(w, wm, x, base, cid):
    return pl.pallas_call(
        weights_in_kernel, in_specs=[ANY, ANY, ANY, VM], out_specs=[ANY] * 4,
        out_shape=[hbm((ND,) + w.shape, w.dtype), hbm((NZ,) + wm.shape, w.dtype), hbm(x.shape, x.dtype), hbm((H, NBK, BLK, BLK), F32)],
        scratch_shapes=Gather.sems() + LineGather.sems() + Exchange.sems() * 2 + [pltpu.VMEM((2, NBK, BLK, BLK), F32), DMA((2,))],
        compiler_params=params(24, cid), name="weights_in")(w, wm, x, base)


def hsum(sel, v):
    return lax.dot_general(sel, v, (((1,), (1,)), ((), ())), precision=lax.Precision.HIGHEST, preferred_element_type=F32)


def grads_out_kernel(g, dgs, dgc, dgf, gpre, gpost, diag, bucket, gt, oq, ok, ov, o_gain, o_pre, o_post, o_tab, gt_o,
                     mc, mx, mz, ms, mr, small, e1, e2, e3, r1, r2, r3, *bufs):
    sca = Scatter(g, [oq, ok, ov], *bufs)
    s, z, c = place()
    zs, ss, co = partners(s, z, c)
    exc = Exchange(gt, gt_o, e1, e2, e3, (0, 2))
    rest = Exchange(gt, gt_o, r1, r2, r3, (1, 2))
    meet_all()
    sca.start((3,))
    exc.start()
    sca.start((2, 1, 0))
    nbk = o_tab.shape[1]
    small[...] = jnp.zeros_like(small)
    for i, d in enumerate((dgs, dgc, dgf)):
        v = jnp.sum(d[...], 0, keepdims=True)
        for j in range(D // 128):
            small[6 * i + j:6 * i + j + 1, :] = v[:, j * 128:(j + 1) * 128]
    sel = (lax.broadcasted_iota(jnp.int32, (H, D), 1) // DH == lax.broadcasted_iota(jnp.int32, (H, D), 0)).astype(F32)
    small[24:24 + H, :H] = hsum(sel, gpre[...])
    small[24:24 + H, 16:16 + H] = hsum(gpost[...], sel)
    tab = jnp.zeros((H, nbk), F32)
    for d in range(NBK):
        hot = (lax.broadcasted_iota(jnp.int32, (nbk, 2 * BLK), 0) == bucket[d:d + 1, :]).astype(F32)
        tab = tab + hsum(diag[:, d, 0, :], hot)
    small[24:24 + H, 32:32 + nbk] = tab
    first = remote(small, mc, ms.at[0], mr.at[0], co)
    first.start()
    sca.away()
    first.wait_recv()
    mx[s] = small[...] + mc[...]
    xy = [remote(mx.at[s], mx.at[s], ms.at[k], mr.at[k], ss[k - 1]) for k in (1, 2, 3)]
    for cp in xy:
        cp.start()
    sca.near()
    rest.start()
    for cp in xy:
        cp.wait_recv()
    mz[z] = (mx[0] + mx[1]) + (mx[2] + mx[3])
    zz = [remote(mz.at[z], mz.at[z], ms.at[3 + k], mr.at[3 + k], zs[k - 1]) for k in (1, 2, 3)]
    for cp in zz:
        cp.start()
    sca.line()
    for cp in zz:
        cp.wait_recv()
    v = (mz[0] + mz[1]) + (mz[2] + mz[3])
    o_pre[...] = v[24:24 + H, :H]
    o_post[...] = v[24:24 + H, 16:16 + H]
    o_tab[...] = v[24:24 + H, 32:32 + nbk]
    o_gain[...] = v[:24]
    exc.end()
    rest.end()
    sca.end()
    for cp in [first] + xy + zz:
        cp.wait_send()


def grads_out(g, small, gt, nbk, cid):
    sm = (40, 128)
    rows = g.shape[3]
    return pl.pallas_call(
        grads_out_kernel,
        in_specs=[ANY] + [VM] * len(small) + [ANY], out_specs=[VM] * 7 + [ANY],
        out_shape=[sds((rows, D), F32)] * 3
        + [sds((24, 128), F32), sds((H, H), F32), sds((H, H), F32), sds((H, nbk), F32), sds(gt.shape, BF)],
        scratch_shapes=[pltpu.VMEM(sm, F32), pltpu.VMEM((4,) + sm, F32), pltpu.VMEM((4,) + sm, F32), DMA((7,)), DMA((7,)),
                        pltpu.VMEM(sm, F32)] + Exchange.sems() * 2 + Scatter.bufs(*g.shape[3:]),
        compiler_params=params(56, cid), name="grads_out")(g, *small, gt)


def finish_kernel(n, *refs):
    acts, plain, rf = refs[:3], refs[3:3 + n], refs[3 + n]
    o_acts, o_plain, o_fo, o_fi = refs[4 + n:7 + n], refs[7 + n:7 + 2 * n], refs[7 + 2 * n], refs[8 + 2 * n]
    for a, b in zip(acts, o_acts):
        b[...] = a[...].astype(b.dtype)

    @pl.when(pl.program_id(0) == 0)
    def _():
        for a, b in zip(plain, o_plain):
            b[...] = a[...]
        nf = o_fi.shape[0]
        for j in range(nf):
            o_fi[j] = rf[:, 2 * j * D:(2 * j + 1) * D]
            o_fo[:, j, :] = rf[:, (2 * j + 1) * D:(2 * j + 2) * D]


def finish(acts, plain, rf):
    rows = rf.shape[0]
    nf = rf.shape[1] // (2 * D)
    blk = pl.BlockSpec((1,) + acts[0].shape[1:], lambda i: (i, 0, 0))
    whole = [pl.BlockSpec(p.shape, lambda i: (0, 0)) for p in plain]
    return pl.pallas_call(
        functools.partial(finish_kernel, len(plain)), grid=(acts[0].shape[0],),
        in_specs=[blk] * 3 + whole + [pl.BlockSpec(rf.shape, lambda i: (0, 0))],
        out_specs=[blk] * 3 + whole + [pl.BlockSpec((rows, nf, D), lambda i: (0, 0, 0)), pl.BlockSpec((nf, rows, D), lambda i: (0, 0, 0))],
        out_shape=[sds(a.shape, t) for a, t in zip(acts, (BF, F32, F32))] + [sds(p.shape, F32) for p in plain]
        + [sds((rows, nf, D), F32), sds((nf, rows, D), F32)],
        name="finish")(*acts, *plain, rf)


EPS = 1e-6
GATE = 0.7978845608028654


def cst(shape):
    return pl.BlockSpec(shape, lambda *a: (0,) * len(shape), pipeline_mode=pl.Buffered(1))


def col(shape, j):
    return pl.BlockSpec(shape, lambda *a: (0, j), pipeline_mode=pl.Buffered(1))


def each(f, unroll=1):
    def step(i, carry):
        f(pl.ds(pl.multiple_of(i * BLK, BLK), BLK))
        return carry

    lax.fori_loop(0, NBK, step, 0, unroll=unroll)


def rows8(v):
    return jnp.sum(v.reshape(v.shape[0] // 8, 8, v.shape[1]), 0)


def norm(x, g):
    return x * lax.rsqrt(jnp.mean(x * x, -1, keepdims=True) + EPS) * g


def norm_grad(x, g, dn):
    r = lax.rsqrt(jnp.mean(x * x, -1, keepdims=True) + EPS)
    gd = g * dn
    dx = r * gd - x * (r * r * r) * jnp.mean(gd * x, -1, keepdims=True)
    return dx, rows8(dn * x * r)


def gelu_pair(x):
    x2 = x * x
    t = jnp.tanh(x * (GATE + GATE * 0.044715 * x2))
    hp = 0.5 + 0.5 * t
    y = x * hp
    d = hp + 0.5 * x * (1.0 - t * t) * (GATE + 3 * GATE * 0.044715 * x2)
    return y, d


def blocks(n=NBK):
    return [slice(i * BLK, (i + 1) * BLK) for i in range(n)]


FWD_PLAN = ((3, "exc", 0), (4, "hop", 0), (5, "exc", 1), (8, "diag", 0))
CROSS_PLAN = ((4, "hop"),)


def self_fwd_kernel(near, st_ref, x_ref, w_ref, gn_ref, bias_ref, pre_ref, post_ref, *refs):
    if near:
        (zm_h, wf_h, enc_h, cot_h, q_ref, k_ref, v_ref, att_ref, gain_ref, mpre_ref, mpost_ref, p_ref, wo_h, zf_h, eo_h, co_h, acc_ref, lo_ref,
         ags, lgs, ex1, ex2) = split(refs, 18, 5, 3, 3, 3)
        gat = PlaneGather(zm_h, wo_h, *ags)
        lin = LineGather(wf_h, zf_h, *lgs)
        exc = [Exchange(enc_h, eo_h, *ex1), Exchange(cot_h, co_h, *ex2)]
    else:
        q_ref, k_ref, v_ref, att_ref, gain_ref, mpre_ref, mpost_ref, p_ref, acc_ref, lo_ref = refs
    h = pl.program_id(0)

    if near:
        @pl.when(h == 0)
        def _():
            meet_all()
            gat.start()
            lin.start()

        for hh, name, k in FWD_PLAN:
            @pl.when(h == hh)
            def _(name=name, k=k):
                if name == "exc":
                    exc[k].start()
                else:
                    getattr(gat, name)()

    @pl.when(h == 0)
    def _():
        acc_ref[...] = jnp.zeros_like(acc_ref)
        gt = gn_ref[...].astype(F32).T
        gain_ref[...] = gt[:8]
        g = gt[:1]

        def project(r):
            n1 = norm(x_ref[r, :].astype(F32), g).astype(BF)
            for j, o in enumerate((q_ref, k_ref, v_ref)):
                o[r, :] = dot(n1, w_ref[:, j * D:(j + 1) * D], 1, 0).astype(BF)

        each(project)
        pos = lax.broadcasted_iota(jnp.int32, (L, 128), 0)
        lo = jnp.zeros((L, 128), jnp.int32)
        me = lax.axis_index("seq")
        for d in range(1, st_ref.shape[1]):
            sd = st_ref[me, d]
            lo = jnp.where(pos >= sd, sd, lo)
        lo_ref[...] = lo
        sel = (lax.broadcasted_iota(jnp.int32, (H, D), 1) // DH == lax.broadcasted_iota(jnp.int32, (H, D), 0)).astype(F32)
        wide = lambda m, k: lax.dot_general(m[...], sel, (((k,), (0,)), ((), ())), precision=lax.Precision.HIGHEST,
                                            preferred_element_type=F32)
        mpre_ref[...] = wide(pre_ref, 0)
        mpost_ref[...] = wide(post_ref, 1)

    mp = mpre_ref[pl.ds(h, 1), :]
    mo = mpost_ref[pl.ds(h, 1), :]

    def scores(i):
        n = (i + 1) * BLK
        qm = (q_ref[i * BLK:n, :].astype(F32) * mp).astype(BF)
        return dot(qm, k_ref[:n, :], 1, 1)

    sc = scores(NBK - 1)
    for i in reversed(range(NBK)):
        nxt = scores(i - 1) if i else None
        n = (i + 1) * BLK
        r = slice(i * BLK, n)
        bias = jnp.concatenate([bias_ref[0, i - j] for j in range(i + 1)], 1) if i else bias_ref[0, 0]
        c = lax.broadcasted_iota(jnp.int32, (BLK, n), 1)
        sc = jnp.where(c >= lo_ref[r, :1], sc + bias, NEG)
        e = jnp.exp(sc - jnp.max(sc, 1, keepdims=True))
        p = (e * (1.0 / jnp.sum(e, 1, keepdims=True))).astype(BF)
        p_ref[0, r, :n] = p
        acc_ref[r, :] += dot(p, v_ref[:n, :], 1, 0) * mo
        sc = nxt

    @pl.when(h == H - 1)
    def _():
        att_ref[...] = acc_ref[...].astype(BF)
        if near:
            lin.end()
            gat.end()
            for e in exc:
                e.end()


def self_fwd(starts, x, w1, bias, mpre, mpost, far=None, cid=None):
    one = cst((L, D))
    near = far is not None
    extra_out = []
    if near:
        extra_out = [sds((NS, NZ, NCORE) + far[0].shape[1:], BF), sds((NZ,) + far[1].shape, BF)] + [sds(f.shape, BF) for f in far[2:]]
    return pl.pallas_call(
        functools.partial(self_fwd_kernel, near),
        grid_spec=pltpu.PrefetchScalarGridSpec(
            num_scalar_prefetch=1, grid=(H,),
            in_specs=[one, col((D, 3 * D), 0), col((D, 128), 18),
                      pl.BlockSpec((1, NBK, BLK, BLK), lambda h, st: (h, 0, 0, 0)), cst((H, H)), cst((H, H))]
            + [ANY] * (4 * near),
            out_specs=[one] * 4 + [cst((8, D)), cst((H, D)), cst((H, D)), pl.BlockSpec((1, L, L), lambda h, st: (h, 0, 0))] + [ANY] * (4 * near),
            scratch_shapes=[pltpu.VMEM((L, D), F32), pltpu.VMEM((L, 128), jnp.int32)]
            + (PlaneGather.sems() + LineGather.sems() + Exchange.sems() * 2 if near else [])),
        out_shape=[sds((L, D), BF)] * 4 + [sds((8, D), F32), sds((H, D), F32), sds((H, D), F32), sds((H, L, L), BF)] + extra_out,
        compiler_params=params(62, cid),
        cost_estimate=pl.CostEstimate(flops=52_000_000_000, bytes_accessed=45_000_000, transcendentals=8_000_000),
        name="self_fwd")(starts, x, w1, w1, bias, mpre, mpost, *(far or ()))


def cross_fwd_kernel(near, x_ref, att_ref, wo_ref, wq_ref, wk_ref, wv_ref, enc_ref, gain_ref, *refs):
    if near:
        zf_h, h1_ref, n2_ref, q_ref, k_ref, v_ref, catt_ref, p_ref, fo_h, ags = split(refs, 9, 5)
        gat = PlaneGather(zf_h, fo_h, *ags)
    else:
        h1_ref, n2_ref, q_ref, k_ref, v_ref, catt_ref, p_ref = refs
    h = pl.program_id(0)

    if near:
        @pl.when(h == 0)
        def _():
            meet_all()
            gat.start()

        for hh, name in CROSS_PLAN:
            @pl.when(h == hh)
            def _(name=name):
                getattr(gat, name)()

    @pl.when(h == 0)
    def _():
        g = gain_ref[1:2, :]

        def project(r):
            h1 = x_ref[r, :].astype(F32) + dot(att_ref[r, :], wo_ref[...], 1, 0)
            h1_ref[r, :] = h1
            n2 = norm(h1, g).astype(BF)
            n2_ref[r, :] = n2
            q_ref[r, :] = dot(n2, wq_ref[...], 1, 0).astype(BF)
            k_ref[r, :] = dot(enc_ref[r, :], wk_ref[...], 1, 0).astype(BF)
            v_ref[r, :] = dot(enc_ref[r, :], wv_ref[...], 1, 0).astype(BF)

        each(project, 2)

    cols = pl.ds(pl.multiple_of(h * 128, 128), 128)
    first = lax.broadcasted_iota(jnp.int32, (1, 128), 1) < DH
    k = k_ref[:, cols]
    v = v_ref[:, cols]
    steps = [(r, e) for r in blocks() for e in range(2)]

    def scores(r, e):
        q = q_ref[r, cols]
        return dot(jnp.where(first if e == 0 else ~first, q, jnp.zeros_like(q)), k, 1, 1)

    sc = scores(*steps[0])
    keep = None
    for n, (r, e) in enumerate(steps):
        nxt = scores(*steps[n + 1]) if n + 1 < len(steps) else None
        ex = jnp.exp(sc - jnp.max(sc, 1, keepdims=True))
        p = (ex * (1.0 / jnp.sum(ex, 1, keepdims=True))).astype(BF)
        p_ref[e, r, :] = p
        o = dot(p, v, 1, 0)
        if e == 0:
            keep = o
        else:
            catt_ref[r, cols] = jnp.where(first, keep, o).astype(BF)
        sc = nxt

    if near:
        @pl.when(h == H // 2 - 1)
        def _():
            gat.diag()
            gat.end()


def cross_fwd(x, att, wmid, enc, gains, far=None, cid=None):
    one = cst((L, D))
    near = far is not None
    return pl.pallas_call(
        functools.partial(cross_fwd_kernel, near), grid=(H // 2,),
        in_specs=[one, one] + [col((D, D), j) for j in range(4)] + [one, cst((8, D))] + [ANY] * near,
        out_specs=[one] * 6 + [pl.BlockSpec((2, L, L), lambda h: (h, 0, 0))] + [ANY] * near,
        out_shape=[sds((L, D), F32)] + [sds((L, D), BF)] * 5 + [sds((H, L, L), BF)]
        + ([sds((NS, NZ, NCORE) + far.shape[1:], BF)] if near else []),
        scratch_shapes=PlaneGather.sems() if near else [],
        compiler_params=params(62, cid),
        cost_estimate=pl.CostEstimate(flops=31_000_000_000, bytes_accessed=50_000_000, transcendentals=12_000_000),
        name="cross_fwd")(x, att, wmid, wmid, wmid, wmid, enc, gains, *([far] if near else []))


def feed_kernel(h1_ref, catt_ref, wco_ref, cot_ref, gain_ref, fi_ref, fo_ref,
                out_ref, bh2_ref, bca_ref, gw_ref, dg_ref,
                n3, n3t, cott, acc, dn, inner, bi):
    a = pl.program_id(0)
    g = gain_ref[2:3, :]

    @pl.when(a == 0)
    def _():

        def enter(r):
            h2 = h1_ref[r, :] + dot(catt_ref[r, :], wco_ref[...], 1, 0)
            bh2_ref[r, :] = h2
            acc[r, :] = h2
            n3[r, :] = norm(h2, g).astype(BF)

        each(enter, NBK)
        n3t[...] = n3[...].T
        cott[...] = cot_ref[...].T
        dn[...] = jnp.zeros_like(dn)

    for r in blocks():
        u = dot(n3[r, :], fi_ref[...], 1, 0)
        y, d = gelu_pair(u)
        y = y.astype(BF)
        inner[r, :] = y
        gy = dot(cot_ref[r, :], fo_ref[...], 1, 1)
        b = (gy * d).astype(BF)
        bi[r, :] = b
        acc[r, :] += dot(y, fo_ref[...], 1, 0)
        dn[r, :] += dot(b, fi_ref[...], 1, 1)
    gw_ref[:, :D] = dot(n3t[...], bi[...], 1, 0).astype(BF)
    gw_ref[:, D:] = dot(cott[...], inner[...], 1, 0).T.astype(BF)

    @pl.when(a == pl.num_programs(0) - 1)
    def _():
        dg_ref[...] = jnp.zeros_like(dg_ref)

        def leave(r):
            out_ref[r, :] = acc[r, :].astype(BF)
            dx, s = norm_grad(bh2_ref[r, :], g, dn[r, :])
            dg_ref[...] += s
            b2 = cot_ref[r, :].astype(F32) + dx
            bh2_ref[r, :] = b2
            bca_ref[r, :] = dot(b2.astype(BF), wco_ref[...], 1, 1).astype(BF)

        each(leave, NBK)


def feed(h1, catt, wmid, cot, gains, wfeed):
    one = cst((L, D))
    nf = wfeed.shape[1] // (2 * D)
    return pl.pallas_call(
        feed_kernel, grid=(nf,),
        in_specs=[one, one, col((D, D), 4), one, cst((8, D)),
                  pl.BlockSpec((D, D), lambda a: (0, 2 * a)), pl.BlockSpec((D, D), lambda a: (0, 2 * a + 1))],
        out_specs=[one, one, one, pl.BlockSpec((D, 2 * D), lambda a: (0, a)), cst((8, D))],
        out_shape=[sds((L, D), BF), sds((L, D), F32), sds((L, D), BF), sds((D, wfeed.shape[1]), BF), sds((8, D), F32)],
        scratch_shapes=[pltpu.VMEM((L, D), BF), pltpu.VMEM((D, L), BF), pltpu.VMEM((D, L), BF), pltpu.VMEM((L, D), F32),
                        pltpu.VMEM((L, D), F32), pltpu.VMEM((L, D), BF), pltpu.VMEM((L, D), BF)],
        compiler_params=pltpu.CompilerParams(vmem_limit_bytes=62 << 20),
        cost_estimate=pl.CostEstimate(flops=32_000_000_000, bytes_accessed=50_000_000, transcendentals=3_000_000),
        name="feed")(h1, catt, wmid, cot, gains, wfeed, wfeed)


def cross_bwd_kernel(near, q_ref, k_ref, v_ref, do_ref, p_ref, gain_ref, n2_h, enc_h, att_h, catt_h, h1_h, bh2_h, w_h, *refs):
    if near:
        gf_h = refs[0]
        gw_ref, genc_ref, bh1_ref, bat_ref, dg_ref, rf_ref = refs[1:7]
        qt, dot_, ds, dq, dk, dv, n2, enc, att, catt, h1, w, sems, sca = split(refs[7:], 13, len(Scatter.bufs(8, D)))
        sca = Scatter(gf_h, [], *sca)
    else:
        gw_ref, genc_ref, bh1_ref, bat_ref, dg_ref = refs[:5]
        qt, dot_, ds, dq, dk, dv, n2, enc, att, catt, h1, w, sems = refs[5:]
    h = pl.program_id(0)
    late = [(n2_h, n2), (enc_h, enc), (att_h, att), (catt_h, catt), (h1_h, h1), (bh2_h, bh1_ref)]
    late += [(w_h.at[:, pl.ds(0, 4 * D)], w)]
    copies = [pltpu.make_async_copy(a, b, sems.at[i]) for i, (a, b) in enumerate(late)]

    @pl.when(h == 0)
    def _():
        if near:
            meet_all()
            sca.start((3,))

    @pl.when(h == 3)
    def _():
        for c in copies:
            c.start()

    if near:
        for hh, name, *more in BWD_PLAN:
            @pl.when(h == hh)
            def _(name=name, more=more):
                getattr(sca, name)(*more)

    e = h % 2
    cols = pl.ds(pl.multiple_of((h // 2) * 128, 128), 128)
    fe = (lax.broadcasted_iota(jnp.int32, (1, 128), 1) // DH) == e
    k = k_ref[...]
    v = v_ref[...]

    @pl.when(e == 0)
    def _():
        qt[...] = q_ref[...].T
        dot_[...] = do_ref[...].T

    for r in blocks():
        do = do_ref[r, :]
        dp = dot(jnp.where(fe, do, jnp.zeros_like(do)), v, 1, 1)
        p = p_ref[0, r, :].astype(F32)
        d = (p * (dp - jnp.sum(dp * p, 1, keepdims=True))).astype(BF)
        ds[r, :] = d
        dq[r, cols] = jnp.where(fe, dot(d, k, 1, 0).astype(BF), dq[r, cols])
    x = dot(dot_[...], p_ref[0], 1, 0).T.astype(BF)
    dv[:, cols] = jnp.where(fe, x, dv[:, cols])
    x = dot(qt[...], ds[...], 1, 0).T.astype(BF)
    dk[:, cols] = jnp.where(fe, x, dk[:, cols])

    @pl.when(h == H - 1)
    def _():
        for c in copies:
            c.wait()
        g = gain_ref[1:2, :]
        dg_ref[...] = jnp.zeros_like(dg_ref)
        gw_ref[:, D:2 * D] = dot(n2[...], dq[...], 0, 0).astype(BF)
        gw_ref[:, 2 * D:3 * D] = dot(enc[...], dk[...], 0, 0).astype(BF)
        gw_ref[:, 3 * D:4 * D] = dot(enc[...], dv[...], 0, 0).astype(BF)

        def leave(r):
            genc_ref[r, :] = (dot(dk[r, :], w[:, 2 * D:3 * D], 1, 1) + dot(dv[r, :], w[:, 3 * D:], 1, 1)).astype(genc_ref.dtype)
            dx, s = norm_grad(h1[r, :], g, dot(dq[r, :], w[:, D:2 * D], 1, 1))
            dg_ref[...] += s
            b2 = bh1_ref[r, :]
            b1 = b2 + dx
            bh1_ref[r, :] = b1
            b1 = b1.astype(BF)
            n2[r, :] = b1
            enc[r, :] = b2.astype(BF)
            bat_ref[r, :] = dot(b1, w[:, :D], 1, 1).astype(BF)

        each(leave)
        gw_ref[:, :D] = dot(att[...], n2[...], 0, 0).astype(BF)
        gw_ref[:, 4 * D:] = dot(catt[...], enc[...], 0, 0).astype(BF)
        if near:
            sca.stop(rf_ref)


BWD_PLAN = ((2, "away"), (2, "start", (2, 1)), (3, "start", (0,)), (6, "near"))


def cross_bwd(q, k, v, do, p, gains, n2, enc, att, catt, h1, bh2, wmid, far=None, cid=None):
    one = cst((L, D))
    near = far is not None
    pair = pl.BlockSpec((L, 128), lambda h: (0, h // 2))
    act = pltpu.VMEM((L, D), BF)
    more = [(NZ,) + far.shape[3:]] if near else []
    return pl.pallas_call(
        functools.partial(cross_bwd_kernel, near), grid=(H,),
        in_specs=[pair] * 4 + [pl.BlockSpec((1, L, L), lambda h: (h, 0, 0)), cst((8, D))] + [ANY] * (7 + near),
        out_specs=[cst((D, 5 * D)), one, one, one, cst((8, D))] + [cst(s) for s in more],
        out_shape=[sds((D, 5 * D), BF), sds((L, D), BF), sds((L, D), F32), sds((L, D), BF), sds((8, D), F32)]
        + [sds(s, BF) for s in more],
        scratch_shapes=[pltpu.VMEM((128, L), BF)] * 2 + [pltpu.VMEM((L, L), BF)] + [act] * 7
        + [pltpu.VMEM((L, D), F32), pltpu.VMEM((D, 4 * D), BF), DMA((7,))] + sum([Scatter.bufs(*s[1:]) for s in more], []),
        compiler_params=params(62, cid),
        cost_estimate=pl.CostEstimate(flops=37_000_000_000, bytes_accessed=70_000_000, transcendentals=0),
        name="cross_bwd")(q, k, v, do, p, gains, n2, enc, att, catt, h1, bh2, wmid, *([far] if near else []))


SELF_PLAN = ((1, "away"), (1, "start", (2, 1, 0)), (3, "near"), (3, "exc", 0), (6, "exc", 1), (8, "line"))


def self_bwd_kernel(near, q_ref, k_ref, v_ref, ba_ref, p_ref, mpre_ref, mpost_ref, gain_ref, x_h, bh1_h, w_h, *refs):
    if near:
        gm_h, zf_h, out_h, ge_h = refs[:4]
        gw_ref, gtok_ref, gpre_ref, gpost_ref, diag_ref, dg_ref = refs[4:10]
        rms, (rf_ref, oo_h, go_h) = refs[10:15], refs[15:18]
        qt, bat, dqa, dkt, dvt, dm, x, bh1, w, sems, sca, lin, ex1, ex2 = split(refs[18:], 10, len(Scatter.bufs(8, D)), 5, 3, 3)
        lin = LineScatter(zf_h, rf_ref, *lin)
        sca = Scatter(gm_h, rms, *sca)
        exc = [Exchange(out_h, oo_h, *ex1), Exchange(ge_h, go_h, *ex2)]
    else:
        gw_ref, gtok_ref, gpre_ref, gpost_ref, diag_ref, dg_ref = refs[:6]
        qt, bat, dqa, dkt, dvt, dm, x, bh1, w, sems = refs[6:]
    h = pl.program_id(0)

    if near:
        @pl.when(h == 0)
        def _():
            meet_all()
            sca.start((3,))
            lin.start()

        for hh, name, *more in SELF_PLAN:
            @pl.when(h == hh)
            def _(name=name, more=more):
                if name == "exc":
                    exc[more[0]].start()
                else:
                    getattr(sca, name)(*more)

    late = [(x_h, x), (bh1_h, bh1), (w_h.at[:, pl.ds(0, 3 * D)], w)]
    copies = [pltpu.make_async_copy(a, b, sems.at[i]) for i, (a, b) in enumerate(late)]

    @pl.when(h == 0)
    def _():
        for c in copies:
            c.start()
        qt[...] = q_ref[...].T
        bat[...] = ba_ref[...].T
        dqa[...] = jnp.zeros_like(dqa)
        dkt[...] = jnp.zeros_like(dkt)
        dvt[...] = jnp.zeros_like(dvt)

    mp = mpre_ref[pl.ds(h, 1), :]
    mo = mpost_ref[pl.ds(h, 1), :]
    gp = jnp.zeros((8, D), F32)
    dacc = [None] * NBK
    for i, r in enumerate(blocks()):
        n = (i + 1) * BLK
        bam = (ba_ref[r, :].astype(F32) * mo).astype(BF)
        dp = dot(bam, v_ref[:n, :], 1, 1)
        p = p_ref[0, r, :n].astype(F32)
        d = p * (dp - jnp.sum(dp * p, 1, keepdims=True))
        for j in range(i + 1):
            t = d[:, j * BLK:(j + 1) * BLK]
            dacc[i - j] = t if dacc[i - j] is None else dacc[i - j] + t
        db = d.astype(BF)
        dm[r, :n] = db
        rr = dot(db, k_ref[:n, :], 1, 0)
        dqa[r, :] += rr * mp
        gp = gp + rows8(rr * q_ref[r, :].astype(F32))
    gpre_ref[pl.ds(h, 1), :] = jnp.sum(gp, 0, keepdims=True)
    for t in range(NBK):
        y = jnp.concatenate([jnp.zeros((BLK, BLK), F32), dacc[t]], 1)
        n = BLK // 2
        while n >= 1:
            y = y[:n] + pltpu.roll(y[n:], 2 * BLK - n, 1)
            n //= 2
        diag_ref[0, t] = y
    mpc = jnp.broadcast_to(mp, (8, D)).T[:, :1]
    moc = jnp.broadcast_to(mo, (8, D)).T[:, :1]
    gq = jnp.zeros((8, D), F32)
    for c in blocks():
        i0 = c.start
        t = dot(bat[:, i0:], p_ref[0, i0:, c], 1, 0)
        dvt[:, c] += t * moc
        gq = gq + rows8(t.T * v_ref[c, :].astype(F32))
        u = dot(qt[:, i0:], dm[i0:, c], 1, 0)
        dkt[:, c] += u * mpc
    gpost_ref[pl.ds(h, 1), :] = jnp.sum(gq, 0, keepdims=True)

    @pl.when(h == H - 1)
    def _():
        for c in copies:
            c.wait()
        g = gain_ref[:1, :]
        dg_ref[...] = jnp.zeros_like(dg_ref)

        def leave(r):
            xr = x[r, :].astype(F32)
            n1 = norm(xr, g).astype(BF)
            dk = dkt[:, r].T.astype(BF)
            dv = dvt[:, r].T.astype(BF)
            dq = dqa[r, :].astype(BF)
            bat[:, r] = n1.T
            dm[r, :D] = dq
            dqa[r, :] = dk.astype(F32)
            back = dot(dq, w[:, :D], 1, 1) + dot(dk, w[:, D:2 * D], 1, 1) + dot(dv, w[:, 2 * D:], 1, 1)
            dx, s = norm_grad(xr, g, back)
            dg_ref[...] += s
            gtok_ref[r, :] = (bh1[r, :] + dx).astype(gtok_ref.dtype)

        each(leave)
        gw_ref[:, :D] = dot(bat[...], dm[:, :D], 1, 0).astype(BF)
        gw_ref[:, D:2 * D] = dot(bat[...], dqa[...].astype(BF), 1, 0).astype(BF)
        gw_ref[:, 2 * D:] = dot(bat[...], dvt[...].astype(BF), 1, 1).astype(BF)
        if near:
            lin.end()
            sca.end()
            for e in exc:
                e.end()


def self_bwd(q, k, v, ba, p, mpre, mpost, gains, x, bh1, w1, far=None, cid=None):
    one = cst((L, D))
    near = far is not None
    rows = far[0].shape[3] if near else 0
    more = [cst((rows, D))] * 5 + [cst(far[1].shape[1:]), ANY, ANY] if near else []
    more_out = []
    if near:
        more_out = [sds((rows, D), F32)] * 5 + [sds(far[1].shape[1:], F32)] + [sds(f.shape, BF) for f in far[2:]]
    return pl.pallas_call(
        functools.partial(self_bwd_kernel, near), grid=(H,),
        in_specs=[one] * 4 + [pl.BlockSpec((1, L, L), lambda h: (h, 0, 0)), cst((H, D)), cst((H, D)), cst((8, D))] + [ANY] * (3 + 4 * near),
        out_specs=[cst((D, 3 * D))] + [one, cst((H, D)), cst((H, D)),
                   pl.BlockSpec((1, NBK, 1, 2 * BLK), lambda h: (h, 0, 0, 0)), cst((8, D))] + more,
        out_shape=[sds((D, 3 * D), BF)] + [sds((L, D), BF), sds((H, D), F32), sds((H, D), F32),
                   sds((H, NBK, 1, 2 * BLK), F32), sds((8, D), F32)] + more_out,
        scratch_shapes=[pltpu.VMEM((D, L), BF)] * 2 + [pltpu.VMEM((L, D), F32)] + [pltpu.VMEM((D, L), F32)] * 2
        + [pltpu.VMEM((L, L), BF), pltpu.VMEM((L, D), BF), pltpu.VMEM((L, D), F32), pltpu.VMEM((D, 3 * D), BF), DMA((3,))]
        + (Scatter.bufs(*far[0].shape[3:]) + LineScatter.bufs(*far[1].shape[1:]) + Exchange.sems() * 2 if near else []),
        compiler_params=params(62, cid),
        cost_estimate=pl.CostEstimate(flops=128_000_000_000, bytes_accessed=50_000_000, transcendentals=0),
        name="self_bwd")(q, k, v, ba, p, mpre, mpost, gains, x, bh1, w1, *(far or ()))


AX = ("seq", "dp")


def gather(w):
    return lax.all_gather(w, AX, axis=0, tiled=True)


def scatter(g):
    return lax.psum_scatter(g, AX, scatter_dimension=0, tiled=True).astype(F32)


def per_device(tokens, encoded, cotangent, doc_starts, rel_bucket, sq, sk, sv, so, cq, ck, cv, co, fi, fo,
               gs, gc, gf, mix_pre, mix_post, rel_table):
    nseq, ndp = lax.axis_size("seq"), lax.axis_size("dp")
    rows = sq.shape[0]
    nf = fo.shape[0] // rows
    ndev = nseq * ndp
    buckets = rel_table.shape[0]
    near = nseq == NS and ndp == NZ * NCORE and rows % 8 == 0
    to_stream = lambda x: lax.all_to_all(x, "seq", 0, 1, tiled=True).reshape(L, D)
    from_stream = lambda x: lax.all_to_all(x.reshape(1, L, D), "seq", 1, 0, tiled=True)
    hot = (rel_bucket[:, None] == jnp.arange(buckets)[None, :]).astype(F32)
    trow = lax.dot_general(rel_table, hot, (((0,), (1,)), ((), ())), precision=lax.Precision.HIGHEST)
    base = make_base(trow)
    gains = jnp.pad(jnp.stack([gs, gc, gf], 1), ((0, 0), (0, 125)))
    w1 = jnp.concatenate([sq, sk, sv, gains], 1)
    wmid = jnp.concatenate([so, cq, ck, cv, co], 1)
    wfeed = jnp.stack([fi.reshape(rows, D, nf).transpose(0, 2, 1), fo.reshape(rows, nf, D)], 2).reshape(rows, 2 * nf * D)
    if near:
        w1, zmid, x, bias = weights_in(w1, wmid, tokens, base, 1)
        w1 = w1.reshape(D, -1)
        x = x.reshape(L, D)
    else:
        w1 = gather(w1)
        x = to_stream(tokens)
        bias = toeplitz(base)
        wmid = gather(wmid)
        wfeed = gather(wfeed)
        enc = to_stream(encoded)
        cot = to_stream(cotangent)
    if near:
        q, k, v, att, gain, mpre, mpost, p, wmid, zfeed, enc, cot = self_fwd(doc_starts, x, w1, bias, mix_pre, mix_post, (zmid, wfeed, encoded, cotangent), 2)
        wmid = wmid.reshape(D, -1)
        enc = enc.reshape(L, D)
        h1, n2, cqx, ckx, cvx, catt, cp, wfeed = cross_fwd(x, att, wmid, enc, gain, zfeed, 3)
        cot = cot.reshape(L, D)
        wfeed = wfeed.reshape(D, -1)
    else:
        q, k, v, att, gain, mpre, mpost, p = self_fwd(doc_starts, x, w1, bias, mix_pre, mix_post)
        h1, n2, cqx, ckx, cvx, catt, cp = cross_fwd(x, att, wmid, enc, gain)
    out, bh2, bca, gw_feed, dgf = feed(h1, catt, wmid, cot, gain, wfeed)
    by_dev = lambda a: a.reshape(NS, NZ, NCORE, rows, -1)
    back = (cqx, ckx, cvx, bca, cp, gain, n2, enc, att, catt, h1, bh2, wmid)
    if near:
        gw_mid, g_enc, bh1, bat, dgc, zfeed = cross_bwd(*back, by_dev(gw_feed), 6)
    else:
        gw_mid, g_enc, bh1, bat, dgc = cross_bwd(*back)
        r_feed = scatter(gw_feed)
    blk = lambda a: a.reshape(nseq, L // nseq, D)
    if near:
        far = (by_dev(gw_mid), zfeed, blk(out), blk(g_enc))
        gw_qkv, g_tok, gpre, gpost, diag, dgs, *r_mid, r_feed, out, g_enc = self_bwd(
            q, k, v, bat, p, mpre, mpost, gain, x, bh1, w1, far, 4)
    else:
        gw_qkv, g_tok, gpre, gpost, diag, dgs = self_bwd(q, k, v, bat, p, mpre, mpost, gain, x, bh1, w1)
    if near:
        pad = jnp.pad(rel_bucket[::-1], (BLK, BLK), constant_values=-1)
        bucket = jnp.stack([lax.slice(pad, (L + BLK - 1 - (d * BLK + BLK),), (L + BLK - 1 - (d * BLK + BLK) + 2 * BLK,))
                            for d in range(NBK)])
        r_q, r_k, r_v, dgain, gpre, gpost, gtab, g_tok = grads_out(
            by_dev(gw_qkv), [dgs, dgc, dgf, gpre, gpost, diag, bucket], blk(g_tok), buckets, 5)
        out, g_tok, g_enc, *plain, g_fo, g_fi = finish([out, g_tok, g_enc], [r_q, r_k, r_v, *r_mid, dgain, gpre, gpost, gtab], r_feed)
        r_q, r_k, r_v = plain[:3]
        r_mid, (dgain, gpre, gpost, gtab) = plain[3:8], plain[8:]
        gtab = gtab.T
        dgain = dgain[:18].reshape(3, D)
    else:
        gpre = gpre.reshape(H, H, DH).sum(-1).T
        gpost = gpost.reshape(H, H, DH).sum(-1)
        dg = diag[:, :, 0, ::-1]
        gt = 0.0
        for d in range(NBK):
            gt = gt + jnp.pad(dg[:, d], ((0, 0), (d * BLK + 1, L - d * BLK - 1)))
        gt = gt[:, BLK:BLK + L]
        gtab = lax.dot_general(hot, gt, (((0,), (1,)), ((), ())), precision=lax.Precision.HIGHEST)
        dgain = jnp.stack([dgs.sum(0), dgc.sum(0), dgf.sum(0)])
        r_mid = jnp.split(scatter(gw_mid), 5, 1)
        r_q, r_k, r_v = jnp.split(scatter(gw_qkv), 3, 1)
        out, g_tok, g_enc = from_stream(out), from_stream(g_tok).astype(F32), from_stream(g_enc).astype(F32)
        dgain, gpre, gpost, gtab = lax.psum((dgain, gpre, gpost, gtab), AX)
        r_feed = r_feed.reshape(rows, nf, 2, D)
        g_fi, g_fo = r_feed[:, :, 0].transpose(1, 0, 2), r_feed[:, :, 1].reshape(rows * nf, D)
    g_fi = g_fi.transpose(1, 2, 0).reshape(rows, nf * D)
    g_fo = g_fo.reshape(rows * nf, D)
    me = lax.axis_index("seq") * ndp + lax.axis_index("dp")
    dgain = lax.dynamic_slice_in_dim(dgain, me * rows, rows, 1)
    return (out, g_tok, g_enc,
            r_q, r_k, r_v, *r_mid,
            g_fi, g_fo,
            dgain[0], dgain[1], dgain[2], gpre, gpost, gtab)


def solution(mesh):
    act = P("dp", "seq", None)
    w = P(AX, None)
    g = P(AX)
    return jax.shard_map(
        per_device, mesh=mesh, in_specs=(act, act, act, P("dp", None), P()) + (w,) * 10 + (g,) * 3 + (P(),) * 3,
        out_specs=(act,) * 3 + (w,) * 10 + (g,) * 3 + (P(),) * 3, check_vma=False)
```
